128 devices in a mesh: row: 16 (over y, z), col: 8 (over x, core).
Axes of the slice: x: 4, y: 4, z: 4, core: 2. Of those that a mesh axis runs over, the one named last changes fastest.
Arguments:
- current_image: float32 [16, 2048, 2048], P(None, 'row', 'col'), may hold values from -6 to 6
- measured: float32 [16, 16, 16, 128], P('col', 'row'), may hold values from -6 to 6
- ray_weight: float32 [16, 16, 128], P('col', 'row'), may hold values from 0.25 to 4
- angle_ids: int32 [16], replicated, may hold values from 0 to 255, as said below
- shadow_start: int32 [16, 16, 16], replicated, may hold values from 0 to 1920, as said below
Outputs:
- smoothed_image: float32 [16, 2048, 2048], P(None, 'row', 'col')
The draws below stay inside these ranges and needn't reach their ends.
Inputs may be any that keep to these rules, and one draw needn't show every extreme that they name: `angle_ids`: distinct angle numbers. `shadow_start`: the shadow of a tile covers the 128 detector bins from this bin on, so it touches one or two detector blocks.
All inputs are finite; a program needn't handle non-finite values.
Results may differ from the reference program's by a relative error of at most 0.0033.
Values may be sent and summed in bfloat16 or wider, within the bound.
No kernel may reach another device: no remote copies, remote signals or barrier semaphores. Data moves between devices by JAX's collectives and lax.ppermute only.
A program may use at most 64 MiB of HBM per device.

```python
import math
import jax
import jax.numpy as jnp
from jax import lax

TILE = 128
SLICES = 16
ANGLES = 16
ALL_ANGLES = 256
TV_STEPS = 4
SIDE_TILES = 16
IMG = 2048
BLOCKS = 16
DET = 2048
N_ROW = 16


def angle_helper(key):
    stride = ALL_ANGLES // ANGLES
    offset = jax.random.randint(jax.random.fold_in(key, 11), (), 0, stride)
    return (offset + stride * jnp.arange(ANGLES, dtype=jnp.int32)).astype(jnp.int32)


def draw_angle_ids(key, part):
    return angle_helper(key)


def draw_shadow_start(key, part):
    total = SIDE_TILES * SIDE_TILES * ANGLES
    starts = jax.random.randint(jax.random.fold_in(key, 23), (total,), 0, DET - TILE + 1)
    places = jax.random.permutation(jax.random.fold_in(key, 29), total)
    starts = starts.at[places[0]].set(0)
    starts = starts.at[places[1]].set(DET - TILE)
    return starts.reshape(SIDE_TILES, SIDE_TILES, ANGLES).astype(jnp.int32)


def shard_levels(own_key, extent, pieces, low, high):
    factor_of, own = 1.0, jax.random.fold_in(own_key, 6)
    for axis_at, blocks in pieces:
        draws = jnp.exp(jax.random.uniform(jax.random.fold_in(own, axis_at), (blocks,), jnp.float32, low / len(pieces), high / len(pieces)))
        factor_of = factor_of * jnp.repeat(draws, extent[axis_at] // blocks).reshape([-1 if axis == axis_at else 1 for axis in range(len(extent))])
    return factor_of


def bell_draw(own_key, extent, scale, limit, split=(), held_as=jnp.bfloat16):
    values = scale * jax.random.normal(own_key, extent, jnp.float32)
    if split:
        values = values * shard_levels(own_key, extent, split, -0.22, 0.18)
    return jnp.clip(values, -limit, limit).astype(held_as)


def setup_inputs(seed: int = 0) -> dict:
    arg_keys = jax.random.split(jax.random.key(seed), 6)
    return {
        "current_image": bell_draw(arg_keys[0], (SLICES, IMG, IMG), 1.0, 6.0, ((1, 16), (2, 8)), jnp.float32),
        "measured": bell_draw(arg_keys[1], (ANGLES, BLOCKS, SLICES, TILE), 1.0, 6.0, ((0, 8), (1, 16)), jnp.float32),
        "ray_weight": jnp.clip(jnp.exp(math.log(4.0) - 2.7725887 * jax.random.uniform(arg_keys[2], (ANGLES, BLOCKS, TILE), jnp.float32) ** shard_levels(arg_keys[2], (ANGLES, BLOCKS, TILE), ((0, 8), (1, 16)), -0.2, 0.2)), 0.25, 4.0),
        "angle_ids": draw_angle_ids(jax.random.fold_in(arg_keys[5], 71), 0),
        "shadow_start": draw_shadow_start(jax.random.fold_in(arg_keys[5], 71), 0),
    }


inverse_root = 0.7071067811865476
proj_scale = 0.03125
relaxation = 8.0
smoothing = 0.25
descent_step = 0.05

def tile_weights(angle_number):
    radians = angle_number.astype(jnp.float32) * (math.pi / ALL_ANGLES)
    cosine = jnp.cos(radians)
    sine_value = jnp.sin(radians)
    centre = (TILE - 1) / 2.0
    position = jnp.arange(TILE, dtype=jnp.float32) - centre
    along_bins = TILE / 2.0 + (position[:, None] * cosine + position[None, :] * sine_value) * inverse_root
    centres = jnp.arange(TILE, dtype=jnp.float32) + 0.5
    hat_values = jnp.maximum(0.0, 1.0 - jnp.abs(along_bins.reshape(-1, 1) - centres[None, :]))
    return (hat_values * proj_scale).astype(jnp.bfloat16)

def ramp(offset):
    is_odd = offset % 2 != 0
    nonzero = jnp.where(offset == 0, 1, offset).astype(jnp.float32)
    values = jnp.where(is_odd, -1.0 / (math.pi * math.pi * nonzero * nonzero), 0.0)
    values = jnp.where(offset == 0, 0.25, values)
    return jnp.where(jnp.abs(offset) < TILE, values, 0.0).astype(jnp.float32)

def tv_gradient(padded):
    corner = padded[:, :-1, :-1]
    step_down = padded[:, 1:, :-1] - corner
    step_right = padded[:, :-1, 1:] - corner
    magnitude = jnp.sqrt(smoothing * smoothing + step_down * step_down + step_right * step_right)
    flow_down = step_down / magnitude
    flow_right = step_right / magnitude
    return flow_down[:, :-1, 1:] - flow_down[:, 1:, 1:] + flow_right[:, 1:, :-1] - flow_right[:, 1:, 1:]

def reference(current_image, measured, ray_weight, angle_ids, shadow_start):
    count = N_ROW * N_ROW
    tile_data = current_image.reshape(SLICES, N_ROW, TILE, N_ROW, TILE).transpose(1, 3, 0, 2, 4)
    tile_data = tile_data.reshape(count * SLICES, TILE * TILE).astype(jnp.bfloat16).astype(jnp.float32)
    starts = shadow_start.reshape(count, ANGLES)
    offsets = jnp.arange(TILE, dtype=jnp.int32)

    def project(angle_index):
        weights = tile_weights(angle_ids[angle_index]).astype(jnp.float32)
        partial_value = jnp.dot(tile_data, weights, precision=lax.Precision.HIGHEST)
        partial_value = partial_value.reshape(count, SLICES, TILE).transpose(1, 0, 2).reshape(SLICES, count * TILE)
        bin_index = (starts[:, angle_index][:, None] + offsets[None, :]).reshape(-1)
        return jnp.zeros((SLICES, DET), jnp.float32).at[:, bin_index].add(partial_value)
    ray_sums = lax.map(project, jnp.arange(ANGLES, dtype=jnp.int32))
    natural = measured.transpose(0, 2, 1, 3).reshape(ANGLES, SLICES, DET)
    weight_rows = ray_weight.reshape(ANGLES, 1, DET)
    residual = weight_rows * (natural - ray_sums)
    detector = jnp.arange(DET, dtype=jnp.int32)
    ramp_table = ramp(detector[None, :] - detector[:, None])
    filtered = jnp.einsum('asi,ij->asj', residual, ramp_table, precision=lax.Precision.HIGHEST)
    filtered = filtered.astype(jnp.bfloat16).astype(jnp.float32)

    def accumulate(angle_index, running):
        weights = tile_weights(angle_ids[angle_index]).astype(jnp.float32)
        bin_index = starts[:, angle_index][:, None] + offsets[None, :]
        shadow = filtered[angle_index][:, bin_index]
        shadow = shadow.transpose(1, 0, 2).reshape(count * SLICES, TILE)
        return running + jnp.dot(shadow, weights.T, precision=lax.Precision.HIGHEST)
    update = lax.fori_loop(0, ANGLES, accumulate, jnp.zeros((count * SLICES, TILE * TILE), jnp.float32))
    update = update.reshape(N_ROW, N_ROW, SLICES, TILE, TILE).transpose(2, 0, 3, 1, 4).reshape(SLICES, IMG, IMG)
    current = current_image + relaxation * update
    for repeat in range(TV_STEPS):
        padded = jnp.pad(current, ((0, 0), (1, 1), (1, 1)))
        current = current - descent_step * tv_gradient(padded)
    return current
```

```python
import functools
import math

import jax
import jax.numpy as jnp
from jax import lax
from jax.experimental import pallas as pl
from jax.experimental.pallas import tpu as pltpu
from jax.sharding import PartitionSpec as P

TILE = 128
ANGLES = 16
ALL_ANGLES = 256
TV_STEPS = 4
SIDE = 16
PATCHES = TILE // SIDE
PIX = SIDE * SIDE
BINS = 24
ROWS = 32
BAND = ANGLES * BINS

inverse_root = 0.7071067811865476
smoothing = 0.25
descent_step = 0.05

VMEM = pltpu.VMEM
F32 = jnp.float32
BF16 = jnp.bfloat16


def geometry(angle_ids):
    radians = angle_ids.astype(F32) * (math.pi / ALL_ANGLES)
    cosine = jnp.cos(radians) * inverse_root
    sine = jnp.sin(radians) * inverse_root
    first = jnp.arange(PATCHES, dtype=F32) * SIDE - (TILE - 1) / 2.0
    corner = TILE / 2.0 + first[:, None, None] * cosine + first[None, :, None] * sine
    corner = corner.reshape(PATCHES * PATCHES, ANGLES)
    low = corner + (SIDE - 1) * (jnp.minimum(cosine, 0.0) + jnp.minimum(sine, 0.0))
    first_bin = jnp.floor(low - 1.5).astype(jnp.int32) + 1
    base = jnp.clip((first_bin >> 3) << 3, 0, TILE - BINS)
    delta = corner - base.astype(F32) - 0.5
    return cosine, sine, base, delta


def forward_kernel(
    base_ref, delta_ref, cs_ref, image0_ref, image1_ref, out_ref, xt, rel, band0, band1, sums
):
    slices = ROWS // 2
    lane = lax.broadcasted_iota(jnp.int32, (BINS, PIX), 1)
    bin_at = lax.broadcasted_iota(jnp.int32, (BINS, PIX), 0).astype(F32)
    down = (lane // SIDE).astype(F32)
    across = (lane % SIDE).astype(F32)
    for a in range(ANGLES):
        rel[a * BINS : (a + 1) * BINS, :] = down * cs_ref[0, a] + across * cs_ref[1, a] - bin_at
    sums[...] = jnp.zeros_like(sums)

    def flip(u, carry):
        both = [ref[pl.ds(u, slices, stride=TILE), :] for ref in (image0_ref, image1_ref)]
        stacked = jnp.concatenate(both, axis=0)
        xt[pl.ds(pl.multiple_of(u * TILE, TILE), TILE), :] = stacked.T.astype(BF16)
        return carry

    lax.fori_loop(0, TILE, flip, 0, unroll=4)

    def build(patch, band):
        for a in range(0, ANGLES, 2):
            pair = []
            for b in (a, a + 1):
                away = jnp.abs(rel[b * BINS : (b + 1) * BINS, :] + delta_ref[patch * ANGLES + b])
                pair.append(jnp.maximum(0.0, 1.0 - away))
            band[a * BINS : (a + 2) * BINS, :] = jnp.concatenate(pair, axis=0).astype(BF16)

    def project(patch, band):
        row = patch // PATCHES
        col = patch % PATCHES
        pieces = []
        for u in range(SIDE):
            start = pl.multiple_of((row * SIDE + u) * TILE + col * SIDE, SIDE)
            pieces.append(xt[pl.ds(start, SIDE), :])
        pixels = jnp.concatenate(pieces, axis=0)
        got = jnp.dot(band[...], pixels, preferred_element_type=F32)
        for a in range(ANGLES):
            start = pl.multiple_of(base_ref[patch * ANGLES + a], 8)
            sums[a, pl.ds(start, BINS), :] += got[a * BINS : (a + 1) * BINS, :]

    build(0, band0)

    def step(i, carry):
        build(2 * i + 1, band1)
        project(2 * i, band0)
        build(jnp.minimum(2 * i + 2, PATCHES * PATCHES - 1), band0)
        project(2 * i + 1, band1)
        return carry

    lax.fori_loop(0, PATCHES * PATCHES // 2, step, 0)
    for a in range(ANGLES):
        turned = sums[a].T * 0.03125
        for t in range(2):
            row = (a // 2) * 4 + t * 2 + a % 2
            out_ref[pl.ds(row, slices, stride=ROWS), :] = turned[t * slices : (t + 1) * slices, :]


def owner_kernel(starts_ref, own_ref, got_ref, given_ref, out_ref, low, high, wide, filt, staged):
    blocks = 16
    groups = got_ref.shape[0] // 8
    low[...] = jnp.zeros_like(low)
    high[...] = jnp.zeros_like(high)
    lane = lax.broadcasted_iota(jnp.int32, (8, TILE), 1)
    sub = lax.broadcasted_iota(jnp.int32, (8, TILE), 0)
    first = own_ref[0] * 2

    def where_of(g, k):
        tile = g * 4 + (k // 4) * 2 + (k // 2) % 2
        start = starts_ref[tile * ANGLES + first + k % 2]
        return start >> 7, start & (TILE - 1)

    def add(g, carry):
        rows = got_ref[pl.ds(pl.multiple_of(g * 8, 8), 8), :]
        for k in range(8):
            block, shift = where_of(g, k)
            turned = jnp.where(sub == k, pltpu.roll(rows, shift, 1), 0.0)
            tail = lane >= shift
            low[block] += jnp.where(tail, turned, 0.0)
            high[block] += jnp.where(tail, 0.0, turned)
        return carry

    lax.fori_loop(0, groups, add, 0)
    wide[...] = jnp.zeros_like(wide)
    for h in range(2):
        for b in range(blocks):
            total = low[b]
            if b:
                total = total + high[b - 1]
            total = jnp.sum(jnp.where(sub % 2 == h, total, 0.0), axis=0, keepdims=True)
            meas = given_ref[b * 4 + h : b * 4 + h + 1, :]
            weight = given_ref[b * 4 + 2 + h : b * 4 + 3 + h, :]
            wide[h * blocks + b : h * blocks + b + 1, TILE : 2 * TILE] = weight * (meas - total)
    centre = wide[:, TILE : 2 * TILE]
    at = lax.broadcasted_iota(jnp.int32, (2 * blocks, TILE), 0) % blocks
    wide[:, :TILE] = jnp.where(at == 0, 0.0, pltpu.roll(centre, 1, 0))
    wide[:, 2 * TILE :] = jnp.where(at == blocks - 1, 0.0, pltpu.roll(centre, 2 * blocks - 1, 0))
    offset = (
        lax.broadcasted_iota(jnp.int32, (3 * TILE, TILE), 1)
        + TILE
        - lax.broadcasted_iota(jnp.int32, (3 * TILE, TILE), 0)
    )
    nonzero = jnp.where(offset == 0, 1, offset).astype(F32)
    ramp = jnp.where((offset & 1) == 1, -1.0 / (math.pi * math.pi * nonzero * nonzero), 0.0)
    ramp = jnp.where(offset == 0, 0.25, ramp)
    ramp = jnp.where(jnp.abs(offset) < TILE, ramp, 0.0)
    done = jnp.dot(wide[...], ramp, precision=lax.Precision.HIGHEST, preferred_element_type=F32)
    wide[:, :TILE] = done.astype(BF16).astype(F32)
    filt[...] = jnp.zeros_like(filt)
    for h in range(2):
        for b in range(blocks):
            row = wide[h * blocks + b : h * blocks + b + 1, :TILE]
            filt[h, b] = jnp.broadcast_to(row, (8, TILE))

    def take(g, carry):
        rows = jnp.zeros((8, TILE), F32)
        for k in range(8):
            block, shift = where_of(g, k)
            mixed = jnp.where(lane >= shift, filt[k % 2, block], filt[k % 2, block + 1])
            rows = jnp.where(sub == k, pltpu.roll(mixed, (TILE - shift) & (TILE - 1), 1), rows)
        staged[pl.ds(pl.multiple_of(g * 8, 8), 8), :] = rows
        return carry

    lax.fori_loop(0, groups, take, 0)
    out_ref[...] = staged[...].astype(BF16)


def backward_kernel(
    base_ref, image0_ref, image1_ref, delta_ref, lanes_ref, got_ref, out_ref, left_ref, right_ref,
    rel, band0, band1, shadows, staged, update,
):
    slices = ROWS // 2
    pixel = lax.broadcasted_iota(jnp.int32, (PIX, BAND), 0)
    rel[...] = (
        (pixel // SIDE).astype(F32) * lanes_ref[0:1, :]
        + (pixel % SIDE).astype(F32) * lanes_ref[1:2, :]
    )
    staged[...] = got_ref[...].astype(F32)
    for a in range(ANGLES):
        parts = []
        for t in range(2):
            row = (a // 2) * 4 + t * 2 + a % 2
            parts.append(staged[pl.ds(row, slices, stride=ROWS), :])
        shadows[a] = jnp.concatenate(parts, axis=0).T

    def build(patch, band):
        shift = delta_ref[pl.ds(patch, 1), :]
        for r in range(0, PIX, 16):
            away = jnp.abs(rel[r : r + 16, :] + shift)
            band[r : r + 16, :] = jnp.maximum(0.0, 1.0 - away).astype(BF16)

    def spread(patch, band):
        row = patch // PATCHES
        col = patch % PATCHES
        pieces = []
        for a in range(ANGLES):
            start = pl.multiple_of(base_ref[patch * ANGLES + a], 8)
            pieces.append(shadows[a, pl.ds(start, BINS), :])
        seen = jnp.concatenate(pieces, axis=0).astype(BF16)
        got = jnp.dot(band[...], seen, preferred_element_type=F32)
        for u in range(SIDE):
            start = pl.multiple_of((row * SIDE + u) * TILE + col * SIDE, SIDE)
            update[pl.ds(start, SIDE), :] = got[u * SIDE : (u + 1) * SIDE, :]

    build(0, band0)

    def step(i, carry):
        build(2 * i + 1, band1)
        spread(2 * i, band0)
        build(jnp.minimum(2 * i + 2, PATCHES * PATCHES - 1), band0)
        spread(2 * i + 1, band1)
        return carry

    lax.fori_loop(0, PATCHES * PATCHES // 2, step, 0)

    lane = lax.broadcasted_iota(jnp.int32, (slices, TILE), 1)
    per = TILE // TV_STEPS

    def finish(g, carry):
        left = jnp.zeros((slices, TILE), F32)
        right = jnp.zeros((slices, TILE), F32)
        for j in range(per):
            u = g * per + j
            turned = update[pl.ds(pl.multiple_of(u * TILE, TILE), TILE), :].T
            for t in range(2):
                here = (image0_ref, image1_ref)[t][pl.ds(u, slices, stride=TILE), :]
                here = here + 0.25 * turned[t * slices : (t + 1) * slices, :]
                out_ref[u, :, t * TILE : (t + 1) * TILE] = here
                mine = (lane >= j * TV_STEPS) & (lane < (j + 1) * TV_STEPS)
                if t == 0:
                    left = jnp.where(mine, pltpu.roll(here, j * TV_STEPS, 1), left)
                else:
                    right = jnp.where(mine, pltpu.roll(here, (j + 1) * TV_STEPS % TILE, 1), right)
        left_ref[g] = left
        right_ref[g] = right
        return carry

    lax.fori_loop(0, TILE // per, finish, 0)


def smooth_kernel(
    place_ref, x_ref, above_ref, below_ref, before_ref, after_ref, out_ref, first, second,
    out0, out1, sems,
):
    slices = ROWS // 2
    high = TILE + 2 * TV_STEPS
    per = TILE // TV_STEPS
    lane = lax.broadcasted_iota(jnp.int32, (slices, TILE), 1)
    has_above, has_below, has_before, has_after = (place_ref[i] for i in range(4))
    keep = ((lane < TV_STEPS) & (has_after == 1)) | (
        (lane >= TILE - TV_STEPS) & (has_before == 1)
    )

    def margin(previous, following, j):
        following = pltpu.roll(following, (TILE - j * TV_STEPS) % TILE, 1)
        previous = pltpu.roll(previous, (TILE - (j + 1) * TV_STEPS) % TILE, 1)
        return jnp.where(keep, jnp.where(lane < TV_STEPS, following, previous), 0.0)

    for r in range(TV_STEPS):
        for ref, start, j in (
            (above_ref, 0, per - TV_STEPS + r),
            (below_ref, TILE + TV_STEPS, r),
        ):
            first[start + r, :, : 2 * TILE] = ref[r]
            first[start + r, :, 2 * TILE :] = margin(
                ref[TV_STEPS, :, :TILE], ref[TV_STEPS, :, TILE:], j
            )

    def load(g, carry):
        for j in range(per):
            u = g * per + j
            first[u + TV_STEPS, :, : 2 * TILE] = x_ref[u]
            first[u + TV_STEPS, :, 2 * TILE :] = margin(before_ref[g], after_ref[g], j)
        return carry

    lax.fori_loop(0, TILE // per, load, 0)

    def flows(here, under):
        down = under - here
        right = pltpu.roll(here, 3 * TILE - 1, 1) - here
        inverse = lax.rsqrt(smoothing * smoothing + down * down + right * right)
        return down * inverse, right * inverse

    edge = lax.broadcasted_iota(jnp.int32, (slices, 3 * TILE), 1)
    keep_all = (
        (edge < 2 * TILE)
        | ((edge < 2 * TILE + TV_STEPS) & (has_after == 1))
        | ((edge >= 3 * TILE - TV_STEPS) & (has_before == 1))
    )

    for k in range(TV_STEPS):
        source, target = (first, second) if k % 2 == 0 else (second, first)
        last = k == TV_STEPS - 1

        def row(r, carry, source=source, target=target, last=last):
            here, came = carry
            under = source[r + 1]
            down, right = flows(here, under)
            change = came - down + pltpu.roll(right, 1, 1) - right
            fresh = here - descent_step * change
            if last:
                out0[pl.ds(r - TV_STEPS, slices, stride=TILE), :] = fresh[:, :TILE]
                out1[pl.ds(r - TV_STEPS, slices, stride=TILE), :] = fresh[:, TILE : 2 * TILE]
            else:
                inside = ((r >= TV_STEPS) | (has_above == 1)) & (
                    (r < TILE + TV_STEPS) | (has_below == 1)
                )
                target[r] = jnp.where(keep_all & inside, fresh, 0.0)
            return under, down

        start = source[k]
        below = source[k + 1]
        came, unused = flows(start, below)
        lax.fori_loop(k + 1, high - k - 1, row, (below, came), unroll=2)
    copies = [
        pltpu.make_async_copy(ref, out_ref.at[:, pl.ds(t * TILE, TILE)], sems.at[t])
        for t, ref in enumerate((out0, out1))
    ]
    for copy in copies:
        copy.start()
    for copy in copies:
        copy.wait()


def call(kernel, scalars, arrays, outs, scratch, flops, halves=(), out_space=VMEM):
    smem = pl.BlockSpec(memory_space=pltpu.SMEM)
    vmem = pl.BlockSpec(memory_space=VMEM)
    specs = [smem] * len(scalars)
    operands = list(scalars)
    for half in halves:
        for t in range(2):
            specs.append(pl.BlockSpec((half.shape[0], TILE), lambda i, t=t: (0, t)))
            operands.append(half)
    specs += [vmem] * len(arrays)
    operands += arrays
    moved = sum(x.size * x.dtype.itemsize for x in (*arrays, *halves))
    return pl.pallas_call(
        kernel,
        grid=(1,),
        out_shape=outs,
        in_specs=specs,
        out_specs=jax.tree.map(lambda x: pl.BlockSpec(memory_space=out_space), outs),
        scratch_shapes=scratch,
        cost_estimate=pl.CostEstimate(flops=flops, bytes_accessed=moved, transcendentals=0),
    )(*operands)


def local(current_image, measured, ray_weight, angle_ids, shadow_start):
    row_index = lax.axis_index("row")
    col_index = lax.axis_index("col")
    rows = lax.axis_size("row")
    cols = lax.axis_size("col")
    slices = current_image.shape[0]
    both = ("row", "col")
    image = current_image.reshape(slices * TILE, 2 * TILE)
    cosine, sine, base, delta = geometry(angle_ids)
    base = base.reshape(-1)

    given = measured[:, 0].transpose(1, 0, 2)
    weight = jnp.broadcast_to(ray_weight[:, 0][None], given.shape)
    given = jnp.concatenate([given, weight], axis=1)
    given = lax.all_to_all(given, "row", split_axis=0, concat_axis=0, tiled=True)

    sent = call(
        forward_kernel,
        (base, delta.reshape(-1), jnp.stack([cosine, sine])),
        (),
        jax.ShapeDtypeStruct((rows * cols * 4, TILE), F32),
        [
            VMEM((TILE * TILE, ROWS), BF16),
            VMEM((BAND, PIX), F32),
            VMEM((BAND, PIX), BF16),
            VMEM((BAND, PIX), BF16),
            VMEM((ANGLES, TILE, ROWS), F32),
        ],
        30_000_000_000,
        halves=(image,),
    )
    got = lax.all_to_all(
        sent.reshape(rows * cols, 4, TILE), both, split_axis=0, concat_axis=0, tiled=True
    )
    blocks = rows
    out = call(
        owner_kernel,
        (shadow_start.reshape(-1), col_index.reshape(1)),
        (got.reshape(-1, TILE), given.reshape(-1, TILE)),
        jax.ShapeDtypeStruct((rows * cols * 4, TILE), BF16),
        [
            VMEM((blocks, 8, TILE), F32),
            VMEM((blocks, 8, TILE), F32),
            VMEM((2 * blocks, 3 * TILE), F32),
            VMEM((2, blocks + 1, 8, TILE), F32),
            VMEM((rows * cols * 4, TILE), F32),
        ],
        10_000_000_000,
    )
    shadows = lax.all_to_all(
        out.reshape(rows * cols, 4, TILE), both, split_axis=0, concat_axis=0, tiled=True
    )
    bins = jnp.arange(BINS, dtype=F32)
    delta_lanes = (delta[:, :, None] - bins).reshape(-1, BAND)
    angle_lanes = jnp.repeat(jnp.stack([cosine, sine]), BINS, axis=1)
    groups = TV_STEPS
    side = jax.ShapeDtypeStruct((groups, slices, TILE), F32)
    x, left, right = call(
        backward_kernel,
        (base,),
        (delta_lanes, angle_lanes, shadows.reshape(-1, TILE)),
        (jax.ShapeDtypeStruct((TILE, slices, 2 * TILE), F32), side, side),
        [
            VMEM((PIX, BAND), F32),
            VMEM((PIX, BAND), BF16),
            VMEM((PIX, BAND), BF16),
            VMEM((ANGLES, TILE, ROWS), F32),
            VMEM((rows * cols * 4, TILE), F32),
            VMEM((TILE * TILE, ROWS), F32),
        ],
        30_000_000_000,
        halves=(image,),
    )
    right_going = [(i, i + 1) for i in range(cols - 1)]
    left_going = [(i + 1, i) for i in range(cols - 1)]
    before = lax.ppermute(right, "col", right_going)
    after = lax.ppermute(left, "col", left_going)
    top = jnp.concatenate(
        [x[:TV_STEPS], jnp.concatenate([before[:1], after[:1]], axis=2)], axis=0
    )
    bottom = jnp.concatenate(
        [x[-TV_STEPS:], jnp.concatenate([before[-1:], after[-1:]], axis=2)], axis=0
    )
    above = lax.ppermute(bottom, "row", [(i, i + 1) for i in range(rows - 1)])
    below = lax.ppermute(top, "row", [(i + 1, i) for i in range(rows - 1)])
    place = jnp.stack(
        [row_index > 0, row_index < rows - 1, col_index > 0, col_index < cols - 1]
    ).astype(jnp.int32)
    wide = VMEM((TILE + 2 * TV_STEPS, slices, 3 * TILE), F32)
    half = VMEM((slices * TILE, TILE), F32)
    smooth = call(
        smooth_kernel,
        (place,),
        (x, above, below, before, after),
        jax.ShapeDtypeStruct((slices * TILE, 2 * TILE), F32),
        [wide, wide, half, half, pltpu.SemaphoreType.DMA((2,))],
        10_000_000_000,
        out_space=pl.ANY,
    )
    return smooth.reshape(current_image.shape)


def solution(mesh):
    return jax.shard_map(
        local,
        mesh=mesh,
        in_specs=(
            P(None, "row", "col"),
            P("col", "row", None, None),
            P("col", "row", None),
            P(),
            P(),
        ),
        out_specs=P(None, "row", "col"),
        check_vma=False,
    )
```

```python
import functools
import math

import jax
import jax.numpy as jnp
from jax import lax
from jax.experimental import pallas as pl
from jax.experimental.pallas import tpu as pltpu
from jax.sharding import PartitionSpec as P

TILE = 128
ANGLES = 16
ALL_ANGLES = 256
TV_STEPS = 4
SIDE = 16
PATCHES = TILE // SIDE
PIX = SIDE * SIDE
BINS = 24
ROWS = 32
BAND = ANGLES * BINS
MESSAGE = 8

inverse_root = 0.7071067811865476
smoothing = 0.25
descent_step = 0.05

VMEM = pltpu.VMEM
F32 = jnp.float32
BF16 = jnp.bfloat16


def geometry(angle_ids):
    radians = angle_ids.astype(F32) * (math.pi / ALL_ANGLES)
    cosine = jnp.cos(radians) * inverse_root
    sine = jnp.sin(radians) * inverse_root
    first = jnp.arange(PATCHES, dtype=F32) * SIDE - (TILE - 1) / 2.0
    corner = TILE / 2.0 + first[:, None, None] * cosine + first[None, :, None] * sine
    corner = corner.reshape(PATCHES * PATCHES, ANGLES)
    low = corner + (SIDE - 1) * (jnp.minimum(cosine, 0.0) + jnp.minimum(sine, 0.0))
    first_bin = jnp.floor(low - 1.5).astype(jnp.int32) + 1
    base = jnp.clip((first_bin >> 3) << 3, 0, TILE - BINS)
    delta = corner - base.astype(F32) - 0.5
    return cosine, sine, base, delta


def forward_kernel(
    base_ref, delta_ref, cs_ref, own_ref, image0_ref, image1_ref, measured_ref, weight_ref,
    out_ref, xt, rel, band0, band1, sums,
):
    slices = ROWS // 2
    lane = lax.broadcasted_iota(jnp.int32, (BINS, PIX), 1)
    bin_at = lax.broadcasted_iota(jnp.int32, (BINS, PIX), 0).astype(F32)
    down = (lane // SIDE).astype(F32)
    across = (lane % SIDE).astype(F32)
    for a in range(ANGLES):
        rel[a * BINS : (a + 1) * BINS, :] = down * cs_ref[0, a] + across * cs_ref[1, a] - bin_at
    sums[...] = jnp.zeros_like(sums)

    def flip(u, carry):
        both = [ref[pl.ds(u, slices, stride=TILE), :] for ref in (image0_ref, image1_ref)]
        stacked = jnp.concatenate(both, axis=0)
        xt[pl.ds(pl.multiple_of(u * TILE, TILE), TILE), :] = stacked.T.astype(BF16)
        return carry

    lax.fori_loop(0, TILE, flip, 0, unroll=16)

    def build(patch, band):
        for a in range(0, ANGLES, 2):
            pair = []
            for b in (a, a + 1):
                away = jnp.abs(rel[b * BINS : (b + 1) * BINS, :] + delta_ref[patch * ANGLES + b])
                pair.append(jnp.maximum(0.0, 1.0 - away))
            band[a * BINS : (a + 2) * BINS, :] = jnp.concatenate(pair, axis=0).astype(BF16)

    def project(patch, band):
        row = patch // PATCHES
        col = patch % PATCHES
        pieces = []
        for u in range(SIDE):
            start = pl.multiple_of((row * SIDE + u) * TILE + col * SIDE, SIDE)
            pieces.append(xt[pl.ds(start, SIDE), :])
        pixels = jnp.concatenate(pieces, axis=0)
        got = jnp.dot(band[...], pixels, preferred_element_type=F32)
        for a in range(ANGLES):
            start = pl.multiple_of(base_ref[patch * ANGLES + a], 8)
            sums[a, pl.ds(start, BINS), :] += got[a * BINS : (a + 1) * BINS, :]

    build(0, band0)

    def step(i, carry):
        build(2 * i + 1, band1)
        project(2 * i, band0)
        build(jnp.minimum(2 * i + 2, PATCHES * PATCHES - 1), band0)
        project(2 * i + 1, band1)
        return carry

    lax.fori_loop(0, PATCHES * PATCHES // 2, step, 0)
    stride = MESSAGE * ANGLES // 2
    for a in range(ANGLES):
        turned = sums[a].T * 0.03125
        for t in range(2):
            row = (a // 2) * MESSAGE + t * 2 + a % 2
            out_ref[pl.ds(row, slices, stride=stride), :] = turned[t * slices : (t + 1) * slices, :]
    row = own_ref[0] * MESSAGE + 4
    for h in range(2):
        out_ref[pl.ds(row + h, slices, stride=stride), :] = measured_ref[h]
        weight = jnp.broadcast_to(weight_ref[h : h + 1, :], (slices, TILE))
        out_ref[pl.ds(row + 2 + h, slices, stride=stride), :] = weight


def owner_kernel(starts_ref, own_ref, got_ref, out_ref, low, high, wide, filt, staged):
    blocks = 16
    per = 8
    groups = staged.shape[0] // (8 * per)
    low[...] = jnp.zeros_like(low)
    high[...] = jnp.zeros_like(high)
    lane = lax.broadcasted_iota(jnp.int32, (8, TILE), 1)
    sub = lax.broadcasted_iota(jnp.int32, (8, TILE), 0)

    def add(g, carry):
        turned = []
        for i in range(2 * per):
            source = g * 2 * per + i
            rows = got_ref[pl.ds(pl.multiple_of(source * MESSAGE, MESSAGE), MESSAGE), :]
            for k in range(4):
                start = starts_ref[source * 4 + k]
                turned.append((start >> 7, start & (TILE - 1), rows, i % 2 * 4 + k, k))
        turned = [
            (block, shift, pltpu.roll(rows, shift, 1), slot) for block, shift, rows, slot, k in turned
        ]
        for block, shift, value, slot in turned:
            tail = jnp.where(lane >= shift, value, 0.0)
            low[slot, block] += tail
            high[slot, block] += value - tail
        return carry

    lax.fori_loop(0, groups, add, 0)
    wide[...] = jnp.zeros_like(wide)
    for b in range(blocks):
        total = jnp.zeros((8, TILE), F32)
        for slot in range(8):
            here = low[slot, b]
            if b:
                here = here + high[slot, b - 1]
            total = total + jnp.where(sub == slot % 4, here, 0.0)
        home = pl.multiple_of((b * 8 + own_ref[0]) * MESSAGE, MESSAGE)
        given = got_ref[pl.ds(home, MESSAGE), :]
        for h in range(2):
            row = total[h : h + 1, :] + total[2 + h : 3 + h, :]
            wide[h * blocks + b : h * blocks + b + 1, TILE : 2 * TILE] = given[6 + h : 7 + h, :] * (
                given[4 + h : 5 + h, :] - row
            )
    centre = wide[:, TILE : 2 * TILE]
    at = lax.broadcasted_iota(jnp.int32, (2 * blocks, TILE), 0) % blocks
    wide[:, :TILE] = jnp.where(at == 0, 0.0, pltpu.roll(centre, 1, 0))
    wide[:, 2 * TILE :] = jnp.where(at == blocks - 1, 0.0, pltpu.roll(centre, 2 * blocks - 1, 0))
    offset = (
        lax.broadcasted_iota(jnp.int32, (3 * TILE, TILE), 1)
        + TILE
        - lax.broadcasted_iota(jnp.int32, (3 * TILE, TILE), 0)
    )
    nonzero = jnp.where(offset == 0, 1, offset).astype(F32)
    ramp = jnp.where((offset & 1) == 1, -1.0 / (math.pi * math.pi * nonzero * nonzero), 0.0)
    ramp = jnp.where(offset == 0, 0.25, ramp)
    ramp = jnp.where(jnp.abs(offset) < TILE, ramp, 0.0)
    done = jnp.dot(wide[...], ramp, precision=lax.Precision.HIGHEST, preferred_element_type=F32)
    wide[:, :TILE] = done.astype(BF16).astype(F32)
    filt[...] = jnp.zeros_like(filt)
    for h in range(2):
        for b in range(blocks):
            row = wide[h * blocks + b : h * blocks + b + 1, :TILE]
            filt[h, b] = jnp.broadcast_to(row, (8, TILE))

    def take(g, carry):
        mixed = []
        for i in range(per):
            for k in range(8):
                start = starts_ref[(g * per + i) * 8 + k]
                block, shift = start >> 7, start & (TILE - 1)
                value = jnp.where(lane >= shift, filt[k % 2, block], filt[k % 2, block + 1])
                mixed.append((value, (TILE - shift) & (TILE - 1)))
        turned = [pltpu.roll(value, shift, 1) for value, shift in mixed]
        for i in range(per):
            rows = turned[i * 8]
            for k in range(1, 8):
                rows = jnp.where(sub == k, turned[i * 8 + k], rows)
            staged[pl.ds(pl.multiple_of((g * per + i) * 8, 8), 8), :] = rows
        return carry

    lax.fori_loop(0, groups, take, 0)
    out_ref[...] = staged[...].astype(BF16)


def backward_kernel(
    base_ref, image0_ref, image1_ref, delta_ref, lanes_ref, got_ref, out_ref, left_ref, right_ref,
    rel, band0, band1, shadows, staged, update,
):
    slices = ROWS // 2
    pixel = lax.broadcasted_iota(jnp.int32, (PIX, BAND), 0)
    rel[...] = (
        (pixel // SIDE).astype(F32) * lanes_ref[0:1, :]
        + (pixel % SIDE).astype(F32) * lanes_ref[1:2, :]
    )
    staged[...] = got_ref[...].astype(F32)
    for a in range(ANGLES):
        parts = []
        for t in range(2):
            row = (a // 2) * 4 + t * 2 + a % 2
            parts.append(staged[pl.ds(row, slices, stride=ROWS), :])
        shadows[a] = jnp.concatenate(parts, axis=0).T

    def build(patch, band):
        shift = delta_ref[pl.ds(patch, 1), :]
        for r in range(0, PIX, 16):
            away = jnp.abs(rel[r : r + 16, :] + shift)
            band[r : r + 16, :] = jnp.maximum(0.0, 1.0 - away).astype(BF16)

    def spread(patch, band):
        row = patch // PATCHES
        col = patch % PATCHES
        pieces = []
        for a in range(ANGLES):
            start = pl.multiple_of(base_ref[patch * ANGLES + a], 8)
            pieces.append(shadows[a, pl.ds(start, BINS), :])
        seen = jnp.concatenate(pieces, axis=0).astype(BF16)
        got = jnp.dot(band[...], seen, preferred_element_type=F32)
        for u in range(SIDE):
            start = pl.multiple_of((row * SIDE + u) * TILE + col * SIDE, SIDE)
            update[pl.ds(start, SIDE), :] = got[u * SIDE : (u + 1) * SIDE, :]

    build(0, band0)

    def step(i, carry):
        build(2 * i + 1, band1)
        spread(2 * i, band0)
        build(jnp.minimum(2 * i + 2, PATCHES * PATCHES - 1), band0)
        spread(2 * i + 1, band1)
        return carry

    lax.fori_loop(0, PATCHES * PATCHES // 2, step, 0)

    lane = lax.broadcasted_iota(jnp.int32, (slices, TILE), 1)
    per = TILE // TV_STEPS

    def finish(g, carry):
        left = jnp.zeros((slices, TILE), F32)
        right = jnp.zeros((slices, TILE), F32)
        for j in range(per):
            u = g * per + j
            turned = update[pl.ds(pl.multiple_of(u * TILE, TILE), TILE), :].T
            for t in range(2):
                here = (image0_ref, image1_ref)[t][pl.ds(u, slices, stride=TILE), :]
                here = here + 0.25 * turned[t * slices : (t + 1) * slices, :]
                out_ref[u, :, t * TILE : (t + 1) * TILE] = here
                mine = (lane >= j * TV_STEPS) & (lane < (j + 1) * TV_STEPS)
                if t == 0:
                    left = jnp.where(mine, pltpu.roll(here, j * TV_STEPS, 1), left)
                else:
                    right = jnp.where(mine, pltpu.roll(here, (j + 1) * TV_STEPS % TILE, 1), right)
        left_ref[g] = left
        right_ref[g] = right
        return carry

    lax.fori_loop(0, TILE // per, finish, 0)


def smooth_kernel(
    place_ref, before_ref, after_ref, above_side_ref, below_side_ref, x_ref, above_ref, below_ref,
    out_ref, first, second, out0, out1, sems,
):
    slices = ROWS // 2
    high = TILE + 2 * TV_STEPS
    per = TILE // TV_STEPS
    width = 2 * TILE
    coming = [
        pltpu.make_async_copy(
            ref.at[pl.ds(0, count)], first.at[pl.ds(start, count), :, pl.ds(0, width)], sems.at[i]
        )
        for i, (ref, start, count) in enumerate(
            (
                (x_ref, TV_STEPS, TILE),
                (above_ref, 0, TV_STEPS),
                (below_ref, TILE + TV_STEPS, TV_STEPS),
            )
        )
    ]
    for copy in coming:
        copy.start()
    lane = lax.broadcasted_iota(jnp.int32, (slices, TILE), 1)
    has_above, has_below, has_before, has_after = (place_ref[i] for i in range(4))
    keep = ((lane < TV_STEPS) & (has_after == 1)) | (
        (lane >= TILE - TV_STEPS) & (has_before == 1)
    )

    def margin(previous, following, j):
        following = pltpu.roll(following, (TILE - j * TV_STEPS) % TILE, 1)
        previous = pltpu.roll(previous, (TILE - (j + 1) * TV_STEPS) % TILE, 1)
        return jnp.where(keep, jnp.where(lane < TV_STEPS, following, previous), 0.0)

    for r in range(TV_STEPS):
        for ref, start, j in (
            (above_side_ref, 0, per - TV_STEPS + r),
            (below_side_ref, TILE + TV_STEPS, r),
        ):
            first[start + r, :, width:] = margin(ref[:, :TILE], ref[:, TILE:], j)

    def load(g, carry):
        previous = before_ref[g]
        following = after_ref[g]
        for j in range(per):
            first[g * per + j + TV_STEPS, :, width:] = margin(previous, following, j)
        return carry

    lax.fori_loop(0, TILE // per, load, 0)
    for copy in coming:
        copy.wait()

    edge = lax.broadcasted_iota(jnp.int32, (1, slices, 3 * TILE), 2)
    keep_all = (
        (edge < width)
        | ((edge < width + TV_STEPS) & (has_after == 1))
        | ((edge >= 3 * TILE - TV_STEPS) & (has_before == 1))
    )

    def flows(here, under):
        down = under - here
        right = pltpu.roll(here, 3 * TILE - 1, here.ndim - 1) - here
        inverse = lax.rsqrt(smoothing * smoothing + down * down + right * right)
        return down * inverse, right * inverse

    for k in range(TV_STEPS):
        source, target = (first, second) if k % 2 == 0 else (second, first)
        last = k == TV_STEPS - 1

        def rows(r, count, came, inside, source=source, target=target, last=last):
            here = source[pl.ds(r, count)]
            down, right = flows(here, source[pl.ds(r + 1, count)])
            came = came[None]
            if count > 1:
                came = jnp.concatenate([came, down[:-1]], axis=0)
            change = came - down + pltpu.roll(right, 1, 2) - right
            fresh = here - descent_step * change
            if last:
                for i in range(count):
                    spot = pl.ds(r + i - TV_STEPS, slices, stride=TILE)
                    out0[spot, :] = fresh[i, :, :TILE]
                    out1[spot, :] = fresh[i, :, TILE:width]
            else:
                keep_here = keep_all if inside is None else keep_all & inside
                target[pl.ds(r, count)] = jnp.where(keep_here, fresh, 0.0)
            return down[count - 1]

        edges = TV_STEPS - 1 - k
        came, unused = flows(source[k], source[k + 1])
        if edges:
            came = rows(k + 1, edges, came, has_above == 1)
        block = 16

        def body(i, came):
            return rows(TV_STEPS + i * block, block, came, None)

        came = lax.fori_loop(0, TILE // block, body, came)
        if edges:
            rows(TILE + TV_STEPS, edges, came, has_below == 1)
    going = [
        pltpu.make_async_copy(ref, out_ref.at[:, pl.ds(t * TILE, TILE)], sems.at[t])
        for t, ref in enumerate((out0, out1))
    ]
    for copy in going:
        copy.start()
    for copy in going:
        copy.wait()


def call(
    kernel, scalars, arrays, outs, scratch, flops, halves=(), left=(), out_space=VMEM
):
    smem = pl.BlockSpec(memory_space=pltpu.SMEM)
    vmem = pl.BlockSpec(memory_space=VMEM)
    specs = [smem] * len(scalars)
    operands = list(scalars)
    for half in halves:
        for t in range(2):
            specs.append(pl.BlockSpec((half.shape[0], TILE), lambda i, t=t: (0, t)))
            operands.append(half)
    specs += [vmem] * len(arrays)
    operands += arrays
    specs += [pl.BlockSpec(memory_space=pl.ANY)] * len(left)
    operands += left
    moved = sum(x.size * x.dtype.itemsize for x in (*arrays, *halves, *left))
    return pl.pallas_call(
        kernel,
        grid=(1,),
        out_shape=outs,
        in_specs=specs,
        out_specs=jax.tree.map(lambda x: pl.BlockSpec(memory_space=out_space), outs),
        scratch_shapes=scratch,
        cost_estimate=pl.CostEstimate(flops=flops, bytes_accessed=moved, transcendentals=0),
    )(*operands)


def local(current_image, measured, ray_weight, angle_ids, shadow_start):
    row_index = lax.axis_index("row")
    col_index = lax.axis_index("col")
    rows = lax.axis_size("row")
    cols = lax.axis_size("col")
    slices = current_image.shape[0]
    both = ("row", "col")
    image = current_image.reshape(slices * TILE, 2 * TILE)
    cosine, sine, base, delta = geometry(angle_ids)
    base = base.reshape(-1)

    sent = call(
        forward_kernel,
        (base, delta.reshape(-1), jnp.stack([cosine, sine]), col_index.reshape(1)),
        (measured[:, 0], ray_weight[:, 0]),
        jax.ShapeDtypeStruct((rows * cols * MESSAGE, TILE), F32),
        [
            VMEM((TILE * TILE, ROWS), BF16),
            VMEM((BAND, PIX), F32),
            VMEM((BAND, PIX), BF16),
            VMEM((BAND, PIX), BF16),
            VMEM((ANGLES, TILE, ROWS), F32),
        ],
        30_000_000_000,
        halves=(image,),
    )
    got = lax.all_to_all(
        sent.reshape(rows * cols, MESSAGE, TILE), both, split_axis=0, concat_axis=0, tiled=True
    )
    blocks = rows
    starts = shadow_start.reshape(-1, ANGLES)
    starts = lax.dynamic_slice_in_dim(starts, col_index * 2, 2, 1).reshape(-1)
    out = call(
        owner_kernel,
        (starts, col_index.reshape(1)),
        (got.reshape(-1, TILE),),
        jax.ShapeDtypeStruct((rows * cols * 4, TILE), BF16),
        [
            VMEM((8, blocks, 8, TILE), F32),
            VMEM((8, blocks, 8, TILE), F32),
            VMEM((2 * blocks, 3 * TILE), F32),
            VMEM((2, blocks + 1, 8, TILE), F32),
            VMEM((rows * cols * 4, TILE), F32),
        ],
        10_000_000_000,
    )
    shadows = lax.all_to_all(
        out.reshape(rows * cols, 4, TILE), both, split_axis=0, concat_axis=0, tiled=True
    )
    bins = jnp.arange(BINS, dtype=F32)
    delta_lanes = (delta[:, :, None] - bins).reshape(-1, BAND)
    angle_lanes = jnp.repeat(jnp.stack([cosine, sine]), BINS, axis=1)
    groups = TV_STEPS
    side = jax.ShapeDtypeStruct((groups, slices, TILE), F32)
    x, left, right = call(
        backward_kernel,
        (base,),
        (delta_lanes, angle_lanes, shadows.reshape(-1, TILE)),
        (jax.ShapeDtypeStruct((TILE, slices, 2 * TILE), F32), side, side),
        [
            VMEM((PIX, BAND), F32),
            VMEM((PIX, BAND), BF16),
            VMEM((PIX, BAND), BF16),
            VMEM((ANGLES, TILE, ROWS), F32),
            VMEM((rows * cols * 4, TILE), F32),
            VMEM((TILE * TILE, ROWS), F32),
        ],
        30_000_000_000,
        halves=(image,),
    )
    right_going = [(i, i + 1) for i in range(cols - 1)]
    left_going = [(i + 1, i) for i in range(cols - 1)]
    before = lax.ppermute(right, "col", right_going)
    after = lax.ppermute(left, "col", left_going)
    upward = jnp.concatenate([before[0], after[0]], axis=1)[None]
    downward = jnp.concatenate([before[-1], after[-1]], axis=1)[None]
    top = jnp.concatenate([x[:TV_STEPS], upward], axis=0)
    bottom = jnp.concatenate([x[-TV_STEPS:], downward], axis=0)
    above = lax.ppermute(bottom, "row", [(i, i + 1) for i in range(rows - 1)])
    below = lax.ppermute(top, "row", [(i + 1, i) for i in range(rows - 1)])
    place = jnp.stack(
        [row_index > 0, row_index < rows - 1, col_index > 0, col_index < cols - 1]
    ).astype(jnp.int32)
    wide = VMEM((TILE + 2 * TV_STEPS, slices, 3 * TILE), F32)
    half = VMEM((slices * TILE, TILE), F32)
    smooth = call(
        smooth_kernel,
        (place,),
        (before, after, above[TV_STEPS], below[TV_STEPS]),
        jax.ShapeDtypeStruct((slices * TILE, 2 * TILE), F32),
        [wide, wide, half, half, pltpu.SemaphoreType.DMA((3,))],
        10_000_000_000,
        left=(x, above, below),
        out_space=pl.ANY,
    )
    return smooth.reshape(current_image.shape)


def solution(mesh):
    return jax.shard_map(
        local,
        mesh=mesh,
        in_specs=(
            P(None, "row", "col"),
            P("col", "row", None, None),
            P("col", "row", None),
            P(),
            P(),
        ),
        out_specs=P(None, "row", "col"),
        check_vma=False,
    )
```

```python
import functools
import math

import jax
import jax.numpy as jnp
from jax import lax
from jax.experimental import pallas as pl
from jax.experimental.pallas import tpu as pltpu
from jax.sharding import PartitionSpec as P

TILE = 128
ANGLES = 16
ALL_ANGLES = 256
TV_STEPS = 4
SIDE = 16
PATCHES = TILE // SIDE
PIX = SIDE * SIDE
BINS = 24
ROWS = 32
BAND = ANGLES * BINS
PAIRS = PATCHES * PATCHES // 2
CHUNK = 16
MESSAGE = 8

inverse_root = 0.7071067811865476
smoothing = 0.25
descent_step = 0.05

VMEM = pltpu.VMEM
F32 = jnp.float32
BF16 = jnp.bfloat16


def geometry(angle_ids):
    radians = angle_ids.astype(F32) * (math.pi / ALL_ANGLES)
    cosine = jnp.cos(radians)[None] * inverse_root
    sine = jnp.sin(radians)[None] * inverse_root
    row = lax.broadcasted_iota(jnp.int32, (2 * PAIRS + 2, ANGLES), 0)
    patch = row % PAIRS
    down = (patch // PATCHES).astype(F32) * SIDE - (TILE - 1) / 2.0
    across = (patch % PATCHES).astype(F32) * SIDE - (TILE - 1) / 2.0
    corner = TILE / 2.0 + down * cosine + across * sine
    low = corner + (SIDE - 1) * (jnp.minimum(cosine, 0.0) + jnp.minimum(sine, 0.0))
    base = jnp.clip(jnp.floor((jnp.floor(low - 1.5) + 1.0) / 8.0) * 8.0, 0.0, TILE - BINS)
    delta = corner - base - 0.5
    ends = jnp.where(row == 2 * PAIRS, cosine, sine)
    return jnp.where(row < PAIRS, base, jnp.where(row < 2 * PAIRS, delta, ends))


def reversal():
    there = lax.broadcasted_iota(jnp.int32, (TILE, TILE), 0)
    here = lax.broadcasted_iota(jnp.int32, (TILE, TILE), 1)
    return jnp.where(there + here == TILE - 1, 1.0, 0.0).astype(BF16)


def reverse_lanes(value):
    high = value.astype(BF16)
    low = (value - high.astype(F32)).astype(BF16)
    both = jnp.concatenate([high, low], axis=1)
    turn = reversal()
    return jnp.dot(both, jnp.concatenate([turn, turn], axis=0), preferred_element_type=F32)


def halves_of(image, targets, sems):
    return [
        pltpu.make_async_copy(image.at[:, pl.ds(t * TILE, TILE)], target, sems.at[t])
        for t, target in enumerate(targets)
    ]


def forward_kernel(
    table_ref, own_ref, measured_ref, weight_ref, image_ref,
    out_ref, xt, rel, band0, band1, sums, tails, image0_ref, image1_ref, sems,
):
    coming = halves_of(image_ref, (image0_ref, image1_ref), sems)
    for copy in coming:
        copy.start()
    slices = ROWS // 2
    lane = lax.broadcasted_iota(jnp.int32, (BINS, PIX), 1)
    bin_at = lax.broadcasted_iota(jnp.int32, (BINS, PIX), 0).astype(F32)
    down = (lane // SIDE).astype(F32)
    across = (lane % SIDE).astype(F32)
    for a in range(ANGLES):
        rel[a * BINS : (a + 1) * BINS, :] = (
            down * table_ref[2 * PAIRS, a] + across * table_ref[2 * PAIRS + 1, a] - bin_at
        )
    sums[...] = jnp.zeros_like(sums)
    turn = reversal()
    for copy in coming:
        copy.wait()

    def rows_of(u):
        both = [ref[pl.ds(u, slices, stride=TILE), :] for ref in (image0_ref, image1_ref)]
        return jnp.concatenate(both, axis=0)

    def flip(i, carry):
        u0 = (i // SIDE) * 2 * SIDE + i % SIDE
        u1 = u0 + SIDE
        mirrored = jnp.concatenate([rows_of(TILE - 1 - u0), rows_of(TILE - 1 - u1)], axis=0)
        mirrored = jnp.dot(mirrored.astype(BF16), turn, preferred_element_type=F32)
        stacked = jnp.concatenate(
            [rows_of(u0), mirrored[:ROWS], rows_of(u1), mirrored[ROWS:]], axis=0
        )
        xt[pl.ds(pl.multiple_of(i * TILE, TILE), TILE), :] = stacked.astype(BF16).T
        return carry

    lax.fori_loop(0, 2 * SIDE, flip, 0, unroll=4)

    def build(patch, band):
        for a in range(0, ANGLES, 2):
            pair = []
            for b in (a, a + 1):
                away = jnp.abs(rel[b * BINS : (b + 1) * BINS, :] + table_ref[PAIRS + patch, b])
                pair.append(jnp.maximum(0.0, 1.0 - away))
            band[a * BINS : (a + 2) * BINS, :] = jnp.concatenate(pair, axis=0).astype(BF16)

    first_half = lax.broadcasted_iota(jnp.int32, (PIX, TILE), 1) < TILE // 2

    def project(patch, band, half, col, own):
        pieces = []
        for u in range(SIDE):
            start = pl.multiple_of((half * SIDE + u) * TILE + col * SIDE, SIDE)
            pieces.append(xt[pl.ds(start, SIDE), :])
        pixels = jnp.concatenate(pieces, axis=0)
        nothing = jnp.zeros_like(pixels)
        pixels = jnp.where(first_half, *((nothing, pixels) if own else (pixels, nothing)))
        got = jnp.dot(band[...], pixels, preferred_element_type=F32)
        for a in range(ANGLES):
            start = pl.multiple_of(table_ref[patch, a].astype(jnp.int32), 8)
            sums[a, pl.ds(start, BINS), :] += got[a * BINS : (a + 1) * BINS, :]

    def patch_of(i):
        return (i // PATCHES) * 2 * PATCHES + i % PATCHES

    build(0, band0)

    def step(i, carry):
        half = i // PATCHES
        col = i % PATCHES
        patch = patch_of(i)
        build(patch + PATCHES, band1)
        project(patch, band0, half, col, 0)
        build(patch_of(jnp.minimum(i + 1, 2 * PATCHES - 1)), band0)
        project(patch + PATCHES, band1, half, col, 1)
        return carry

    lax.fori_loop(0, 2 * PATCHES, step, 0)
    stride = MESSAGE * ANGLES // 2
    for a in range(ANGLES):
        tails[a * TILE : (a + 1) * TILE, :] = sums[a].T * 0.03125
    mirrored = [
        tails[a * TILE + ROWS : a * TILE + 2 * ROWS, :]
        + tails[a * TILE + 3 * ROWS : (a + 1) * TILE, :]
        for a in range(ANGLES)
    ]
    mirrored = reverse_lanes(jnp.concatenate(mirrored, axis=0))
    for a in range(ANGLES):
        total = tails[a * TILE : a * TILE + ROWS, :] + tails[a * TILE + 2 * ROWS : a * TILE + 3 * ROWS, :]
        total = total + mirrored[a * ROWS : (a + 1) * ROWS, :]
        for t in range(2):
            row = (a // 2) * MESSAGE + t * 2 + a % 2
            out_ref[pl.ds(row, slices, stride=stride), :] = total[t * slices : (t + 1) * slices, :]
    row = own_ref[0] * MESSAGE + 4
    for h in range(2):
        out_ref[pl.ds(row + h, slices, stride=stride), :] = measured_ref[h]
        weight = jnp.broadcast_to(weight_ref[h : h + 1, :], (slices, TILE))
        out_ref[pl.ds(row + 2 + h, slices, stride=stride), :] = weight


def owner_kernel(starts_ref, own_ref, got_ref, out_ref, wide, filt, staged, *sums):
    low, high = sums[:8], sums[8:]
    blocks = 16
    per = 8
    groups = staged.shape[0] // (8 * per)
    for ref in sums:
        ref[...] = jnp.zeros_like(ref)
    lane = lax.broadcasted_iota(jnp.int32, (8, TILE), 1)
    sub = lax.broadcasted_iota(jnp.int32, (8, TILE), 0)

    def add(g, carry):
        turned = []
        for i in range(2 * per):
            source = g * 2 * per + i
            rows = got_ref[pl.ds(pl.multiple_of(source * MESSAGE, MESSAGE), MESSAGE), :]
            for k in range(4):
                start = starts_ref[source * 4 + k]
                turned.append((start >> 7, start & (TILE - 1), rows, i % 2 * 4 + k, k))
        turned = [
            (block, shift, pltpu.roll(rows, shift, 1), slot) for block, shift, rows, slot, k in turned
        ]
        for block, shift, value, slot in turned:
            tail = jnp.where(lane >= shift, value, 0.0)
            low[slot][block] += tail
            high[slot][block] += value - tail
        return carry

    lax.fori_loop(0, groups, add, 0)
    wide[...] = jnp.zeros_like(wide)
    for b in range(blocks):
        total = jnp.zeros((8, TILE), F32)
        for slot in range(8):
            here = low[slot][b]
            if b:
                here = here + high[slot][b - 1]
            total = total + jnp.where(sub == slot % 4, here, 0.0)
        home = pl.multiple_of((b * 8 + own_ref[0]) * MESSAGE, MESSAGE)
        given = got_ref[pl.ds(home, MESSAGE), :]
        for h in range(2):
            row = total[h : h + 1, :] + total[2 + h : 3 + h, :]
            wide[h * blocks + b : h * blocks + b + 1, TILE : 2 * TILE] = given[6 + h : 7 + h, :] * (
                given[4 + h : 5 + h, :] - row
            )
    centre = wide[:, TILE : 2 * TILE]
    at = lax.broadcasted_iota(jnp.int32, (2 * blocks, TILE), 0) % blocks
    wide[:, :TILE] = jnp.where(at == 0, 0.0, pltpu.roll(centre, 1, 0))
    wide[:, 2 * TILE :] = jnp.where(at == blocks - 1, 0.0, pltpu.roll(centre, 2 * blocks - 1, 0))
    offset = (
        lax.broadcasted_iota(jnp.int32, (3 * TILE, TILE), 1)
        + TILE
        - lax.broadcasted_iota(jnp.int32, (3 * TILE, TILE), 0)
    )
    nonzero = jnp.where(offset == 0, 1, offset).astype(F32)
    ramp = jnp.where((offset & 1) == 1, -1.0 / (math.pi * math.pi * nonzero * nonzero), 0.0)
    ramp = jnp.where(offset == 0, 0.25, ramp)
    ramp = jnp.where(jnp.abs(offset) < TILE, ramp, 0.0)
    done = jnp.dot(wide[...], ramp, precision=lax.Precision.HIGHEST, preferred_element_type=F32)
    wide[:, :TILE] = done.astype(BF16).astype(F32)
    filt[...] = jnp.zeros_like(filt)
    for h in range(2):
        for b in range(blocks):
            row = wide[h * blocks + b : h * blocks + b + 1, :TILE]
            filt[h, b] = jnp.broadcast_to(row, (8, TILE))

    def take(g, carry):
        mixed = []
        for i in range(per):
            for k in range(8):
                start = starts_ref[(g * per + i) * 8 + k]
                block, shift = start >> 7, start & (TILE - 1)
                value = jnp.where(lane >= shift, filt[k % 2, block], filt[k % 2, block + 1])
                mixed.append((value, (TILE - shift) & (TILE - 1)))
        turned = [pltpu.roll(value, shift, 1) for value, shift in mixed]
        for i in range(per):
            rows = turned[i * 8]
            for k in range(1, 8):
                rows = jnp.where(sub == k, turned[i * 8 + k], rows)
            staged[pl.ds(pl.multiple_of((g * per + i) * 8, 8), 8), :] = rows
        return carry

    lax.fori_loop(0, groups, take, 0)
    out_ref[...] = staged[...].astype(BF16)


def backward_kernel(
    table_ref, delta_ref, lanes_ref, got_ref, image_ref, final_ref, left_ref, right_ref,
    rel, band0, band1, shadows, staged, mirror, update, out_ref, image0_ref, image1_ref, sems,
):
    slices = ROWS // 2
    coming = halves_of(image_ref, (image0_ref, image1_ref), sems)
    for copy in coming:
        copy.start()
    pixel = lax.broadcasted_iota(jnp.int32, (PIX, BAND), 0)
    rel[...] = (
        (pixel // SIDE).astype(F32) * lanes_ref[0:1, :]
        + (pixel % SIDE).astype(F32) * lanes_ref[1:2, :]
    )
    staged[...] = got_ref[...].astype(F32)
    mirror[...] = jnp.dot(got_ref[...], reversal(), preferred_element_type=F32)
    for a in range(ANGLES):
        parts = []
        for ref in (staged, mirror):
            for t in range(2):
                row = (a // 2) * 4 + t * 2 + a % 2
                parts.append(ref[pl.ds(row, slices, stride=ROWS), :])
        shadows[a] = jnp.concatenate(parts + parts, axis=0).T

    def build(patch, band):
        shift = delta_ref[pl.ds(patch, 1), :]
        for r in range(0, PIX, 16):
            away = jnp.abs(rel[r : r + 16, :] + shift)
            band[r : r + 16, :] = jnp.maximum(0.0, 1.0 - away).astype(BF16)

    def spread(patch, band, half, col, own):
        pieces = []
        for a in range(ANGLES):
            start = pl.multiple_of(table_ref[patch, a].astype(jnp.int32), 8)
            pieces.append(shadows[a, pl.ds(start, BINS), :])
        seen = jnp.concatenate(pieces, axis=0).astype(BF16)
        got = jnp.dot(band[...], seen, preferred_element_type=F32)
        for u in range(SIDE):
            start = pl.multiple_of((half * SIDE + u) * TILE + col * SIDE, SIDE)
            piece = got[u * SIDE : (u + 1) * SIDE, :]
            if own:
                update[pl.ds(start, SIDE), TILE // 2 :] = piece[:, TILE // 2 :]
            else:
                update[pl.ds(start, SIDE), :] = piece

    def patch_of(i):
        return (i // PATCHES) * 2 * PATCHES + i % PATCHES

    build(0, band0)

    def step(i, carry):
        half = i // PATCHES
        col = i % PATCHES
        patch = patch_of(i)
        build(patch + PATCHES, band1)
        spread(patch, band0, half, col, 0)
        build(patch_of(jnp.minimum(i + 1, 2 * PATCHES - 1)), band0)
        spread(patch + PATCHES, band1, half, col, 1)
        return carry

    lax.fori_loop(0, 2 * PATCHES, step, 0)

    def finish(i, carry):
        u0 = (i // SIDE) * 2 * SIDE + i % SIDE
        u1 = u0 + SIDE
        turned = update[pl.ds(pl.multiple_of(i * TILE, TILE), TILE), :].T
        mirrored = jnp.concatenate([turned[ROWS : 2 * ROWS], turned[3 * ROWS :]], axis=0)
        mirrored = reverse_lanes(mirrored)
        for u, value in (
            (u0, turned[:ROWS]),
            (u1, turned[2 * ROWS : 3 * ROWS]),
            (TILE - 1 - u0, mirrored[:ROWS]),
            (TILE - 1 - u1, mirrored[ROWS:]),
        ):
            for t, ref in enumerate((image0_ref, image1_ref)):
                here = ref[pl.ds(u, slices, stride=TILE), :]
                here = here + 0.25 * value[t * slices : (t + 1) * slices, :]
                out_ref[u, :, t * TILE : (t + 1) * TILE] = here
        return carry

    def leave(start, count, sem):
        spot = pl.ds(start, count)
        return pltpu.make_async_copy(out_ref.at[spot], final_ref.at[spot], sems.at[sem])

    for copy in coming:
        copy.wait()
    lax.fori_loop(0, SIDE, finish, 0, unroll=2)
    going = [leave(0, 2 * SIDE, 2), leave(TILE - 2 * SIDE, 2 * SIDE, 3)]
    for copy in going:
        copy.start()
    lax.fori_loop(SIDE, 2 * SIDE, finish, 0, unroll=2)
    going.append(leave(2 * SIDE, TILE - 4 * SIDE, 4))
    going[-1].start()

    lane = lax.broadcasted_iota(jnp.int32, (slices, TILE), 1)
    per = TILE // TV_STEPS

    def sides(g, carry):
        left = jnp.zeros((slices, TILE), F32)
        right = jnp.zeros((slices, TILE), F32)
        for j in range(per):
            u = g * per + j
            mine = (lane >= j * TV_STEPS) & (lane < (j + 1) * TV_STEPS)
            left = jnp.where(mine, pltpu.roll(out_ref[u, :, :TILE], j * TV_STEPS, 1), left)
            shift = (j + 1) * TV_STEPS % TILE
            right = jnp.where(mine, pltpu.roll(out_ref[u, :, TILE:], shift, 1), right)
        left_ref[g] = left
        right_ref[g] = right
        return carry

    lax.fori_loop(0, TILE // per, sides, 0)
    for copy in going:
        copy.wait()


def smooth_kernel(
    place_ref, before_ref, after_ref, above_ref, below_ref, x_ref,
    out_ref, first, second, out0, out1, sems,
):
    per = TILE // TV_STEPS
    half = TILE // 2
    width = 2 * TILE
    coming = [
        pltpu.make_async_copy(
            x_ref.at[:, pl.ds(h * 8, 8), :],
            first.at[pl.ds(TV_STEPS, TILE), :, pl.ds(h * width, width)],
            sems.at[h],
        )
        for h in range(2)
    ]
    for copy in coming:
        copy.start()
    lane = lax.broadcasted_iota(jnp.int32, (8, TILE), 1)
    has_above, has_below, has_before, has_after = (place_ref[i] for i in range(4))
    folded = lane & (half - 1)
    keep = ((folded < TV_STEPS) & (has_after == 1)) | (
        (folded >= half - TV_STEPS) & (has_before == 1)
    )

    def margin(previous, following, j):
        def spot(value, lanes):
            return pltpu.roll(value, (lanes - j * TV_STEPS) % TILE, 1)

        following = jnp.where(
            lane < half, spot(following[:8], 0), spot(following[8:], half)
        )
        previous = jnp.where(
            lane < half, spot(previous[8:], half - TV_STEPS), spot(previous[:8], -TV_STEPS)
        )
        return jnp.where(keep, jnp.where(folded < TV_STEPS, following, previous), 0.0)

    for r in range(TV_STEPS):
        for ref, start, j in (
            (above_ref, 0, per - TV_STEPS + r),
            (below_ref, TILE + TV_STEPS, r),
        ):
            for h in range(2):
                first[start + r, :, h * width : (h + 1) * width] = ref[r, h * 8 : (h + 1) * 8, :]
            first[start + r, :, 2 * width :] = margin(
                ref[TV_STEPS, :, :TILE], ref[TV_STEPS, :, TILE:], j
            )

    def load(g, carry):
        previous = before_ref[g]
        following = after_ref[g]
        for j in range(per):
            first[g * per + j + TV_STEPS, :, 2 * width :] = margin(previous, following, j)
        return carry

    lax.fori_loop(0, TILE // per, load, 0)
    for copy in coming:
        copy.wait()

    def roll(value, shift):
        return pltpu.roll(value.reshape(-1, TILE), shift, 1).reshape(value.shape)

    def blocks_of(ref, r, count):
        return [ref[pl.ds(r, count), :, i * TILE : (i + 1) * TILE] for i in range(5)]

    end = (lane == TILE - 1)[None]
    middle = (lane == half - 1)[None]

    def next_column(tiles):
        a0, a1, b0, b1, m = (roll(t, TILE - 1) for t in tiles)
        return [
            jnp.where(end, a1, a0),
            jnp.where(end, m, a1),
            jnp.where(end, b1, b0),
            jnp.where(end, roll(tiles[4], half - 1), b1),
            jnp.where(end, a0, jnp.where(middle, roll(tiles[2], half - 1), m)),
        ]

    begin = (lane == 0)[None]
    centre = (lane == half)[None]

    def previous_column(tiles):
        a0, a1, b0, b1, m = (roll(t, 1) for t in tiles)
        return [
            jnp.where(begin, m, a0),
            jnp.where(begin, a0, a1),
            jnp.where(begin, roll(tiles[4], half + 1), b0),
            jnp.where(begin, b0, b1),
            jnp.where(begin, a1, jnp.where(centre, roll(tiles[3], half + 1), m)),
        ]

    def flows(here, under):
        downs, rights = [], []
        for h, u, n in zip(here, under, next_column(here)):
            down = u - h
            right = n - h
            inverse = lax.rsqrt(smoothing * smoothing + down * down + right * right)
            downs.append(down * inverse)
            rights.append(right * inverse)
        return downs, rights

    for k in range(TV_STEPS):
        source, target = (first, second) if k % 2 == 0 else (second, first)
        last = k == TV_STEPS - 1

        def rows(r, count, came, inside, source=source, target=target, last=last):
            here = blocks_of(source, r, count)
            downs, rights = flows(here, blocks_of(source, r + 1, count))
            for i, (h, down, right, left) in enumerate(
                zip(here, downs, rights, previous_column(rights))
            ):
                above = came[i][None]
                if count > 1:
                    above = jnp.concatenate([above, down[:-1]], axis=0)
                fresh = h - descent_step * (above - down + left - right)
                if last:
                    if i < 4:
                        for c in range(count):
                            start = (i // 2) * 8 * TILE + r + c - TV_STEPS
                            (out0, out1)[i % 2][pl.ds(start, 8, stride=TILE), :] = fresh[c]
                    continue
                kept = keep[None] if i == 4 else None
                if inside is not None:
                    kept = inside if kept is None else kept & inside
                if kept is not None:
                    fresh = jnp.where(kept, fresh, 0.0)
                target[pl.ds(r, count), :, i * TILE : (i + 1) * TILE] = fresh
            return [down[count - 1] for down in downs]

        edges = TV_STEPS - 1 - k
        came, unused = flows(blocks_of(source, k, 1), blocks_of(source, k + 1, 1))
        came = [c[0] for c in came]
        if edges:
            came = rows(k + 1, edges, came, has_above == 1)

        def body(i, came):
            return rows(TV_STEPS + i * CHUNK, CHUNK, came, None)

        came = lax.fori_loop(0, TILE // CHUNK, body, came)
        if edges:
            rows(TILE + TV_STEPS, edges, came, has_below == 1)
    going = [
        pltpu.make_async_copy(ref, out_ref.at[:, pl.ds(t * TILE, TILE)], sems.at[t])
        for t, ref in enumerate((out0, out1))
    ]
    for copy in going:
        copy.start()
    for copy in going:
        copy.wait()


def call(kernel, scalars, arrays, left, outs, scratch, flops):
    vmem = pl.BlockSpec(memory_space=VMEM)
    stays = pl.BlockSpec(memory_space=pl.ANY)
    smem = pl.BlockSpec(memory_space=pltpu.SMEM)
    operands = (*scalars, *arrays, *left)
    moved = sum(x.size * x.dtype.itemsize for x in operands)
    big = 1 << 20
    return pl.pallas_call(
        kernel,
        out_shape=outs,
        in_specs=[smem] * len(scalars) + [vmem] * len(arrays) + [stays] * len(left),
        out_specs=jax.tree.map(lambda x: stays if x.size * 4 > big else vmem, outs),
        scratch_shapes=scratch,
        cost_estimate=pl.CostEstimate(flops=flops, bytes_accessed=moved, transcendentals=0),
    )(*operands)


def local(current_image, measured, ray_weight, angle_ids, shadow_start):
    row_index = lax.axis_index("row")
    col_index = lax.axis_index("col")
    rows = lax.axis_size("row")
    cols = lax.axis_size("col")
    slices = current_image.shape[0]
    both = ("row", "col")
    image = current_image.reshape(slices * TILE, 2 * TILE)
    table = geometry(angle_ids)
    half = VMEM((slices * TILE, TILE), F32)
    band = VMEM((BAND, PIX), BF16)

    sent = call(
        forward_kernel,
        (table, col_index.reshape(1)),
        (measured[:, 0], ray_weight[:, 0]),
        (image,),
        jax.ShapeDtypeStruct((rows * cols * MESSAGE, TILE), F32),
        [
            VMEM((2 * SIDE * TILE, TILE), BF16),
            VMEM((BAND, PIX), F32),
            band,
            band,
            VMEM((ANGLES, TILE, TILE), F32),
            VMEM((ANGLES * TILE, TILE), F32),
            half,
            half,
            pltpu.SemaphoreType.DMA((2,)),
        ],
        30_000_000_000,
    )
    got = lax.all_to_all(
        sent.reshape(rows * cols, MESSAGE, TILE), both, split_axis=0, concat_axis=0, tiled=True
    )
    blocks = rows
    starts = shadow_start.reshape(-1, ANGLES)
    starts = lax.dynamic_slice_in_dim(starts, col_index * 2, 2, 1).reshape(-1)
    out = call(
        owner_kernel,
        (starts, col_index.reshape(1)),
        (got.reshape(-1, TILE),),
        (),
        jax.ShapeDtypeStruct((rows * cols * 4, TILE), BF16),
        [
            VMEM((2 * blocks, 3 * TILE), F32),
            VMEM((2, blocks + 1, 8, TILE), F32),
            VMEM((rows * cols * 4, TILE), F32),
        ]
        + [VMEM((blocks, 8, TILE), F32)] * 16,
        10_000_000_000,
    )
    shadows = lax.all_to_all(
        out.reshape(rows * cols, 4, TILE), both, split_axis=0, concat_axis=0, tiled=True
    )
    bins = jnp.arange(BINS, dtype=F32)
    delta_lanes = (table[PAIRS : 2 * PAIRS, :, None] - bins).reshape(-1, BAND)
    angle_lanes = jnp.repeat(table[2 * PAIRS :], BINS, axis=1)
    side = jax.ShapeDtypeStruct((TV_STEPS, slices, TILE), F32)
    whole = VMEM((TILE, slices, 2 * TILE), F32)
    x, left, right = call(
        backward_kernel,
        (table,),
        (delta_lanes, angle_lanes, shadows.reshape(-1, TILE)),
        (image,),
        (jax.ShapeDtypeStruct(whole.shape, F32), side, side),
        [
            VMEM((PIX, BAND), F32),
            VMEM((PIX, BAND), BF16),
            VMEM((PIX, BAND), BF16),
            VMEM((ANGLES, TILE, TILE), F32),
            VMEM((rows * cols * 4, TILE), F32),
            VMEM((rows * cols * 4, TILE), F32),
            VMEM((2 * SIDE * TILE, TILE), F32),
            whole,
            half,
            half,
            pltpu.SemaphoreType.DMA((5,)),
        ],
        30_000_000_000,
    )
    before = lax.ppermute(right, "col", [(i, i + 1) for i in range(cols - 1)])
    after = lax.ppermute(left, "col", [(i + 1, i) for i in range(cols - 1)])
    upward = jnp.concatenate([before[0], after[0]], axis=1)[None]
    downward = jnp.concatenate([before[-1], after[-1]], axis=1)[None]
    top = jnp.concatenate([x[:TV_STEPS], upward], axis=0)
    bottom = jnp.concatenate([x[-TV_STEPS:], downward], axis=0)
    above = lax.ppermute(bottom, "row", [(i, i + 1) for i in range(rows - 1)])
    below = lax.ppermute(top, "row", [(i + 1, i) for i in range(rows - 1)])
    place = jnp.stack(
        [row_index > 0, row_index < rows - 1, col_index > 0, col_index < cols - 1]
    ).astype(jnp.int32)
    wide = VMEM((TILE + 2 * TV_STEPS, 8, 5 * TILE), F32)
    smooth = call(
        smooth_kernel,
        (place,),
        (before, after, above, below),
        (x,),
        jax.ShapeDtypeStruct((slices * TILE, 2 * TILE), F32),
        [wide, wide, half, half, pltpu.SemaphoreType.DMA((2,))],
        10_000_000_000,
    )
    return smooth.reshape(current_image.shape)


def solution(mesh):
    return jax.shard_map(
        local,
        mesh=mesh,
        in_specs=(
            P(None, "row", "col"),
            P("col", "row", None, None),
            P("col", "row", None),
            P(),
            P(),
        ),
        out_specs=P(None, "row", "col"),
        check_vma=False,
    )
```

```python
import functools
import math

import jax
import jax.numpy as jnp
from jax import lax
from jax.experimental import pallas as pl
from jax.experimental.pallas import tpu as pltpu
from jax.sharding import PartitionSpec as P

TILE = 128
ANGLES = 16
ALL_ANGLES = 256
TV_STEPS = 4
SIDE = 16
PATCHES = TILE // SIDE
PIX = SIDE * SIDE
BINS = 24
ROWS = 32
BAND = ANGLES * BINS
PAIRS = PATCHES * PATCHES // 2
MESSAGE = 8

inverse_root = 0.7071067811865476
smoothing = 0.25
descent_step = 0.05

VMEM = pltpu.VMEM
F32 = jnp.float32
BF16 = jnp.bfloat16


def geometry(angle_ids):
    radians = angle_ids.astype(F32) * (math.pi / ALL_ANGLES)
    cosine = jnp.cos(radians)[None] * inverse_root
    sine = jnp.sin(radians)[None] * inverse_root
    row = lax.broadcasted_iota(jnp.int32, (2 * PAIRS + 2, ANGLES), 0)
    patch = row % PAIRS
    down = (patch // PATCHES).astype(F32) * SIDE - (TILE - 1) / 2.0
    across = (patch % PATCHES).astype(F32) * SIDE - (TILE - 1) / 2.0
    corner = TILE / 2.0 + down * cosine + across * sine
    low = corner + (SIDE - 1) * (jnp.minimum(cosine, 0.0) + jnp.minimum(sine, 0.0))
    base = jnp.clip(jnp.floor((jnp.floor(low - 1.5) + 1.0) / 8.0) * 8.0, 0.0, TILE - BINS)
    delta = corner - base - 0.5
    ends = jnp.where(row == 2 * PAIRS, cosine, sine)
    return jnp.where(row < PAIRS, base, jnp.where(row < 2 * PAIRS, delta, ends))


def reversal():
    there = lax.broadcasted_iota(jnp.int32, (TILE, TILE), 0)
    here = lax.broadcasted_iota(jnp.int32, (TILE, TILE), 1)
    return jnp.where(there + here == TILE - 1, 1.0, 0.0).astype(BF16)


def reverse_lanes(value):
    high = value.astype(BF16)
    low = (value - high.astype(F32)).astype(BF16)
    both = jnp.concatenate([high, low], axis=1)
    turn = reversal()
    return jnp.dot(both, jnp.concatenate([turn, turn], axis=0), preferred_element_type=F32)


def pipeline(build, use, bands):
    def pair(i, action, slots):
        half = i // PATCHES
        col = i % PATCHES
        for own in range(2):
            patch = (2 * half + own) * PATCHES + col
            if action is build:
                build(patch, bands.at[slots + own])
            else:
                use(patch, bands.at[slots + own], half, col, own)

    pair(0, build, 0)

    def step(i, carry):
        pair(2 * i + 1, build, 2)
        pair(2 * i, use, 0)
        pair(jnp.minimum(2 * i + 2, 2 * PATCHES - 1), build, 0)
        pair(2 * i + 1, use, 2)
        return carry

    lax.fori_loop(0, PATCHES, step, 0)


def blocks_at(half):
    return 2 * half, PATCHES - 1 - 2 * half, 2 * half + 1, PATCHES - 2 - 2 * half


def reflected(ref, i):
    other = (i // SIDE) * SIDE + SIDE - 1 - i % SIDE
    back = 7 - lax.broadcasted_iota(jnp.int32, (8, TILE), 0)
    mirrored = lax.broadcasted_iota(jnp.int32, (8, TILE), 1) & ROWS != 0
    parts = []
    for g in range(TILE // 8):
        far = ref[other, TILE - 8 * (g + 1) : TILE - 8 * g, :]
        far = jnp.take_along_axis(far, back, axis=0)
        parts.append(jnp.where(mirrored, far, ref[i, 8 * g : 8 * (g + 1), :]))
    return jnp.concatenate(parts, axis=0)


def halves_of(image, targets, sems):
    return [
        pltpu.make_async_copy(image.at[:, pl.ds(t * TILE, TILE)], target, sems.at[t])
        for t, target in enumerate(targets)
    ]


def forward_kernel(
    table_ref, own_ref, measured_ref, weight_ref, image_ref,
    out_ref, turned_ref, xt, rel, bands, tails, message, image0_ref, image1_ref, flat, sems,
    *sums,
):
    coming = halves_of(image_ref, (image0_ref, image1_ref), sems)
    for copy in coming:
        copy.start()
    slices = ROWS // 2
    lane = lax.broadcasted_iota(jnp.int32, (BINS, PIX), 1)
    bin_at = lax.broadcasted_iota(jnp.int32, (BINS, PIX), 0).astype(F32)
    down = (lane // SIDE).astype(F32)
    across = (lane % SIDE).astype(F32)
    for a in range(ANGLES):
        rel[a * BINS : (a + 1) * BINS, :] = (
            down * table_ref[2 * PAIRS, a] + across * table_ref[2 * PAIRS + 1, a] - bin_at
        )
    for ref in sums:
        ref[...] = jnp.zeros_like(ref)
    for copy in coming:
        copy.wait()

    def rows_of(u):
        return [ref[pl.ds(u, slices, stride=TILE), :] for ref in (image0_ref, image1_ref)]

    def flip(i, carry):
        rows = []
        for block in blocks_at(i // SIDE):
            rows += rows_of(block * SIDE + i % SIDE)
        flat[i] = jnp.concatenate(rows, axis=0).T
        return carry

    lax.fori_loop(0, 2 * SIDE, flip, 0, unroll=4)
    going = pltpu.make_async_copy(flat, turned_ref, sems.at[2])
    going.start()

    def reflect(i, carry):
        value = reflected(flat, i)
        xt[pl.ds(pl.multiple_of(i * TILE, TILE), TILE), :] = value.astype(BF16)
        return carry

    lax.fori_loop(0, 2 * SIDE, reflect, 0, unroll=2)

    def build(patch, band):
        for a in range(0, ANGLES, 2):
            pair = []
            for b in (a, a + 1):
                away = jnp.abs(rel[b * BINS : (b + 1) * BINS, :] + table_ref[PAIRS + patch, b])
                pair.append(jnp.maximum(0.0, 1.0 - away))
            band[a * BINS : (a + 2) * BINS, :] = jnp.concatenate(pair, axis=0).astype(BF16)

    first_half = lax.broadcasted_iota(jnp.int32, (PIX, TILE), 1) < TILE // 2

    def project(patch, band, half, col, own):
        pieces = []
        for u in range(SIDE):
            start = pl.multiple_of((half * SIDE + u) * TILE + col * SIDE, SIDE)
            pieces.append(xt[pl.ds(start, SIDE), :])
        pixels = jnp.concatenate(pieces, axis=0)
        nothing = jnp.zeros_like(pixels)
        pixels = jnp.where(first_half, *((nothing, pixels) if own else (pixels, nothing)))
        got = jnp.dot(band[...], pixels, preferred_element_type=F32)
        for a in range(ANGLES):
            start = pl.multiple_of(table_ref[patch, a].astype(jnp.int32), 8)
            sums[a][pl.ds(start, BINS), :] += got[a * BINS : (a + 1) * BINS, :]

    pipeline(build, project, bands)
    stride = MESSAGE * ANGLES // 2
    for a in range(ANGLES):
        tails[a * TILE : (a + 1) * TILE, :] = sums[a][...].T * 0.03125
    mirrored = [
        tails[a * TILE + ROWS : a * TILE + 2 * ROWS, :]
        + tails[a * TILE + 3 * ROWS : (a + 1) * TILE, :]
        for a in range(ANGLES)
    ]
    mirrored = reverse_lanes(jnp.concatenate(mirrored, axis=0))
    for a in range(ANGLES):
        total = tails[a * TILE : a * TILE + ROWS, :] + tails[a * TILE + 2 * ROWS : a * TILE + 3 * ROWS, :]
        total = total + mirrored[a * ROWS : (a + 1) * ROWS, :]
        for t in range(2):
            row = (a // 2) * MESSAGE + t * 2 + a % 2
            message[pl.ds(row, slices, stride=stride), :] = total[t * slices : (t + 1) * slices, :]
    row = own_ref[0] * MESSAGE + 4
    for h in range(2):
        message[pl.ds(row + h, slices, stride=stride), :] = measured_ref[h]
        weight = jnp.broadcast_to(weight_ref[h : h + 1, :], (slices, TILE))
        message[pl.ds(row + 2 + h, slices, stride=stride), :] = weight
    out_ref[...] = message[...].astype(BF16)
    going.wait()


def owner_kernel(
    starts_ref, own_ref, sent_ref, out_ref, wide, filt, staged, ramp_ref, got_ref, came, sem, *sums
):
    coming = pltpu.make_async_copy(sent_ref, came, sem)
    coming.start()
    low, high = sums[:8], sums[8:]
    blocks = 16
    per = 8
    groups = staged.shape[0] // (8 * per)
    for ref in sums:
        ref[...] = jnp.zeros_like(ref)
    lane = lax.broadcasted_iota(jnp.int32, (8, TILE), 1)
    sub = lax.broadcasted_iota(jnp.int32, (8, TILE), 0)

    offset = (
        lax.broadcasted_iota(jnp.int32, (3 * TILE, TILE), 1)
        + TILE
        - lax.broadcasted_iota(jnp.int32, (3 * TILE, TILE), 0)
    )
    nonzero = jnp.where(offset == 0, 1, offset).astype(F32)
    ramp = jnp.where((offset & 1) == 1, -1.0 / (math.pi * math.pi * nonzero * nonzero), 0.0)
    ramp = jnp.where(offset == 0, 0.25, ramp)
    ramp = jnp.where(jnp.abs(offset) < TILE, ramp, 0.0)
    ramp_ref[...] = ramp
    coming.wait()
    got_ref[...] = came[...].astype(F32)

    def add(g, carry):
        turned = []
        for i in range(2 * per):
            source = g * 2 * per + i
            rows = got_ref[pl.ds(pl.multiple_of(source * MESSAGE, MESSAGE), MESSAGE), :]
            for k in range(4):
                start = starts_ref[source * 4 + k]
                turned.append((start >> 7, start & (TILE - 1), rows, i % 2 * 4 + k, k))
        turned = [
            (block, shift, pltpu.roll(rows, shift, 1), slot) for block, shift, rows, slot, k in turned
        ]
        for block, shift, value, slot in turned:
            tail = jnp.where(lane >= shift, value, 0.0)
            low[slot][block] += tail
            high[slot][block] += value - tail
        return carry

    lax.fori_loop(0, groups, add, 0)
    wide[...] = jnp.zeros_like(wide)
    for b in range(blocks):
        total = jnp.zeros((8, TILE), F32)
        for slot in range(8):
            here = low[slot][b]
            if b:
                here = here + high[slot][b - 1]
            total = total + jnp.where(sub == slot % 4, here, 0.0)
        home = pl.multiple_of((b * 8 + own_ref[0]) * MESSAGE, MESSAGE)
        given = got_ref[pl.ds(home, MESSAGE), :]
        for h in range(2):
            row = total[h : h + 1, :] + total[2 + h : 3 + h, :]
            wide[h * blocks + b : h * blocks + b + 1, TILE : 2 * TILE] = given[6 + h : 7 + h, :] * (
                given[4 + h : 5 + h, :] - row
            )
    centre = wide[:, TILE : 2 * TILE]
    at = lax.broadcasted_iota(jnp.int32, (2 * blocks, TILE), 0) % blocks
    wide[:, :TILE] = jnp.where(at == 0, 0.0, pltpu.roll(centre, 1, 0))
    wide[:, 2 * TILE :] = jnp.where(at == blocks - 1, 0.0, pltpu.roll(centre, 2 * blocks - 1, 0))
    done = jnp.dot(wide[...], ramp_ref[...], precision=lax.Precision.HIGHEST, preferred_element_type=F32)
    wide[:, :TILE] = done.astype(BF16).astype(F32)
    filt[...] = jnp.zeros_like(filt)
    for h in range(2):
        for b in range(blocks):
            row = wide[h * blocks + b : h * blocks + b + 1, :TILE]
            filt[h, b] = jnp.broadcast_to(row, (8, TILE))

    def take(g, carry):
        mixed = []
        for i in range(per):
            for k in range(8):
                start = starts_ref[(g * per + i) * 8 + k]
                block, shift = start >> 7, start & (TILE - 1)
                value = jnp.where(lane >= shift, filt[k % 2, block], filt[k % 2, block + 1])
                mixed.append((value, (TILE - shift) & (TILE - 1)))
        turned = [pltpu.roll(value, shift, 1) for value, shift in mixed]
        for i in range(per):
            rows = turned[i * 8]
            for k in range(1, 8):
                rows = jnp.where(sub == k, turned[i * 8 + k], rows)
            staged[pl.ds(pl.multiple_of((g * per + i) * 8, 8), 8), :] = rows
        return carry

    lax.fori_loop(0, groups, take, 0)
    out_ref[...] = staged[...].astype(BF16)


def backward_kernel(
    table_ref, delta_ref, lanes_ref, image_ref, sent_ref,
    final_ref, left_ref, right_ref, top_ref, bottom_ref,
    rel, bands, shadows, staged, mirror, update, image, got_ref, sems,
):
    slices = ROWS // 2
    arriving = pltpu.make_async_copy(sent_ref, got_ref, sems.at[1])
    arriving.start()
    coming = pltpu.make_async_copy(image_ref, image, sems.at[0])
    coming.start()
    pixel = lax.broadcasted_iota(jnp.int32, (PIX, BAND), 0)
    rel[...] = (
        (pixel // SIDE).astype(F32) * lanes_ref[0:1, :]
        + (pixel % SIDE).astype(F32) * lanes_ref[1:2, :]
    )
    arriving.wait()
    staged[...] = got_ref[...].astype(F32)
    mirror[...] = jnp.dot(got_ref[...], reversal(), preferred_element_type=F32)
    for a in range(ANGLES):
        parts = []
        for ref in (staged, mirror):
            for t in range(2):
                row = (a // 2) * 4 + t * 2 + a % 2
                parts.append(ref[pl.ds(row, slices, stride=ROWS), :])
        shadows[a] = jnp.concatenate(parts + parts, axis=0).T

    def build(patch, band):
        shift = delta_ref[pl.ds(patch, 1), :]
        for r in range(0, PIX, 16):
            away = jnp.abs(rel[r : r + 16, :] + shift)
            band[r : r + 16, :] = jnp.maximum(0.0, 1.0 - away).astype(BF16)

    def spread(patch, band, half, col, own):
        pieces = []
        for a in range(ANGLES):
            start = pl.multiple_of(table_ref[patch, a].astype(jnp.int32), 8)
            pieces.append(shadows[a, pl.ds(start, BINS), :])
        seen = jnp.concatenate(pieces, axis=0).astype(BF16)
        got = jnp.dot(band[...], seen, preferred_element_type=F32)
        for u in range(SIDE):
            spot = pl.ds(pl.multiple_of(col * SIDE, SIDE), SIDE)
            piece = got[u * SIDE : (u + 1) * SIDE, :]
            if own:
                update[half * SIDE + u, spot, TILE // 2 :] = piece[:, TILE // 2 :]
            else:
                update[half * SIDE + u, spot, :] = piece

    pipeline(build, spread, bands)

    coming.wait()

    def finish(i, carry):
        image[i] = image[i] + 0.25 * reflected(update, i)
        return carry

    lax.fori_loop(0, SIDE, finish, 0, unroll=2)
    going = [
        pltpu.make_async_copy(
            image.at[pl.ds(h * SIDE, SIDE)], final_ref.at[pl.ds(h * SIDE, SIDE)], sems.at[h]
        )
        for h in range(2)
    ]
    going[0].start()
    lax.fori_loop(SIDE, 2 * SIDE, finish, 0, unroll=2)
    going[1].start()
    lane = lax.broadcasted_iota(jnp.int32, (8, TILE), 1)
    sub = lax.broadcasted_iota(jnp.int32, (8, TILE), 0)
    second = lane & slices != 0

    def column(u, start, far):
        value = [image[h * SIDE + u, start : start + 8, :] for h in range(2)]
        value[far] = pltpu.roll(value[far], 4, 0)
        return jnp.where(sub < 4, value[0], value[1])

    for u in range(8):
        here, there = column(u, 0, 1), column(u + 8, 0, 1)
        left_ref[u] = jnp.where(second, pltpu.roll(there, slices, 1), here)
        here, there = column(u, TILE - 8, 0), column(u + 8, TILE - 8, 0)
        right_ref[u] = jnp.where(second, here, pltpu.roll(there, TILE - slices, 1))
    lanes = lax.broadcasted_iota(jnp.int32, (TILE, TILE), 1) // ROWS
    for ref, row, shift in ((top_ref, 0, 0), (bottom_ref, SIDE - TV_STEPS, TILE - ROWS)):
        packed = jnp.zeros((TILE, TILE), F32)
        for k in range(TV_STEPS):
            turned = pltpu.roll(image[row + k], (k * ROWS + shift) % TILE, 1)
            packed = jnp.where(lanes == k, turned, packed)
        ref[...] = packed.reshape(TILE // 8, 8, TILE)
    for copy in going:
        copy.wait()


def smooth_kernel(half, place_ref, before_ref, after_ref, *refs):
    if half == 0:
        above_ref, below_ref, x_ref, unused, out_ref = refs[:5]
    else:
        x_ref, out_ref = refs[:2]
    first, second, other, flow, out0, out1, sems = refs[-7:]
    slices = ROWS // 2
    own = pl.ds(16, TILE)
    wide = TILE + 16
    last_rows = SIDE - TV_STEPS
    coming = [
        pltpu.make_async_copy(
            x_ref.at[pl.ds(start, count)], ref.at[pl.ds(row, count), own, :], sems.at[i]
        )
        for i, (start, count, ref, row) in enumerate(
            (
                (half * SIDE, SIDE, first, TV_STEPS),
                ((1 - half) * SIDE, TV_STEPS, other, 0),
                ((1 - half) * SIDE + last_rows, TV_STEPS, other, TV_STEPS),
            )
        )
    ]
    for copy in coming:
        copy.start()
    lane = lax.broadcasted_iota(jnp.int32, (8, TILE), 1)
    later = lane & slices != 0
    has_above, has_below, has_before, has_after = (place_ref[i] for i in range(4))

    def roll(value, shift):
        return pltpu.roll(value, shift % TILE, 1)

    def sink(value):
        return pltpu.roll(value, 4, 0)

    if half == 0:
        for ref, row, shift, left, right in (
            (above_ref, 0, 0, -ROWS, -ROWS),
            (below_ref, SIDE + TV_STEPS, ROWS, slices, ROWS + slices),
        ):
            for k in range(TV_STEPS):
                back = shift - k * ROWS
                lead = jnp.where(
                    later,
                    roll(ref[TILE // 8 - 1], back + slices),
                    sink(roll(ref[TILE // 8 + k], left)),
                )
                trail = jnp.where(
                    later,
                    roll(ref[TILE // 8 + TV_STEPS + k], right),
                    roll(ref[0], back - slices),
                )
                first[row + k, 8:16, :] = lead
                for g in range(TILE // 8):
                    first[row + k, 16 + 8 * g : 24 + 8 * g, :] = roll(ref[g], back)
                first[row + k, 16 + TILE : 24 + TILE, :] = trail
    for copy in coming:
        copy.wait()
    sides = [(first, u + TV_STEPS, u, half) for u in range(SIDE)]
    sides += [(other, k, k, 1 - half) for k in range(TV_STEPS)]
    sides += [(other, TV_STEPS + k, last_rows + k, 1 - half) for k in range(TV_STEPS)]
    for ref, row, u, h in sides:
        before = before_ref[u % 8]
        after = after_ref[u % 8]
        if u < 8:
            before, after = roll(before, -slices), roll(after, slices)
        if h:
            after = sink(after)
        else:
            before = sink(before)
        lead = jnp.where(later, roll(ref[row, 8 + TILE : 16 + TILE, :], slices), before)
        trail = jnp.where(later, after, roll(ref[row, 16:24, :], -slices))
        ref[row, 8:16, :] = lead
        ref[row, 16 + TILE : 24 + TILE, :] = trail

    group = lax.broadcasted_iota(jnp.int32, (wide, TILE), 1) // ROWS
    span = pl.ds(8, wide)
    for k in range(TV_STEPS):
        for mine, others, target, low in (
            (SIDE + k, TV_STEPS + k, k, True),
            (TV_STEPS + k, k, SIDE + TV_STEPS + k, False),
        ):
            mine = first[mine, span, :]
            others = roll(other[others, span, :], 2 * ROWS)
            swapped = roll(mine, 2 * ROWS)
            if half == 0:
                value = jnp.where(group == (3 if low else 2), others, swapped)
                outer = group == (0 if low else 1)
                value = jnp.where(outer, first[target, span, :], value)
            else:
                step = roll(mine, ROWS if low else -ROWS)
                value = jnp.where(group == (3 if low else 2), step, swapped)
                value = jnp.where(group == (0 if low else 1), others, value)
            first[target, span, :] = value

    keep_lead = later | (has_before == 1)
    keep_trail = jnp.logical_not(later) | (has_after == 1)

    def flows(source, r):
        here = source[r, span, :]
        down = source[r + 1, span, :] - here
        right = source[r, pl.ds(9, wide), :] - here
        inverse = lax.rsqrt(smoothing * smoothing + down * down + right * right)
        return here, down * inverse, right * inverse

    for k in range(TV_STEPS):
        source, target = (first, second) if k % 2 == 0 else (second, first)
        last = k == TV_STEPS - 1

        def row(r, came, slot, inside=None, source=source, target=target, last=last):
            here, down, right = flows(source, r)
            flow[slot, span, :] = right
            left = flow[slot, pl.ds(7, wide), :]
            fresh = here - descent_step * (came - down + left - right)
            if last:
                turned = fresh[8 : 8 + TILE, :].T
                for g, block in enumerate(blocks_at(half)):
                    spot = pl.ds(block * SIDE + r - TV_STEPS, slices, stride=TILE)
                    for t, ref in enumerate((out0, out1)):
                        start = g * ROWS + t * slices
                        ref[spot, :] = turned[start : start + slices, :]
                return down
            if inside is not None:
                fresh = jnp.where(inside, fresh, 0.0)
            target[r, 8:16, :] = jnp.where(keep_lead, fresh[:8, :], 0.0)
            target[r, own, :] = fresh[8 : 8 + TILE, :]
            target[r, 16 + TILE : 24 + TILE, :] = jnp.where(keep_trail, fresh[wide - 8 :, :], 0.0)
            return down

        unused, came, unused = flows(source, k)
        for r in range(k + 1, TV_STEPS):
            came = row(r, came, r % 2, None if half else (group != 0) | (has_above == 1))

        def pair(i, came, row=row):
            came = row(TV_STEPS + 2 * i, came, 0)
            return row(TV_STEPS + 2 * i + 1, came, 1)

        came = lax.fori_loop(0, SIDE // 2, pair, came)
        for r in range(SIDE + TV_STEPS, SIDE + 2 * TV_STEPS - 1 - k):
            came = row(r, came, r % 2, None if half else (group != 1) | (has_below == 1))
    spans = ((2 * SIDE, 4 * SIDE),) if half else ((0, 2 * SIDE), (TILE - 2 * SIDE, 2 * SIDE))
    going = [
        pltpu.make_async_copy(
            ref.reshape(slices, TILE, TILE).at[:, pl.ds(start, count), :],
            out_ref.at[:, pl.ds(start, count), pl.ds(t * TILE, TILE)],
            sems.at[2 * i + t],
        )
        for i, (start, count) in enumerate(spans)
        for t, ref in enumerate((out0, out1))
    ]
    for copy in going:
        copy.start()
    for copy in going:
        copy.wait()


def call(kernel, scalars, arrays, left, outs, scratch, flops, aliases=None):
    vmem = pl.BlockSpec(memory_space=VMEM)
    stays = pl.BlockSpec(memory_space=pl.ANY)
    smem = pl.BlockSpec(memory_space=pltpu.SMEM)
    operands = (*scalars, *arrays, *left)
    moved = sum(x.size * x.dtype.itemsize for x in operands)
    big = 1 << 20
    inside = [x for x in (*arrays, *jax.tree.leaves(outs)) if x.size * 4 <= big]
    held = sum(x.size * 4 for x in inside)
    held += sum(math.prod(x.shape) * 4 for x in scratch if hasattr(x, "shape"))
    return pl.pallas_call(
        kernel,
        out_shape=outs,
        in_specs=[smem] * len(scalars) + [vmem] * len(arrays) + [stays] * len(left),
        out_specs=jax.tree.map(lambda x: stays if x.size * 4 > big else vmem, outs),
        scratch_shapes=scratch,
        input_output_aliases=aliases or {},
        compiler_params=pltpu.CompilerParams(vmem_limit_bytes=held + (6 << 20)),
        cost_estimate=pl.CostEstimate(flops=flops, bytes_accessed=moved, transcendentals=0),
    )(*operands)


def local(current_image, measured, ray_weight, angle_ids, shadow_start):
    row_index = lax.axis_index("row")
    col_index = lax.axis_index("col")
    rows = lax.axis_size("row")
    cols = lax.axis_size("col")
    slices = current_image.shape[0]
    both = ("row", "col")
    image = current_image.reshape(slices * TILE, 2 * TILE)
    table = geometry(angle_ids)
    half = VMEM((slices * TILE, TILE), F32)

    turned = jax.ShapeDtypeStruct((2 * SIDE, TILE, TILE), F32)
    sent, image = call(
        forward_kernel,
        (table, col_index.reshape(1)),
        (measured[:, 0], ray_weight[:, 0]),
        (image,),
        (jax.ShapeDtypeStruct((rows * cols * MESSAGE, TILE), BF16), turned),
        [
            VMEM((2 * SIDE * TILE, TILE), BF16),
            VMEM((BAND, PIX), F32),
            VMEM((4, BAND, PIX), BF16),
            VMEM((ANGLES * TILE, TILE), F32),
            VMEM((rows * cols * MESSAGE, TILE), F32),
            half,
            half,
            VMEM(turned.shape, F32),
            pltpu.SemaphoreType.DMA((3,)),
        ]
        + [VMEM((TILE, TILE), F32)] * ANGLES,
        30_000_000_000,
    )
    got = lax.all_to_all(
        sent.reshape(rows * cols, MESSAGE, TILE), both, split_axis=0, concat_axis=0, tiled=True
    )
    blocks = rows
    starts = shadow_start.reshape(-1, ANGLES)
    starts = lax.dynamic_slice_in_dim(starts, col_index * 2, 2, 1).reshape(-1)
    out = call(
        owner_kernel,
        (starts, col_index.reshape(1)),
        (),
        (got.reshape(-1, TILE),),
        jax.ShapeDtypeStruct((rows * cols * 4, TILE), BF16),
        [
            VMEM((2 * blocks, 3 * TILE), F32),
            VMEM((2, blocks + 1, 8, TILE), F32),
            VMEM((rows * cols * 4, TILE), F32),
            VMEM((3 * TILE, TILE), F32),
            VMEM((rows * cols * MESSAGE, TILE), F32),
            VMEM((rows * cols * MESSAGE, TILE), BF16),
            pltpu.SemaphoreType.DMA,
        ]
        + [VMEM((blocks, 8, TILE), F32)] * 16,
        10_000_000_000,
    )
    shadows = lax.all_to_all(
        out.reshape(rows * cols, 4, TILE), both, split_axis=0, concat_axis=0, tiled=True
    )
    bins = jnp.arange(BINS, dtype=F32)
    delta_lanes = (table[PAIRS : 2 * PAIRS, :, None] - bins).reshape(-1, BAND)
    angle_lanes = jnp.repeat(table[2 * PAIRS :], BINS, axis=1)
    side = jax.ShapeDtypeStruct((8, 8, TILE), F32)
    edge = jax.ShapeDtypeStruct((TILE // 8, 8, TILE), F32)
    x, left, right, top, bottom = call(
        backward_kernel,
        (table,),
        (delta_lanes, angle_lanes),
        (image, shadows.reshape(-1, TILE)),
        (turned, side, side, edge, edge),
        [
            VMEM((PIX, BAND), F32),
            VMEM((4, PIX, BAND), BF16),
            VMEM((ANGLES, TILE, TILE), F32),
            VMEM((rows * cols * 4, TILE), F32),
            VMEM((rows * cols * 4, TILE), F32),
            VMEM(turned.shape, F32),
            VMEM(turned.shape, F32),
            VMEM((rows * cols * 4, TILE), BF16),
            pltpu.SemaphoreType.DMA((2,)),
        ],
        30_000_000_000,
    )
    before = lax.ppermute(right, "col", [(i, i + 1) for i in range(cols - 1)])
    after = lax.ppermute(left, "col", [(i + 1, i) for i in range(cols - 1)])
    upward = jnp.concatenate([top, before[:TV_STEPS], after[:TV_STEPS]], axis=0)
    downward = jnp.concatenate([bottom, before[TV_STEPS:], after[TV_STEPS:]], axis=0)
    above = lax.ppermute(downward, "row", [(i, i + 1) for i in range(rows - 1)])
    below = lax.ppermute(upward, "row", [(i + 1, i) for i in range(rows - 1)])
    place = jnp.stack(
        [row_index > 0, row_index < rows - 1, col_index > 0, col_index < cols - 1]
    ).astype(jnp.int32)
    wide = VMEM((SIDE + 2 * TV_STEPS, TILE + 32, TILE), F32)
    few = VMEM((2 * TV_STEPS, TILE + 32, TILE), F32)
    scratch = [wide, wide, few, VMEM((2, TILE + 32, TILE), F32), half, half]
    scratch.append(pltpu.SemaphoreType.DMA((4,)))
    final = jax.ShapeDtypeStruct(current_image.shape, F32)
    smooth = call(
        functools.partial(smooth_kernel, 1),
        (place,),
        (before, after),
        (x,),
        final,
        scratch,
        10_000_000_000,
    )
    return call(
        functools.partial(smooth_kernel, 0),
        (place,),
        (before, after, above, below),
        (x, smooth),
        final,
        scratch,
        10_000_000_000,
        {6: 0},
    )


def solution(mesh):
    return jax.shard_map(
        local,
        mesh=mesh,
        in_specs=(
            P(None, "row", "col"),
            P("col", "row", None, None),
            P("col", "row", None),
            P(),
            P(),
        ),
        out_specs=P(None, "row", "col"),
        check_vma=False,
    )
```

```python
import functools
import math

import jax
import jax.numpy as jnp
from jax import lax
from jax.experimental import pallas as pl
from jax.experimental.pallas import tpu as pltpu
from jax.sharding import PartitionSpec as P

TILE = 128
ANGLES = 16
ALL_ANGLES = 256
TV_STEPS = 4
SIDE = 16
PATCHES = TILE // SIDE
PIX = SIDE * SIDE
BINS = 24
ROWS = 32
BAND = ANGLES * BINS
PAIRS = PATCHES * PATCHES // 2
PHASE = 4
STRIDE = 4
MESSAGE = 8

inverse_root = 0.7071067811865476
smoothing = 0.25
descent_step = 0.05

VMEM = pltpu.VMEM
F32 = jnp.float32
BF16 = jnp.bfloat16


def geometry(angle_ids):
    radians = angle_ids.astype(F32) * (math.pi / ALL_ANGLES)
    cosine = jnp.cos(radians)[None] * inverse_root
    sine = jnp.sin(radians)[None] * inverse_root
    row = lax.broadcasted_iota(jnp.int32, (2 * PAIRS + 2, ANGLES), 0)
    patch = row & (PAIRS - 1)
    down = (patch >> 3).astype(F32) * SIDE - (TILE - 1) / 2.0
    across = (patch & (PATCHES - 1)).astype(F32) * SIDE - (TILE - 1) / 2.0
    corner = TILE / 2.0 + down * cosine + across * sine
    low = corner + (SIDE - 1) * (jnp.minimum(cosine, 0.0) + jnp.minimum(sine, 0.0))
    base = jnp.clip(jnp.floor((jnp.floor(low - 1.5) + 1.0) / 8.0) * 8.0, 0.0, TILE - BINS)
    delta = corner - base - 0.5
    ends = jnp.where(row == 2 * PAIRS, cosine, sine)
    return jnp.where(row < PAIRS, base, jnp.where(row < 2 * PAIRS, delta, ends))


def reversal():
    there = lax.broadcasted_iota(jnp.int32, (TILE, TILE), 0)
    here = lax.broadcasted_iota(jnp.int32, (TILE, TILE), 1)
    return jnp.where(there + here == TILE - 1, 1.0, 0.0).astype(BF16)


def reverse_lanes(value):
    high = value.astype(BF16)
    low = (value - high.astype(F32)).astype(BF16)
    both = jnp.concatenate([high, low], axis=1)
    turn = reversal()
    return jnp.dot(both, jnp.concatenate([turn, turn], axis=0), preferred_element_type=F32)


def pipeline(build, use, bands):
    def phase(i, action, slot):
        for j in range(PHASE):
            at = i * PHASE + j
            half = at // PATCHES
            col = at % PATCHES
            for own in range(2):
                patch = (2 * half + own) * PATCHES + col
                band = bands.at[(slot * PHASE + j) * 2 + own]
                if action is build:
                    build(patch, band)
                else:
                    use(patch, band, half, col, own)

    phase(0, build, 0)
    phases = 2 * PATCHES // PHASE

    def step(i, carry):
        phase(2 * i + 1, build, 1)
        phase(2 * i, use, 0)
        phase(jnp.minimum(2 * i + 2, phases - 1), build, 0)
        phase(2 * i + 1, use, 1)
        return carry

    lax.fori_loop(0, phases // 2, step, 0)


def blocks_at(half):
    return 2 * half, PATCHES - 1 - 2 * half, 2 * half + 1, PATCHES - 2 - 2 * half


def reflected(ref, i):
    other = (i // SIDE) * SIDE + SIDE - 1 - i % SIDE
    back = 7 - lax.broadcasted_iota(jnp.int32, (8, TILE), 0)
    mirrored = lax.broadcasted_iota(jnp.int32, (8, TILE), 1) & ROWS != 0
    parts = []
    for g in range(TILE // 8):
        far = ref[other, TILE - 8 * (g + 1) : TILE - 8 * g, :]
        far = jnp.take_along_axis(far, back, axis=0)
        parts.append(jnp.where(mirrored, far, ref[i, 8 * g : 8 * (g + 1), :]))
    return jnp.concatenate(parts, axis=0)


def forward_kernel(
    table_ref, own_ref, image_ref, given_ref, given_weight_ref,
    out_ref, turned_ref, xt, rel, bands, tails, message, image0_ref, image1_ref, flat,
    measured_ref, weight_ref, sems, *sums,
):
    slices = ROWS // 2
    coming = [[], []]
    for part, start in ((0, 0), (0, 6), (1, 2), (1, 4)):
        spot = pl.ds(start * SIDE, 2 * SIDE)
        for t, ref in enumerate((image0_ref, image1_ref)):
            coming[part].append(
                pltpu.make_async_copy(
                    image_ref.at[:, spot, pl.ds(t * TILE, TILE)],
                    ref.reshape(slices, TILE, TILE).at[:, spot, :],
                    sems.at[2 + start + t],
                )
            )
    small = [
        pltpu.make_async_copy(given_ref, measured_ref, sems.at[0]),
        pltpu.make_async_copy(given_weight_ref, weight_ref, sems.at[1]),
    ]
    for copy in (*coming[0], *coming[1], *small):
        copy.start()
    lane = lax.broadcasted_iota(jnp.int32, (BINS, PIX), 1)
    bin_at = lax.broadcasted_iota(jnp.int32, (BINS, PIX), 0).astype(F32)
    down = (lane // SIDE).astype(F32)
    across = (lane % SIDE).astype(F32)
    for a in range(ANGLES):
        rel[a * BINS : (a + 1) * BINS, :] = (
            down * table_ref[2 * PAIRS, a] + across * table_ref[2 * PAIRS + 1, a] - bin_at
        )
    for ref in sums:
        ref[...] = jnp.zeros_like(ref)
    def rows_of(u):
        return [ref[pl.ds(u, slices, stride=TILE), :] for ref in (image0_ref, image1_ref)]

    def flip(i, carry):
        rows = []
        for block in blocks_at(i // SIDE):
            rows += rows_of(block * SIDE + i % SIDE)
        flat[i] = jnp.concatenate(rows, axis=0).T
        return carry

    for part in range(2):
        for copy in coming[part]:
            copy.wait()
        lax.fori_loop(part * SIDE, (part + 1) * SIDE, flip, 0, unroll=4)
    for copy in small:
        copy.wait()
    going = pltpu.make_async_copy(flat, turned_ref, sems.at[0])
    going.start()

    def reflect(i, carry):
        value = reflected(flat, i)
        xt[pl.ds(pl.multiple_of(i * TILE, TILE), TILE), :] = value.astype(BF16)
        return carry

    lax.fori_loop(0, 2 * SIDE, reflect, 0, unroll=2)

    def build(patch, band):
        for a in range(0, ANGLES, 2):
            pair = []
            for b in (a, a + 1):
                away = jnp.abs(rel[b * BINS : (b + 1) * BINS, :] + table_ref[PAIRS + patch, b])
                pair.append(1.0 - away)
            rounded = jnp.concatenate(pair, axis=0).astype(BF16)
            band[a * BINS : (a + 2) * BINS, :] = jnp.maximum(rounded, jnp.zeros_like(rounded))

    first_half = lax.broadcasted_iota(jnp.int32, (PIX, TILE), 1) < TILE // 2

    def project(patch, band, half, col, own):
        pieces = []
        for u in range(SIDE):
            start = pl.multiple_of((half * SIDE + u) * TILE + col * SIDE, SIDE)
            pieces.append(xt[pl.ds(start, SIDE), :])
        pixels = jnp.concatenate(pieces, axis=0)
        nothing = jnp.zeros_like(pixels)
        pixels = jnp.where(first_half, *((nothing, pixels) if own else (pixels, nothing)))
        got = jnp.dot(band[...], pixels, preferred_element_type=F32)
        for a in range(ANGLES):
            start = pl.multiple_of(table_ref[patch, a].astype(jnp.int32), 8)
            sums[a][pl.ds(start, BINS), :] += got[a * BINS : (a + 1) * BINS, :]

    pipeline(build, project, bands)
    stride = MESSAGE * ANGLES // 2
    for a in range(ANGLES):
        tails[a * TILE : (a + 1) * TILE, :] = sums[a][...].T * 0.03125
    mirrored = [
        tails[a * TILE + ROWS : a * TILE + 2 * ROWS, :]
        + tails[a * TILE + 3 * ROWS : (a + 1) * TILE, :]
        for a in range(ANGLES)
    ]
    mirrored = reverse_lanes(jnp.concatenate(mirrored, axis=0))
    for a in range(ANGLES):
        total = tails[a * TILE : a * TILE + ROWS, :] + tails[a * TILE + 2 * ROWS : a * TILE + 3 * ROWS, :]
        total = total + mirrored[a * ROWS : (a + 1) * ROWS, :]
        for t in range(2):
            row = (a // 2) * MESSAGE + t * 2 + a % 2
            message[pl.ds(row, slices, stride=stride), :] = total[t * slices : (t + 1) * slices, :]
    row = own_ref[0] * MESSAGE + 4
    for h in range(2):
        message[pl.ds(row + h, slices, stride=stride), :] = measured_ref[h]
        weight = jnp.broadcast_to(weight_ref[h : h + 1, :], (slices, TILE))
        message[pl.ds(row + 2 + h, slices, stride=stride), :] = weight
    out_ref[...] = message[...].astype(BF16)
    going.wait()


def owner_kernel(
    starts_ref, own_ref, sent_ref, out_ref, wide, filt, staged, ramp_ref, got_ref, came, sem, *sums
):
    coming = pltpu.make_async_copy(sent_ref, came, sem)
    coming.start()
    low, high = sums[:8], sums[8:]
    blocks = 16
    per = 8
    groups = staged.shape[0] // (8 * per)
    for ref in sums:
        ref[...] = jnp.zeros_like(ref)
    lane = lax.broadcasted_iota(jnp.int32, (8, TILE), 1)
    sub = lax.broadcasted_iota(jnp.int32, (8, TILE), 0)

    offset = (
        lax.broadcasted_iota(jnp.int32, (3 * TILE, TILE), 1)
        + TILE
        - lax.broadcasted_iota(jnp.int32, (3 * TILE, TILE), 0)
    )
    nonzero = jnp.where(offset == 0, 1, offset).astype(F32)
    ramp = jnp.where((offset & 1) == 1, -1.0 / (math.pi * math.pi * nonzero * nonzero), 0.0)
    ramp = jnp.where(offset == 0, 0.25, ramp)
    ramp = jnp.where(jnp.abs(offset) < TILE, ramp, 0.0)
    ramp_ref[...] = ramp
    coming.wait()
    got_ref[...] = came[...].astype(F32)

    def add(g, carry):
        turned = []
        for i in range(2 * per):
            source = g * 2 * per + i
            rows = got_ref[pl.ds(pl.multiple_of(source * MESSAGE, MESSAGE), MESSAGE), :]
            for k in range(4):
                start = starts_ref[source * 4 + k]
                turned.append((start >> 7, start & (TILE - 1), rows, i % 2 * 4 + k, k))
        turned = [
            (block, shift, pltpu.roll(rows, shift, 1), slot) for block, shift, rows, slot, k in turned
        ]
        for block, shift, value, slot in turned:
            tail = jnp.where(lane >= shift, value, 0.0)
            low[slot][block] += tail
            high[slot][block] += value - tail
        return carry

    lax.fori_loop(0, groups, add, 0)
    wide[...] = jnp.zeros_like(wide)
    for b in range(blocks):
        total = jnp.zeros((8, TILE), F32)
        for slot in range(8):
            here = low[slot][b]
            if b:
                here = here + high[slot][b - 1]
            total = total + jnp.where(sub == slot % 4, here, 0.0)
        home = pl.multiple_of((b * 8 + own_ref[0]) * MESSAGE, MESSAGE)
        given = got_ref[pl.ds(home, MESSAGE), :]
        for h in range(2):
            row = total[h : h + 1, :] + total[2 + h : 3 + h, :]
            wide[h * blocks + b : h * blocks + b + 1, TILE : 2 * TILE] = given[6 + h : 7 + h, :] * (
                given[4 + h : 5 + h, :] - row
            )
    centre = wide[:, TILE : 2 * TILE]
    at = lax.broadcasted_iota(jnp.int32, (2 * blocks, TILE), 0) % blocks
    wide[:, :TILE] = jnp.where(at == 0, 0.0, pltpu.roll(centre, 1, 0))
    wide[:, 2 * TILE :] = jnp.where(at == blocks - 1, 0.0, pltpu.roll(centre, 2 * blocks - 1, 0))
    done = jnp.dot(wide[...], ramp_ref[...], precision=lax.Precision.HIGHEST, preferred_element_type=F32)
    wide[:, :TILE] = done.astype(BF16).astype(F32)
    filt[...] = jnp.zeros_like(filt)
    for h in range(2):
        for b in range(blocks):
            row = wide[h * blocks + b : h * blocks + b + 1, :TILE]
            filt[h, b] = jnp.broadcast_to(row, (8, TILE))

    def take(g, carry):
        mixed = []
        for i in range(per):
            for k in range(8):
                start = starts_ref[(g * per + i) * 8 + k]
                block, shift = start >> 7, start & (TILE - 1)
                value = jnp.where(lane >= shift, filt[k % 2, block], filt[k % 2, block + 1])
                mixed.append((value, (TILE - shift) & (TILE - 1)))
        turned = [pltpu.roll(value, shift, 1) for value, shift in mixed]
        for i in range(per):
            rows = turned[i * 8]
            for k in range(1, 8):
                rows = jnp.where(sub == k, turned[i * 8 + k], rows)
            staged[pl.ds(pl.multiple_of((g * per + i) * 8, 8), 8), :] = rows
        return carry

    lax.fori_loop(0, groups, take, 0)
    out_ref[...] = staged[...].astype(BF16)


def backward_kernel(
    table_ref, delta_ref, lanes_ref, image_ref, sent_ref,
    final_ref, left_ref, right_ref, top_ref, bottom_ref,
    rel, bands, shadows, staged, mirror, update, image, got_ref, sems,
):
    slices = ROWS // 2
    arriving = pltpu.make_async_copy(sent_ref, got_ref, sems.at[1])
    arriving.start()
    coming = pltpu.make_async_copy(image_ref, image, sems.at[0])
    coming.start()
    pixel = lax.broadcasted_iota(jnp.int32, (PIX, BAND), 0)
    rel[...] = (
        (pixel // SIDE).astype(F32) * lanes_ref[0:1, :]
        + (pixel % SIDE).astype(F32) * lanes_ref[1:2, :]
    )
    arriving.wait()
    staged[...] = got_ref[...].astype(F32)
    mirror[...] = jnp.dot(got_ref[...], reversal(), preferred_element_type=F32)
    for a in range(ANGLES):
        parts = []
        for ref in (staged, mirror):
            for t in range(2):
                row = (a // 2) * 4 + t * 2 + a % 2
                parts.append(ref[pl.ds(row, slices, stride=ROWS), :])
        shadows[a] = jnp.concatenate(parts + parts, axis=0).T

    def build(patch, band):
        shift = delta_ref[pl.ds(patch, 1), :]
        for r in range(0, PIX, 16):
            away = jnp.abs(rel[r : r + 16, :] + shift)
            rounded = (1.0 - away).astype(BF16)
            band[r : r + 16, :] = jnp.maximum(rounded, jnp.zeros_like(rounded))

    def spread(patch, band, half, col, own):
        pieces = []
        for a in range(ANGLES):
            start = pl.multiple_of(table_ref[patch, a].astype(jnp.int32), 8)
            pieces.append(shadows[a, pl.ds(start, BINS), :])
        seen = jnp.concatenate(pieces, axis=0).astype(BF16)
        got = jnp.dot(band[...], seen, preferred_element_type=F32)
        for u in range(SIDE):
            spot = pl.ds(pl.multiple_of(col * SIDE, SIDE), SIDE)
            piece = got[u * SIDE : (u + 1) * SIDE, :]
            if own:
                update[half * SIDE + u, spot, TILE // 2 :] = piece[:, TILE // 2 :]
            else:
                update[half * SIDE + u, spot, :] = piece

    pipeline(build, spread, bands)

    coming.wait()

    def finish(i, carry):
        image[i] = image[i] + 0.25 * reflected(update, i)
        return carry

    lax.fori_loop(0, SIDE, finish, 0, unroll=2)
    going = [
        pltpu.make_async_copy(
            image.at[pl.ds(h * SIDE, SIDE)], final_ref.at[pl.ds(h * SIDE, SIDE)], sems.at[h]
        )
        for h in range(2)
    ]
    going[0].start()
    lax.fori_loop(SIDE, 2 * SIDE, finish, 0, unroll=2)
    going[1].start()
    lane = lax.broadcasted_iota(jnp.int32, (8, TILE), 1)
    sub = lax.broadcasted_iota(jnp.int32, (8, TILE), 0)
    second = lane & slices != 0

    def column(u, start, far):
        value = [image[h * SIDE + u, start : start + 8, :] for h in range(2)]
        value[far] = pltpu.roll(value[far], 4, 0)
        return jnp.where(sub < 4, value[0], value[1])

    for u in range(8):
        here, there = column(u, 0, 1), column(u + 8, 0, 1)
        left_ref[u] = jnp.where(second, pltpu.roll(there, slices, 1), here)
        here, there = column(u, TILE - 8, 0), column(u + 8, TILE - 8, 0)
        right_ref[u] = jnp.where(second, here, pltpu.roll(there, TILE - slices, 1))
    lanes = lax.broadcasted_iota(jnp.int32, (TILE, TILE), 1) // ROWS
    for ref, row, shift in ((top_ref, 0, 0), (bottom_ref, SIDE - TV_STEPS, TILE - ROWS)):
        packed = jnp.zeros((TILE, TILE), F32)
        for k in range(TV_STEPS):
            turned = pltpu.roll(image[row + k], (k * ROWS + shift) % TILE, 1)
            packed = jnp.where(lanes == k, turned, packed)
        ref[...] = packed.reshape(TILE // 8, 8, TILE)
    for copy in going:
        copy.wait()


def smooth_kernel(half, place_ref, before_ref, after_ref, *refs):
    if half == 0:
        above_ref, below_ref, x_ref, unused, out_ref = refs[:5]
    else:
        x_ref, out_ref = refs[:2]
    first, second, other, flow, out0, out1, sems = refs[-7:]
    slices = ROWS // 2
    own = pl.ds(16, TILE)
    wide = TILE + 16
    last_rows = SIDE - TV_STEPS
    coming = [
        pltpu.make_async_copy(
            x_ref.at[pl.ds(start, count)], ref.at[pl.ds(row, count), own, :], sems.at[i]
        )
        for i, (start, count, ref, row) in enumerate(
            (
                (half * SIDE, SIDE, first, TV_STEPS),
                ((1 - half) * SIDE, TV_STEPS, other, 0),
                ((1 - half) * SIDE + last_rows, TV_STEPS, other, TV_STEPS),
            )
        )
    ]
    for copy in coming:
        copy.start()
    lane = lax.broadcasted_iota(jnp.int32, (8, TILE), 1)
    later = lane & slices != 0
    has_above, has_below, has_before, has_after = (place_ref[i] for i in range(4))

    def roll(value, shift):
        return pltpu.roll(value, shift % TILE, 1)

    def sink(value):
        return pltpu.roll(value, 4, 0)

    if half == 0:
        for ref, row, shift, left, right in (
            (above_ref, 0, 0, -ROWS, -ROWS),
            (below_ref, SIDE + TV_STEPS, ROWS, slices, ROWS + slices),
        ):
            for k in range(TV_STEPS):
                back = shift - k * ROWS
                lead = jnp.where(
                    later,
                    roll(ref[TILE // 8 - 1], back + slices),
                    sink(roll(ref[TILE // 8 + k], left)),
                )
                trail = jnp.where(
                    later,
                    roll(ref[TILE // 8 + TV_STEPS + k], right),
                    roll(ref[0], back - slices),
                )
                first[row + k, 8:16, :] = lead
                for g in range(TILE // 8):
                    first[row + k, 16 + 8 * g : 24 + 8 * g, :] = roll(ref[g], back)
                first[row + k, 16 + TILE : 24 + TILE, :] = trail
    for copy in coming:
        copy.wait()
    sides = [(first, u + TV_STEPS, u, half) for u in range(SIDE)]
    sides += [(other, k, k, 1 - half) for k in range(TV_STEPS)]
    sides += [(other, TV_STEPS + k, last_rows + k, 1 - half) for k in range(TV_STEPS)]
    for ref, row, u, h in sides:
        before = before_ref[u % 8]
        after = after_ref[u % 8]
        if u < 8:
            before, after = roll(before, -slices), roll(after, slices)
        if h:
            after = sink(after)
        else:
            before = sink(before)
        lead = jnp.where(later, roll(ref[row, 8 + TILE : 16 + TILE, :], slices), before)
        trail = jnp.where(later, after, roll(ref[row, 16:24, :], -slices))
        ref[row, 8:16, :] = lead
        ref[row, 16 + TILE : 24 + TILE, :] = trail

    group = lax.broadcasted_iota(jnp.int32, (wide, TILE), 1) // ROWS
    span = pl.ds(8, wide)
    for k in range(TV_STEPS):
        for mine, others, target, low in (
            (SIDE + k, TV_STEPS + k, k, True),
            (TV_STEPS + k, k, SIDE + TV_STEPS + k, False),
        ):
            mine = first[mine, span, :]
            others = roll(other[others, span, :], 2 * ROWS)
            swapped = roll(mine, 2 * ROWS)
            if half == 0:
                value = jnp.where(group == (3 if low else 2), others, swapped)
                outer = group == (0 if low else 1)
                value = jnp.where(outer, first[target, span, :], value)
            else:
                step = roll(mine, ROWS if low else -ROWS)
                value = jnp.where(group == (3 if low else 2), step, swapped)
                value = jnp.where(group == (0 if low else 1), others, value)
            first[target, span, :] = value

    keep_lead = later | (has_before == 1)
    keep_trail = jnp.logical_not(later) | (has_after == 1)

    def flows(source, r):
        here = source[r, span, :]
        down = source[r + 1, span, :] - here
        right = source[r, pl.ds(9, wide), :] - here
        inverse = lax.rsqrt(smoothing * smoothing + down * down + right * right)
        return here, down * inverse, right * inverse

    for k in range(TV_STEPS):
        source, target = (first, second) if k % 2 == 0 else (second, first)
        last = k == TV_STEPS - 1

        def row(r, came, slot, inside=None, source=source, target=target, last=last):
            here, down, right = flows(source, r)
            flow[slot, span, :] = right
            left = flow[slot, pl.ds(7, wide), :]
            fresh = here - descent_step * (came - down + left - right)
            if last:
                turned = fresh[8 : 8 + TILE, :].T
                for g, block in enumerate(blocks_at(half)):
                    spot = pl.ds(block * SIDE + r - TV_STEPS, slices, stride=TILE)
                    for t, ref in enumerate((out0, out1)):
                        start = g * ROWS + t * slices
                        ref[spot, :] = turned[start : start + slices, :]
                return down
            if inside is not None:
                fresh = jnp.where(inside, fresh, 0.0)
            target[r, 8:16, :] = jnp.where(keep_lead, fresh[:8, :], 0.0)
            target[r, own, :] = fresh[8 : 8 + TILE, :]
            target[r, 16 + TILE : 24 + TILE, :] = jnp.where(keep_trail, fresh[wide - 8 :, :], 0.0)
            return down

        unused, came, unused = flows(source, k)
        for r in range(k + 1, TV_STEPS):
            came = row(r, came, r % 2, None if half else (group != 0) | (has_above == 1))

        def some(i, came, row=row):
            for j in range(STRIDE):
                came = row(TV_STEPS + STRIDE * i + j, came, j % 2)
            return came

        if not last:
            came = lax.fori_loop(0, SIDE // STRIDE, some, came)
        for r in range(SIDE + TV_STEPS, SIDE + 2 * TV_STEPS - 1 - k):
            came = row(r, came, r % 2, None if half else (group != 1) | (has_below == 1))
    going = []
    for part in range(2):
        came = lax.fori_loop(
            part * SIDE // 2 // STRIDE, (part + 1) * SIDE // 2 // STRIDE, some, came
        )
        for block in blocks_at(half):
            spot = pl.ds(block * SIDE + part * 8, 8)
            for t, ref in enumerate((out0, out1)):
                going.append(
                    pltpu.make_async_copy(
                        ref.reshape(slices, TILE, TILE).at[:, spot, :],
                        out_ref.at[:, spot, pl.ds(t * TILE, TILE)],
                        sems.at[len(going)],
                    )
                )
                going[-1].start()
    for copy in going:
        copy.wait()


def call(
    kernel, scalars, arrays, left, outs, scratch, flops, aliases=None, tight=True
):
    vmem = pl.BlockSpec(memory_space=VMEM)
    smem = pl.BlockSpec(memory_space=pltpu.SMEM)
    operands = (*scalars, *arrays, *left)
    bytes_of = lambda x: math.prod(x.shape) * x.dtype.itemsize
    stays = lambda x: bytes_of(x) > 1 << 20
    held = sum(bytes_of(x) for x in arrays)
    held += sum(bytes_of(x) for x in jax.tree.leaves(outs) if not stays(x))
    held += sum(bytes_of(x) for x in scratch if getattr(x, "memory_space", None) == VMEM)
    return pl.pallas_call(
        kernel,
        out_shape=outs,
        in_specs=[smem] * len(scalars)
        + [vmem] * len(arrays)
        + [pl.BlockSpec(memory_space=pl.ANY)] * len(left),
        out_specs=jax.tree.map(
            lambda x: pl.BlockSpec(memory_space=pl.ANY) if stays(x) else vmem, outs
        ),
        scratch_shapes=scratch,
        input_output_aliases=aliases or {},
        compiler_params=pltpu.CompilerParams(vmem_limit_bytes=held + (6 << 20) if tight else None),
        cost_estimate=pl.CostEstimate(
            flops=flops, bytes_accessed=sum(map(bytes_of, operands)), transcendentals=0
        ),
    )(*operands)


def local(current_image, measured, ray_weight, angle_ids, shadow_start):
    row_index = lax.axis_index("row")
    col_index = lax.axis_index("col")
    rows = lax.axis_size("row")
    cols = lax.axis_size("col")
    slices = current_image.shape[0]
    both = ("row", "col")
    table = geometry(angle_ids)
    half = VMEM((slices * TILE, TILE), F32)

    turned = jax.ShapeDtypeStruct((2 * SIDE, TILE, TILE), F32)
    sent, image = call(
        forward_kernel,
        (table, col_index.reshape(1)),
        (),
        (current_image, measured[:, 0], ray_weight[:, 0]),
        (jax.ShapeDtypeStruct((rows * cols * MESSAGE, TILE), BF16), turned),
        [
            VMEM((2 * SIDE * TILE, TILE), BF16),
            VMEM((BAND, PIX), F32),
            VMEM((4 * PHASE, BAND, PIX), BF16),
            VMEM((ANGLES * TILE, TILE), F32),
            VMEM((rows * cols * MESSAGE, TILE), F32),
            half,
            half,
            VMEM(turned.shape, F32),
            VMEM(measured[:, 0].shape, F32),
            VMEM(ray_weight[:, 0].shape, F32),
            pltpu.SemaphoreType.DMA((10,)),
        ]
        + [VMEM((TILE, TILE), F32)] * ANGLES,
        30_000_000_000,
        tight=False,
    )
    got = lax.all_to_all(
        sent.reshape(rows * cols, MESSAGE, TILE), both, split_axis=0, concat_axis=0, tiled=True
    )
    blocks = rows
    starts = shadow_start.reshape(-1, ANGLES)
    starts = lax.dynamic_slice_in_dim(starts, col_index * 2, 2, 1).reshape(-1)
    out = call(
        owner_kernel,
        (starts, col_index.reshape(1)),
        (),
        (got.reshape(-1, TILE),),
        jax.ShapeDtypeStruct((rows * cols * 4, TILE), BF16),
        [
            VMEM((2 * blocks, 3 * TILE), F32),
            VMEM((2, blocks + 1, 8, TILE), F32),
            VMEM((rows * cols * 4, TILE), F32),
            VMEM((3 * TILE, TILE), F32),
            VMEM((rows * cols * MESSAGE, TILE), F32),
            VMEM((rows * cols * MESSAGE, TILE), BF16),
            pltpu.SemaphoreType.DMA,
        ]
        + [VMEM((blocks, 8, TILE), F32)] * 16,
        10_000_000_000,
    )
    shadows = lax.all_to_all(
        out.reshape(rows * cols, 4, TILE), both, split_axis=0, concat_axis=0, tiled=True
    )
    bins = jnp.arange(BINS, dtype=F32)
    delta_lanes = (table[PAIRS : 2 * PAIRS, :, None] - bins).reshape(-1, BAND)
    angle_lanes = jnp.repeat(table[2 * PAIRS :], BINS, axis=1)
    side = jax.ShapeDtypeStruct((8, 8, TILE), F32)
    edge = jax.ShapeDtypeStruct((TILE // 8, 8, TILE), F32)
    x, left, right, top, bottom = call(
        backward_kernel,
        (table,),
        (delta_lanes, angle_lanes),
        (image, shadows.reshape(-1, TILE)),
        (turned, side, side, edge, edge),
        [
            VMEM((PIX, BAND), F32),
            VMEM((4 * PHASE, PIX, BAND), BF16),
            VMEM((ANGLES, TILE, TILE), F32),
            VMEM((rows * cols * 4, TILE), F32),
            VMEM((rows * cols * 4, TILE), F32),
            VMEM(turned.shape, F32),
            VMEM(turned.shape, F32),
            VMEM((rows * cols * 4, TILE), BF16),
            pltpu.SemaphoreType.DMA((2,)),
        ],
        30_000_000_000,
    )
    before = lax.ppermute(right, "col", [(i, i + 1) for i in range(cols - 1)])
    after = lax.ppermute(left, "col", [(i + 1, i) for i in range(cols - 1)])
    upward = jnp.concatenate([top, before[:TV_STEPS], after[:TV_STEPS]], axis=0)
    downward = jnp.concatenate([bottom, before[TV_STEPS:], after[TV_STEPS:]], axis=0)
    above = lax.ppermute(downward, "row", [(i, i + 1) for i in range(rows - 1)])
    below = lax.ppermute(upward, "row", [(i + 1, i) for i in range(rows - 1)])
    place = jnp.stack(
        [row_index > 0, row_index < rows - 1, col_index > 0, col_index < cols - 1]
    ).astype(jnp.int32)
    wide = VMEM((SIDE + 2 * TV_STEPS, TILE + 32, TILE), F32)
    few = VMEM((2 * TV_STEPS, TILE + 32, TILE), F32)
    scratch = [wide, wide, few, VMEM((2, TILE + 32, TILE), F32), half, half]
    scratch.append(pltpu.SemaphoreType.DMA((16,)))
    final = jax.ShapeDtypeStruct(current_image.shape, F32)
    smooth = call(
        functools.partial(smooth_kernel, 1),
        (place,),
        (before, after),
        (x,),
        final,
        scratch,
        10_000_000_000,
    )
    return call(
        functools.partial(smooth_kernel, 0),
        (place,),
        (before, after, above, below),
        (x, smooth),
        final,
        scratch,
        10_000_000_000,
        {6: 0},
    )


def solution(mesh):
    return jax.shard_map(
        local,
        mesh=mesh,
        in_specs=(
            P(None, "row", "col"),
            P("col", "row", None, None),
            P("col", "row", None),
            P(),
            P(),
        ),
        out_specs=P(None, "row", "col"),
        check_vma=False,
    )
```

```python
import functools
import math

import jax
import jax.numpy as jnp
from jax import lax
from jax.experimental import pallas as pl
from jax.experimental.pallas import tpu as pltpu
from jax.sharding import PartitionSpec as P

TILE = 128
ANGLES = 16
ALL_ANGLES = 256
TV_STEPS = 4
SIDE = 16
PATCHES = TILE // SIDE
PIX = SIDE * SIDE
BINS = 24
ROWS = 32
BAND = ANGLES * BINS
PAIRS = PATCHES * PATCHES // 2
PHASE = 4
STRIDE = 4
TABLE = 2 * PAIRS + 8
MESSAGE = 8

inverse_root = 0.7071067811865476
smoothing = 0.25
descent_step = 0.05

VMEM = pltpu.VMEM
F32 = jnp.float32
BF16 = jnp.bfloat16


def geometry(angle_ids):
    radians = angle_ids.astype(F32) * (math.pi / ALL_ANGLES)
    cosine = jnp.cos(radians) * inverse_root
    sine = jnp.sin(radians) * inverse_root
    row = lax.broadcasted_iota(jnp.int32, (TABLE, TILE), 0)
    patch = row & (PAIRS - 1)
    down = (patch >> 3).astype(F32) * SIDE - (TILE - 1) / 2.0
    across = (patch & (PATCHES - 1)).astype(F32) * SIDE - (TILE - 1) / 2.0
    corner = TILE / 2.0 + down * cosine + across * sine
    low = corner + (SIDE - 1) * (jnp.minimum(cosine, 0.0) + jnp.minimum(sine, 0.0))
    base = jnp.clip(jnp.floor((jnp.floor(low - 1.5) + 1.0) / 8.0) * 8.0, 0.0, TILE - BINS)
    delta = corner - base - 0.5
    ends = jnp.where(row == 2 * PAIRS, cosine, sine)
    return jnp.where(row < PAIRS, base, jnp.where(row < 2 * PAIRS, delta, ends))


def reversal():
    there = lax.broadcasted_iota(jnp.int32, (TILE, TILE), 0)
    here = lax.broadcasted_iota(jnp.int32, (TILE, TILE), 1)
    return jnp.where(there + here == TILE - 1, 1.0, 0.0).astype(BF16)


def reverse_lanes(value):
    high = value.astype(BF16)
    low = (value - high.astype(F32)).astype(BF16)
    both = jnp.concatenate([high, low], axis=1)
    turn = reversal()
    return jnp.dot(both, jnp.concatenate([turn, turn], axis=0), preferred_element_type=F32)


def pipeline(build, use, bands):
    def phase(i, action, slot):
        for j in range(PHASE):
            at = i * PHASE + j
            half = at // PATCHES
            col = at % PATCHES
            for own in range(2):
                patch = (2 * half + own) * PATCHES + col
                band = bands.at[(slot * PHASE + j) * 2 + own]
                if action is build:
                    build(patch, band)
                else:
                    use(patch, band, half, col, own)

    phase(0, build, 0)
    phases = 2 * PATCHES // PHASE

    def step(i, carry):
        phase(2 * i + 1, build, 1)
        phase(2 * i, use, 0)
        phase(jnp.minimum(2 * i + 2, phases - 1), build, 0)
        phase(2 * i + 1, use, 1)
        return carry

    lax.fori_loop(0, phases // 2, step, 0)


def blocks_at(half):
    return 2 * half, PATCHES - 1 - 2 * half, 2 * half + 1, PATCHES - 2 - 2 * half


def reflected(ref, i):
    other = (i // SIDE) * SIDE + SIDE - 1 - i % SIDE
    back = 7 - lax.broadcasted_iota(jnp.int32, (8, TILE), 0)
    mirrored = lax.broadcasted_iota(jnp.int32, (8, TILE), 1) & ROWS != 0
    parts = []
    for g in range(TILE // 8):
        far = ref[other, TILE - 8 * (g + 1) : TILE - 8 * g, :]
        far = jnp.take_along_axis(far, back, axis=0)
        parts.append(jnp.where(mirrored, far, ref[i, 8 * g : 8 * (g + 1), :]))
    return jnp.concatenate(parts, axis=0)


def forward_kernel(
    own_ref, angles_ref, image_ref, given_ref, given_weight_ref,
    out_ref, turned_ref, geometry_ref, table_ref, xt, rel, bands, tails, message, image0_ref,
    image1_ref, flat,
    measured_ref, weight_ref, sems, *sums,
):
    slices = ROWS // 2
    coming = [[], []]
    for part, start in ((0, 0), (0, 6), (1, 2), (1, 4)):
        spot = pl.ds(start * SIDE, 2 * SIDE)
        for t, ref in enumerate((image0_ref, image1_ref)):
            coming[part].append(
                pltpu.make_async_copy(
                    image_ref.at[:, spot, pl.ds(t * TILE, TILE)],
                    ref.reshape(slices, TILE, TILE).at[:, spot, :],
                    sems.at[2 + start + t],
                )
            )
    small = [
        pltpu.make_async_copy(given_ref, measured_ref, sems.at[0]),
        pltpu.make_async_copy(given_weight_ref, weight_ref, sems.at[1]),
    ]
    for copy in (*coming[0], *coming[1], *small):
        copy.start()
    place = lax.broadcasted_iota(jnp.int32, (1, TILE), 1)
    angles = jnp.zeros((1, TILE), jnp.int32)
    for a in range(ANGLES):
        angles = jnp.where(place == a, angles_ref[a], angles)
    geometry_ref[...] = geometry(angles)
    table = pltpu.make_async_copy(geometry_ref, table_ref, sems.at[10])
    table.start()
    for ref in sums:
        ref[...] = jnp.zeros_like(ref)
    def rows_of(u):
        return [ref[pl.ds(u, slices, stride=TILE), :] for ref in (image0_ref, image1_ref)]

    def flip(i, carry):
        rows = []
        for block in blocks_at(i // SIDE):
            rows += rows_of(block * SIDE + i % SIDE)
        flat[i] = jnp.concatenate(rows, axis=0).T
        return carry

    for part in range(2):
        for copy in coming[part]:
            copy.wait()
        lax.fori_loop(part * SIDE, (part + 1) * SIDE, flip, 0, unroll=4)
    for copy in small:
        copy.wait()
    going = pltpu.make_async_copy(flat, turned_ref, sems.at[0])
    going.start()

    def reflect(i, carry):
        value = reflected(flat, i)
        xt[pl.ds(pl.multiple_of(i * TILE, TILE), TILE), :] = value.astype(BF16)
        return carry

    lax.fori_loop(0, 2 * SIDE, reflect, 0, unroll=2)

    table.wait()
    lane = lax.broadcasted_iota(jnp.int32, (BINS, PIX), 1)
    bin_at = lax.broadcasted_iota(jnp.int32, (BINS, PIX), 0).astype(F32)
    down = (lane // SIDE).astype(F32)
    across = (lane % SIDE).astype(F32)
    for a in range(ANGLES):
        rel[a * BINS : (a + 1) * BINS, :] = (
            down * table_ref[2 * PAIRS, a] + across * table_ref[2 * PAIRS + 1, a] - bin_at
        )

    def build(patch, band):
        for a in range(0, ANGLES, 2):
            pair = []
            for b in (a, a + 1):
                away = jnp.abs(rel[b * BINS : (b + 1) * BINS, :] + table_ref[PAIRS + patch, b])
                pair.append(1.0 - away)
            rounded = jnp.concatenate(pair, axis=0).astype(BF16)
            band[a * BINS : (a + 2) * BINS, :] = jnp.maximum(rounded, jnp.zeros_like(rounded))

    first_half = lax.broadcasted_iota(jnp.int32, (PIX, TILE), 1) < TILE // 2

    def project(patch, band, half, col, own):
        pieces = []
        for u in range(SIDE):
            start = pl.multiple_of((half * SIDE + u) * TILE + col * SIDE, SIDE)
            pieces.append(xt[pl.ds(start, SIDE), :])
        pixels = jnp.concatenate(pieces, axis=0)
        nothing = jnp.zeros_like(pixels)
        pixels = jnp.where(first_half, *((nothing, pixels) if own else (pixels, nothing)))
        got = jnp.dot(band[...], pixels, preferred_element_type=F32)
        for a in range(ANGLES):
            start = pl.multiple_of(table_ref[patch, a].astype(jnp.int32), 8)
            sums[a][pl.ds(start, BINS), :] += got[a * BINS : (a + 1) * BINS, :]

    pipeline(build, project, bands)
    stride = MESSAGE * ANGLES // 2
    for a in range(ANGLES):
        tails[a * TILE : (a + 1) * TILE, :] = sums[a][...].T * 0.03125
    mirrored = [
        tails[a * TILE + ROWS : a * TILE + 2 * ROWS, :]
        + tails[a * TILE + 3 * ROWS : (a + 1) * TILE, :]
        for a in range(ANGLES)
    ]
    mirrored = reverse_lanes(jnp.concatenate(mirrored, axis=0))
    for a in range(ANGLES):
        total = tails[a * TILE : a * TILE + ROWS, :] + tails[a * TILE + 2 * ROWS : a * TILE + 3 * ROWS, :]
        total = total + mirrored[a * ROWS : (a + 1) * ROWS, :]
        for t in range(2):
            row = (a // 2) * MESSAGE + t * 2 + a % 2
            message[pl.ds(row, slices, stride=stride), :] = total[t * slices : (t + 1) * slices, :]
    row = own_ref[0] * MESSAGE + 4
    for h in range(2):
        message[pl.ds(row + h, slices, stride=stride), :] = measured_ref[h]
        weight = jnp.broadcast_to(weight_ref[h : h + 1, :], (slices, TILE))
        message[pl.ds(row + 2 + h, slices, stride=stride), :] = weight
    out_ref[...] = message[...].astype(BF16)
    going.wait()


def owner_kernel(
    starts_ref, own_ref, sent_ref, out_ref, wide, filt, staged, ramp_ref, got_ref, came, sem, *sums
):
    coming = pltpu.make_async_copy(sent_ref, came, sem)
    coming.start()
    blocks = 16
    per = 8
    groups = staged.shape[0] // (8 * per)
    for ref in sums:
        ref[...] = jnp.zeros_like(ref)
    lane = lax.broadcasted_iota(jnp.int32, (8, TILE), 1)
    sub = lax.broadcasted_iota(jnp.int32, (8, TILE), 0)

    offset = (
        lax.broadcasted_iota(jnp.int32, (3 * TILE, TILE), 1)
        + TILE
        - lax.broadcasted_iota(jnp.int32, (3 * TILE, TILE), 0)
    )
    nonzero = jnp.where(offset == 0, 1, offset).astype(F32)
    ramp = jnp.where((offset & 1) == 1, -1.0 / (math.pi * math.pi * nonzero * nonzero), 0.0)
    ramp = jnp.where(offset == 0, 0.25, ramp)
    ramp = jnp.where(jnp.abs(offset) < TILE, ramp, 0.0)
    ramp_ref[...] = ramp
    coming.wait()
    got_ref[...] = came[...].astype(F32)

    def add(g, carry):
        turned = []
        for i in range(2 * per):
            source = g * 2 * per + i
            rows = got_ref[pl.ds(pl.multiple_of(source * MESSAGE, MESSAGE), MESSAGE), :]
            for k in range(4):
                start = starts_ref[source * 4 + k]
                turned.append((start >> 7, start & (TILE - 1), rows, i % 2 * 4 + k, k))
        turned = [
            (block, shift, pltpu.roll(rows, shift, 1), slot) for block, shift, rows, slot, k in turned
        ]
        for block, shift, value, slot in turned:
            tail = jnp.where(lane >= shift, value, 0.0)
            sums[slot][block, 0] += tail
            sums[slot][block, 1] += value - tail
        return carry

    lax.fori_loop(0, groups, add, 0)
    wide[...] = jnp.zeros_like(wide)
    for b in range(blocks):
        total = jnp.zeros((8, TILE), F32)
        for slot in range(8):
            here = sums[slot][b, 0]
            if b:
                here = here + sums[slot][b - 1, 1]
            total = total + jnp.where(sub == slot % 4, here, 0.0)
        home = pl.multiple_of((b * 8 + own_ref[0]) * MESSAGE, MESSAGE)
        given = got_ref[pl.ds(home, MESSAGE), :]
        for h in range(2):
            row = total[h : h + 1, :] + total[2 + h : 3 + h, :]
            wide[h * blocks + b : h * blocks + b + 1, TILE : 2 * TILE] = given[6 + h : 7 + h, :] * (
                given[4 + h : 5 + h, :] - row
            )
    centre = wide[:, TILE : 2 * TILE]
    at = lax.broadcasted_iota(jnp.int32, (2 * blocks, TILE), 0) % blocks
    wide[:, :TILE] = jnp.where(at == 0, 0.0, pltpu.roll(centre, 1, 0))
    wide[:, 2 * TILE :] = jnp.where(at == blocks - 1, 0.0, pltpu.roll(centre, 2 * blocks - 1, 0))
    done = jnp.dot(wide[...], ramp_ref[...], precision=lax.Precision.HIGHEST, preferred_element_type=F32)
    wide[:, :TILE] = done.astype(BF16).astype(F32)
    filt[...] = jnp.zeros_like(filt)
    for h in range(2):
        for b in range(blocks):
            row = wide[h * blocks + b : h * blocks + b + 1, :TILE]
            filt[h, b] = jnp.broadcast_to(row, (8, TILE))

    def take(g, carry):
        mixed = []
        for i in range(per):
            for k in range(8):
                start = starts_ref[(g * per + i) * 8 + k]
                block, shift = start >> 7, start & (TILE - 1)
                value = jnp.where(lane >= shift, filt[k % 2, block], filt[k % 2, block + 1])
                mixed.append((value, (TILE - shift) & (TILE - 1)))
        turned = [pltpu.roll(value, shift, 1) for value, shift in mixed]
        for i in range(per):
            rows = turned[i * 8]
            for k in range(1, 8):
                rows = jnp.where(sub == k, turned[i * 8 + k], rows)
            staged[pl.ds(pl.multiple_of((g * per + i) * 8, 8), 8), :] = rows
        return carry

    lax.fori_loop(0, groups, take, 0)
    out_ref[...] = staged[...].astype(BF16)


def backward_kernel(
    table_ref, delta_ref, lanes_ref, image_ref, sent_ref,
    final_ref, left_ref, right_ref, top_ref, bottom_ref,
    rel, bands, shadows, staged, mirror, update, image, got_ref, sems,
):
    slices = ROWS // 2
    arriving = pltpu.make_async_copy(sent_ref, got_ref, sems.at[1])
    arriving.start()
    coming = pltpu.make_async_copy(image_ref, image, sems.at[0])
    coming.start()
    pixel = lax.broadcasted_iota(jnp.int32, (PIX, BAND), 0)
    rel[...] = (
        (pixel // SIDE).astype(F32) * lanes_ref[0:1, :]
        + (pixel % SIDE).astype(F32) * lanes_ref[1:2, :]
    )
    arriving.wait()
    staged[...] = got_ref[...].astype(F32)
    mirror[...] = jnp.dot(got_ref[...], reversal(), preferred_element_type=F32)
    for a in range(ANGLES):
        parts = []
        for ref in (staged, mirror):
            for t in range(2):
                row = (a // 2) * 4 + t * 2 + a % 2
                parts.append(ref[pl.ds(row, slices, stride=ROWS), :])
        shadows[a] = jnp.concatenate(parts + parts, axis=0).T

    def build(patch, band):
        shift = delta_ref[pl.ds(patch, 1), :]
        for r in range(0, PIX, 16):
            away = jnp.abs(rel[r : r + 16, :] + shift)
            rounded = (1.0 - away).astype(BF16)
            band[r : r + 16, :] = jnp.maximum(rounded, jnp.zeros_like(rounded))

    def spread(patch, band, half, col, own):
        pieces = []
        for a in range(ANGLES):
            start = pl.multiple_of(table_ref[patch, a].astype(jnp.int32), 8)
            pieces.append(shadows[a, pl.ds(start, BINS), :])
        seen = jnp.concatenate(pieces, axis=0).astype(BF16)
        got = jnp.dot(band[...], seen, preferred_element_type=F32)
        for u in range(SIDE):
            spot = pl.ds(pl.multiple_of(col * SIDE, SIDE), SIDE)
            piece = got[u * SIDE : (u + 1) * SIDE, :]
            if own:
                update[half * SIDE + u, spot, TILE // 2 :] = piece[:, TILE // 2 :]
            else:
                update[half * SIDE + u, spot, :] = piece

    pipeline(build, spread, bands)

    coming.wait()

    def finish(i, carry):
        image[i] = image[i] + 0.25 * reflected(update, i)
        return carry

    lax.fori_loop(0, SIDE, finish, 0, unroll=2)
    going = [
        pltpu.make_async_copy(
            image.at[pl.ds(h * SIDE, SIDE)], final_ref.at[pl.ds(h * SIDE, SIDE)], sems.at[h]
        )
        for h in range(2)
    ]
    going[0].start()
    lax.fori_loop(SIDE, 2 * SIDE, finish, 0, unroll=2)
    going[1].start()
    lane = lax.broadcasted_iota(jnp.int32, (8, TILE), 1)
    sub = lax.broadcasted_iota(jnp.int32, (8, TILE), 0)
    second = lane & slices != 0

    def column(u, start, far):
        value = [image[h * SIDE + u, start : start + 8, :] for h in range(2)]
        value[far] = pltpu.roll(value[far], 4, 0)
        return jnp.where(sub < 4, value[0], value[1])

    for u in range(8):
        here, there = column(u, 0, 1), column(u + 8, 0, 1)
        left_ref[u] = jnp.where(second, pltpu.roll(there, slices, 1), here)
        here, there = column(u, TILE - 8, 0), column(u + 8, TILE - 8, 0)
        right_ref[u] = jnp.where(second, here, pltpu.roll(there, TILE - slices, 1))
    lanes = lax.broadcasted_iota(jnp.int32, (TILE, TILE), 1) // ROWS
    for ref, row, shift in ((top_ref, 0, 0), (bottom_ref, SIDE - TV_STEPS, TILE - ROWS)):
        packed = jnp.zeros((TILE, TILE), F32)
        for k in range(TV_STEPS):
            turned = pltpu.roll(image[row + k], (k * ROWS + shift) % TILE, 1)
            packed = jnp.where(lanes == k, turned, packed)
        ref[...] = packed.reshape(TILE // 8, 8, TILE)
    for copy in going:
        copy.wait()


def smooth_kernel(half, place_ref, before_ref, after_ref, *refs):
    if half == 0:
        above_ref, below_ref, x_ref, unused, out_ref = refs[:5]
    else:
        x_ref, out_ref = refs[:2]
    first, second, other, flow, out0, out1, sems = refs[-7:]
    slices = ROWS // 2
    own = pl.ds(16, TILE)
    wide = TILE + 16
    last_rows = SIDE - TV_STEPS
    coming = [
        pltpu.make_async_copy(
            x_ref.at[pl.ds(start, count)], ref.at[pl.ds(row, count), own, :], sems.at[i]
        )
        for i, (start, count, ref, row) in enumerate(
            (
                (half * SIDE, SIDE, first, TV_STEPS),
                ((1 - half) * SIDE, TV_STEPS, other, 0),
                ((1 - half) * SIDE + last_rows, TV_STEPS, other, TV_STEPS),
            )
        )
    ]
    for copy in coming:
        copy.start()
    lane = lax.broadcasted_iota(jnp.int32, (8, TILE), 1)
    later = lane & slices != 0
    has_above, has_below, has_before, has_after = (place_ref[i] for i in range(4))

    def roll(value, shift):
        return pltpu.roll(value, shift % TILE, 1)

    def sink(value):
        return pltpu.roll(value, 4, 0)

    if half == 0:
        for ref, row, shift, left, right in (
            (above_ref, 0, 0, -ROWS, -ROWS),
            (below_ref, SIDE + TV_STEPS, ROWS, slices, ROWS + slices),
        ):
            for k in range(TV_STEPS):
                back = shift - k * ROWS
                lead = jnp.where(
                    later,
                    roll(ref[TILE // 8 - 1], back + slices),
                    sink(roll(ref[TILE // 8 + k], left)),
                )
                trail = jnp.where(
                    later,
                    roll(ref[TILE // 8 + TV_STEPS + k], right),
                    roll(ref[0], back - slices),
                )
                first[row + k, 8:16, :] = lead
                for g in range(TILE // 8):
                    first[row + k, 16 + 8 * g : 24 + 8 * g, :] = roll(ref[g], back)
                first[row + k, 16 + TILE : 24 + TILE, :] = trail
    for copy in coming:
        copy.wait()
    sides = [(first, u + TV_STEPS, u, half) for u in range(SIDE)]
    sides += [(other, k, k, 1 - half) for k in range(TV_STEPS)]
    sides += [(other, TV_STEPS + k, last_rows + k, 1 - half) for k in range(TV_STEPS)]
    for ref, row, u, h in sides:
        before = before_ref[u % 8]
        after = after_ref[u % 8]
        if u < 8:
            before, after = roll(before, -slices), roll(after, slices)
        if h:
            after = sink(after)
        else:
            before = sink(before)
        lead = jnp.where(later, roll(ref[row, 8 + TILE : 16 + TILE, :], slices), before)
        trail = jnp.where(later, after, roll(ref[row, 16:24, :], -slices))
        ref[row, 8:16, :] = lead
        ref[row, 16 + TILE : 24 + TILE, :] = trail

    group = lax.broadcasted_iota(jnp.int32, (wide, TILE), 1) // ROWS
    span = pl.ds(8, wide)
    for k in range(TV_STEPS):
        for mine, others, target, low in (
            (SIDE + k, TV_STEPS + k, k, True),
            (TV_STEPS + k, k, SIDE + TV_STEPS + k, False),
        ):
            mine = first[mine, span, :]
            others = other[others, span, :]
            if half == 0:
                value = roll(jnp.where(group == (1 if low else 0), others, mine), 2 * ROWS)
                outer = group == (0 if low else 1)
                value = jnp.where(outer, first[target, span, :], value)
            else:
                value = roll(jnp.where(group == (2 if low else 3), others, mine), 2 * ROWS)
                step = roll(mine, ROWS if low else -ROWS)
                value = jnp.where(group == (3 if low else 2), step, value)
            first[target, span, :] = value

    keep_lead = later | (has_before == 1)
    keep_trail = jnp.logical_not(later) | (has_after == 1)

    def flows(source, r):
        here = source[r, span, :]
        down = source[r + 1, span, :] - here
        right = source[r, pl.ds(9, wide), :] - here
        inverse = lax.rsqrt(smoothing * smoothing + down * down + right * right)
        return here, down * inverse, right * inverse

    for k in range(TV_STEPS):
        source, target = (first, second) if k % 2 == 0 else (second, first)
        last = k == TV_STEPS - 1

        def row(r, came, slot, inside=None, source=source, target=target, last=last):
            here, down, right = flows(source, r)
            flow[slot, span, :] = right
            left = flow[slot, pl.ds(7, wide), :]
            fresh = here - descent_step * (came - down + left - right)
            if last:
                turned = fresh[8 : 8 + TILE, :].T
                for g, block in enumerate(blocks_at(half)):
                    spot = pl.ds(block * SIDE + r - TV_STEPS, slices, stride=TILE)
                    for t, ref in enumerate((out0, out1)):
                        start = g * ROWS + t * slices
                        ref[spot, :] = turned[start : start + slices, :]
                return down
            if inside is not None:
                fresh = jnp.where(inside, fresh, 0.0)
            target[r, 8:16, :] = jnp.where(keep_lead, fresh[:8, :], 0.0)
            target[r, own, :] = fresh[8 : 8 + TILE, :]
            target[r, 16 + TILE : 24 + TILE, :] = jnp.where(keep_trail, fresh[wide - 8 :, :], 0.0)
            return down

        unused, came, unused = flows(source, k)
        for r in range(k + 1, TV_STEPS):
            came = row(r, came, r % 2, None if half else (group != 0) | (has_above == 1))

        def some(i, came, row=row):
            for j in range(STRIDE):
                came = row(TV_STEPS + STRIDE * i + j, came, j % 2)
            return came

        if not last:
            came = lax.fori_loop(0, SIDE // STRIDE, some, came)
        for r in range(SIDE + TV_STEPS, SIDE + 2 * TV_STEPS - 1 - k):
            came = row(r, came, r % 2, None if half else (group != 1) | (has_below == 1))
    going = []
    for part in range(2):
        came = lax.fori_loop(
            part * SIDE // 2 // STRIDE, (part + 1) * SIDE // 2 // STRIDE, some, came
        )
        for block in blocks_at(half):
            spot = pl.ds(block * SIDE + part * 8, 8)
            for t, ref in enumerate((out0, out1)):
                going.append(
                    pltpu.make_async_copy(
                        ref.reshape(slices, TILE, TILE).at[:, spot, :],
                        out_ref.at[:, spot, pl.ds(t * TILE, TILE)],
                        sems.at[len(going)],
                    )
                )
                going[-1].start()
    for copy in going:
        copy.wait()


def call(
    kernel, scalars, arrays, left, outs, scratch, flops, aliases=None, tight=True
):
    vmem = pl.BlockSpec(memory_space=VMEM)
    smem = pl.BlockSpec(memory_space=pltpu.SMEM)
    operands = (*scalars, *arrays, *left)
    bytes_of = lambda x: math.prod(x.shape) * x.dtype.itemsize
    stays = lambda x: bytes_of(x) > 1 << 20
    held = sum(bytes_of(x) for x in arrays)
    held += sum(bytes_of(x) for x in jax.tree.leaves(outs) if not stays(x))
    held += sum(bytes_of(x) for x in scratch if getattr(x, "memory_space", None) == VMEM)
    return pl.pallas_call(
        kernel,
        out_shape=outs,
        in_specs=[smem] * len(scalars)
        + [vmem] * len(arrays)
        + [pl.BlockSpec(memory_space=pl.ANY)] * len(left),
        out_specs=jax.tree.map(
            lambda x: pl.BlockSpec(memory_space=pl.ANY) if stays(x) else vmem, outs
        ),
        scratch_shapes=scratch,
        input_output_aliases=aliases or {},
        compiler_params=pltpu.CompilerParams(vmem_limit_bytes=held + (6 << 20) if tight else None),
        cost_estimate=pl.CostEstimate(
            flops=flops, bytes_accessed=sum(map(bytes_of, operands)), transcendentals=0
        ),
    )(*operands)


def local(current_image, measured, ray_weight, angle_ids, shadow_start):
    row_index = lax.axis_index("row")
    col_index = lax.axis_index("col")
    rows = lax.axis_size("row")
    cols = lax.axis_size("col")
    slices = current_image.shape[0]
    both = ("row", "col")
    half = VMEM((slices * TILE, TILE), F32)

    turned = jax.ShapeDtypeStruct((2 * SIDE, TILE, TILE), F32)
    sent, image, table = call(
        forward_kernel,
        (col_index.reshape(1), angle_ids),
        (),
        (current_image, measured[:, 0], ray_weight[:, 0]),
        (jax.ShapeDtypeStruct((rows * cols * MESSAGE, TILE), BF16), turned, jax.ShapeDtypeStruct((TABLE, TILE), F32)),
        [
            pltpu.SMEM((TABLE, TILE), F32),
            VMEM((2 * SIDE * TILE, TILE), BF16),
            VMEM((BAND, PIX), F32),
            VMEM((4 * PHASE, BAND, PIX), BF16),
            VMEM((ANGLES * TILE, TILE), F32),
            VMEM((rows * cols * MESSAGE, TILE), F32),
            half,
            half,
            VMEM(turned.shape, F32),
            VMEM(measured[:, 0].shape, F32),
            VMEM(ray_weight[:, 0].shape, F32),
            pltpu.SemaphoreType.DMA((11,)),
        ]
        + [VMEM((TILE, TILE), F32)] * ANGLES,
        30_000_000_000,
        tight=False,
    )
    got = lax.all_to_all(
        sent.reshape(rows * cols, MESSAGE, TILE), both, split_axis=0, concat_axis=0, tiled=True
    )
    blocks = rows
    starts = shadow_start.reshape(-1, ANGLES)
    starts = lax.dynamic_slice_in_dim(starts, col_index * 2, 2, 1).reshape(-1)
    out = call(
        owner_kernel,
        (starts, col_index.reshape(1)),
        (),
        (got.reshape(-1, TILE),),
        jax.ShapeDtypeStruct((rows * cols * 4, TILE), BF16),
        [
            VMEM((2 * blocks, 3 * TILE), F32),
            VMEM((2, blocks + 1, 8, TILE), F32),
            VMEM((rows * cols * 4, TILE), F32),
            VMEM((3 * TILE, TILE), F32),
            VMEM((rows * cols * MESSAGE, TILE), F32),
            VMEM((rows * cols * MESSAGE, TILE), BF16),
            pltpu.SemaphoreType.DMA,
        ]
        + [VMEM((blocks, 2, 8, TILE), F32)] * 8,
        10_000_000_000,
    )
    shadows = lax.all_to_all(
        out.reshape(rows * cols, 4, TILE), both, split_axis=0, concat_axis=0, tiled=True
    )
    table = table[: 2 * PAIRS + 2, :ANGLES]
    bins = jnp.arange(BINS, dtype=F32)
    delta_lanes = (table[PAIRS : 2 * PAIRS, :, None] - bins).reshape(-1, BAND)
    angle_lanes = jnp.repeat(table[2 * PAIRS :], BINS, axis=1)
    side = jax.ShapeDtypeStruct((8, 8, TILE), F32)
    edge = jax.ShapeDtypeStruct((TILE // 8, 8, TILE), F32)
    x, left, right, top, bottom = call(
        backward_kernel,
        (table[:PAIRS],),
        (delta_lanes, angle_lanes),
        (image, shadows.reshape(-1, TILE)),
        (turned, side, side, edge, edge),
        [
            VMEM((PIX, BAND), F32),
            VMEM((4 * PHASE, PIX, BAND), BF16),
            VMEM((ANGLES, TILE, TILE), F32),
            VMEM((rows * cols * 4, TILE), F32),
            VMEM((rows * cols * 4, TILE), F32),
            VMEM(turned.shape, F32),
            VMEM(turned.shape, F32),
            VMEM((rows * cols * 4, TILE), BF16),
            pltpu.SemaphoreType.DMA((2,)),
        ],
        30_000_000_000,
    )
    before = lax.ppermute(right, "col", [(i, i + 1) for i in range(cols - 1)])
    after = lax.ppermute(left, "col", [(i + 1, i) for i in range(cols - 1)])
    upward = jnp.concatenate([top, before[:TV_STEPS], after[:TV_STEPS]], axis=0)
    downward = jnp.concatenate([bottom, before[TV_STEPS:], after[TV_STEPS:]], axis=0)
    above = lax.ppermute(downward, "row", [(i, i + 1) for i in range(rows - 1)])
    below = lax.ppermute(upward, "row", [(i + 1, i) for i in range(rows - 1)])
    place = jnp.stack(
        [row_index > 0, row_index < rows - 1, col_index > 0, col_index < cols - 1]
    ).astype(jnp.int32)
    wide = VMEM((SIDE + 2 * TV_STEPS, TILE + 32, TILE), F32)
    few = VMEM((2 * TV_STEPS, TILE + 32, TILE), F32)
    scratch = [wide, wide, few, VMEM((2, TILE + 32, TILE), F32), half, half]
    scratch.append(pltpu.SemaphoreType.DMA((16,)))
    final = jax.ShapeDtypeStruct(current_image.shape, F32)
    smooth = call(
        functools.partial(smooth_kernel, 1),
        (place,),
        (before, after),
        (x,),
        final,
        scratch,
        10_000_000_000,
    )
    return call(
        functools.partial(smooth_kernel, 0),
        (place,),
        (before, after, above, below),
        (x, smooth),
        final,
        scratch,
        10_000_000_000,
        {6: 0},
    )


def solution(mesh):
    return jax.shard_map(
        local,
        mesh=mesh,
        in_specs=(
            P(None, "row", "col"),
            P("col", "row", None, None),
            P("col", "row", None),
            P(),
            P(),
        ),
        out_specs=P(None, "row", "col"),
        check_vma=False,
    )
```

```python
import functools
import math

import jax
import jax.numpy as jnp
from jax import lax
from jax.experimental import pallas as pl
from jax.experimental.pallas import tpu as pltpu
from jax.sharding import PartitionSpec as P

TILE = 128
ANGLES = 16
ALL_ANGLES = 256
TV_STEPS = 4
SIDE = 16
PATCHES = TILE // SIDE
PIX = SIDE * SIDE
BINS = 24
ROWS = 32
BAND = ANGLES * BINS
PAIRS = PATCHES * PATCHES // 2
PHASE = 4
STRIDE = 4
TABLE = 2 * PAIRS + 8
MESSAGE = 8

inverse_root = 0.7071067811865476
smoothing = 0.25
descent_step = 0.05

VMEM = pltpu.VMEM
F32 = jnp.float32
BF16 = jnp.bfloat16


def geometry(angle_ids):
    radians = angle_ids.astype(F32) * (math.pi / ALL_ANGLES)
    cosine = jnp.cos(radians) * inverse_root
    sine = jnp.sin(radians) * inverse_root
    row = lax.broadcasted_iota(jnp.int32, (TABLE, TILE), 0)
    patch = row & (PAIRS - 1)
    down = (patch >> 3).astype(F32) * SIDE - (TILE - 1) / 2.0
    across = (patch & (PATCHES - 1)).astype(F32) * SIDE - (TILE - 1) / 2.0
    corner = TILE / 2.0 + down * cosine + across * sine
    low = corner + (SIDE - 1) * (jnp.minimum(cosine, 0.0) + jnp.minimum(sine, 0.0))
    base = jnp.clip(jnp.floor((jnp.floor(low - 1.5) + 1.0) / 8.0) * 8.0, 0.0, TILE - BINS)
    delta = corner - base - 0.5
    ends = jnp.where(row == 2 * PAIRS, cosine, sine)
    return jnp.where(row < PAIRS, base, jnp.where(row < 2 * PAIRS, delta, ends))


def reversal():
    there = lax.broadcasted_iota(jnp.int32, (TILE, TILE), 0)
    here = lax.broadcasted_iota(jnp.int32, (TILE, TILE), 1)
    return jnp.where(there + here == TILE - 1, 1.0, 0.0).astype(BF16)


def reverse_lanes(value):
    high = value.astype(BF16)
    low = (value - high.astype(F32)).astype(BF16)
    both = jnp.concatenate([high, low], axis=1)
    turn = reversal()
    return jnp.dot(both, jnp.concatenate([turn, turn], axis=0), preferred_element_type=F32)


def pipeline(build, use, bands):
    def phase(i, action, slot):
        for j in range(PHASE):
            at = i * PHASE + j
            half = at // PATCHES
            col = at % PATCHES
            for own in range(2):
                patch = (2 * half + own) * PATCHES + col
                band = bands.at[(slot * PHASE + j) * 2 + own]
                if action is build:
                    build(patch, band)
                else:
                    use(patch, band, half, col, own)

    phase(0, build, 0)
    phases = 2 * PATCHES // PHASE

    def step(i, carry):
        phase(2 * i + 1, build, 1)
        phase(2 * i, use, 0)
        phase(jnp.minimum(2 * i + 2, phases - 1), build, 0)
        phase(2 * i + 1, use, 1)
        return carry

    lax.fori_loop(0, phases // 2, step, 0)


def blocks_at(half):
    return 2 * half, PATCHES - 1 - 2 * half, 2 * half + 1, PATCHES - 2 - 2 * half


def reflected(ref, i):
    other = (i // SIDE) * SIDE + SIDE - 1 - i % SIDE
    back = 7 - lax.broadcasted_iota(jnp.int32, (8, TILE), 0)
    mirrored = lax.broadcasted_iota(jnp.int32, (8, TILE), 1) & ROWS != 0
    parts = []
    for g in range(TILE // 8):
        far = ref[other, TILE - 8 * (g + 1) : TILE - 8 * g, :]
        far = jnp.take_along_axis(far, back, axis=0)
        parts.append(jnp.where(mirrored, far, ref[i, 8 * g : 8 * (g + 1), :]))
    return jnp.concatenate(parts, axis=0)


def forward_kernel(
    own_ref, angles_ref, image_ref, given_ref, given_weight_ref,
    out_ref, turned_ref, geometry_ref, table_ref, xt, rel, bands, tails, message, image0_ref,
    image1_ref, flat,
    measured_ref, weight_ref, sems, *sums,
):
    slices = ROWS // 2
    coming = [[], []]
    for part, start in ((0, 0), (0, 6), (1, 2), (1, 4)):
        spot = pl.ds(start * SIDE, 2 * SIDE)
        for t, ref in enumerate((image0_ref, image1_ref)):
            coming[part].append(
                pltpu.make_async_copy(
                    image_ref.at[:, spot, pl.ds(t * TILE, TILE)],
                    ref.reshape(slices, TILE, TILE).at[:, spot, :],
                    sems.at[2 + start + t],
                )
            )
    small = [
        pltpu.make_async_copy(given_ref, measured_ref, sems.at[0]),
        pltpu.make_async_copy(given_weight_ref, weight_ref, sems.at[1]),
    ]
    for copy in (*coming[0], *coming[1], *small):
        copy.start()
    place = lax.broadcasted_iota(jnp.int32, (1, TILE), 1)
    angles = jnp.zeros((1, TILE), jnp.int32)
    for a in range(ANGLES):
        angles = jnp.where(place == a, angles_ref[a], angles)
    geometry_ref[...] = geometry(angles)
    table = pltpu.make_async_copy(geometry_ref, table_ref, sems.at[10])
    table.start()
    for ref in sums:
        ref[...] = jnp.zeros_like(ref)
    def rows_of(u):
        return [ref[pl.ds(u, slices, stride=TILE), :] for ref in (image0_ref, image1_ref)]

    def flip(i, carry):
        rows = []
        for block in blocks_at(i // SIDE):
            rows += rows_of(block * SIDE + i % SIDE)
        flat[i] = jnp.concatenate(rows, axis=0).T
        return carry

    for part in range(2):
        for copy in coming[part]:
            copy.wait()
        lax.fori_loop(part * SIDE, (part + 1) * SIDE, flip, 0, unroll=8)
    for copy in small:
        copy.wait()
    going = pltpu.make_async_copy(flat, turned_ref, sems.at[0])
    going.start()

    def reflect(i, carry):
        value = reflected(flat, i)
        xt[pl.ds(pl.multiple_of(i * TILE, TILE), TILE), :] = value.astype(BF16)
        return carry

    lax.fori_loop(0, 2 * SIDE, reflect, 0, unroll=2)

    table.wait()
    lane = lax.broadcasted_iota(jnp.int32, (BINS, PIX), 1)
    bin_at = lax.broadcasted_iota(jnp.int32, (BINS, PIX), 0).astype(F32)
    down = (lane // SIDE).astype(F32)
    across = (lane % SIDE).astype(F32)
    for a in range(ANGLES):
        rel[a * BINS : (a + 1) * BINS, :] = (
            down * table_ref[2 * PAIRS, a] + across * table_ref[2 * PAIRS + 1, a] - bin_at
        )

    def build(patch, band):
        for a in range(0, ANGLES, 2):
            pair = []
            for b in (a, a + 1):
                away = jnp.abs(rel[b * BINS : (b + 1) * BINS, :] + table_ref[PAIRS + patch, b])
                pair.append(1.0 - away)
            rounded = jnp.concatenate(pair, axis=0).astype(BF16)
            band[a * BINS : (a + 2) * BINS, :] = jnp.maximum(rounded, jnp.zeros_like(rounded))

    first_half = lax.broadcasted_iota(jnp.int32, (PIX, TILE), 1) < TILE // 2

    def project(patch, band, half, col, own):
        pieces = []
        for u in range(SIDE):
            start = pl.multiple_of((half * SIDE + u) * TILE + col * SIDE, SIDE)
            pieces.append(xt[pl.ds(start, SIDE), :])
        pixels = jnp.concatenate(pieces, axis=0)
        nothing = jnp.zeros_like(pixels)
        pixels = jnp.where(first_half, *((nothing, pixels) if own else (pixels, nothing)))
        got = jnp.dot(band[...], pixels, preferred_element_type=F32)
        for a in range(ANGLES):
            start = pl.multiple_of(table_ref[patch, a].astype(jnp.int32), 8)
            sums[a][pl.ds(start, BINS), :] += got[a * BINS : (a + 1) * BINS, :]

    pipeline(build, project, bands)
    stride = MESSAGE * ANGLES // 2
    for a in range(ANGLES):
        tails[a * TILE : (a + 1) * TILE, :] = sums[a][...].T * 0.03125
    mirrored = [
        tails[a * TILE + ROWS : a * TILE + 2 * ROWS, :]
        + tails[a * TILE + 3 * ROWS : (a + 1) * TILE, :]
        for a in range(ANGLES)
    ]
    mirrored = reverse_lanes(jnp.concatenate(mirrored, axis=0))
    for a in range(ANGLES):
        total = tails[a * TILE : a * TILE + ROWS, :] + tails[a * TILE + 2 * ROWS : a * TILE + 3 * ROWS, :]
        total = total + mirrored[a * ROWS : (a + 1) * ROWS, :]
        for t in range(2):
            row = (a // 2) * MESSAGE + t * 2 + a % 2
            message[pl.ds(row, slices, stride=stride), :] = total[t * slices : (t + 1) * slices, :]
    row = own_ref[0] * MESSAGE + 4
    for h in range(2):
        message[pl.ds(row + h, slices, stride=stride), :] = measured_ref[h]
        weight = jnp.broadcast_to(weight_ref[h : h + 1, :], (slices, TILE))
        message[pl.ds(row + 2 + h, slices, stride=stride), :] = weight
    out_ref[...] = message[...].astype(BF16)
    going.wait()


def owner_kernel(
    starts_ref, own_ref, sent_ref, out_ref, wide, filt, staged, ramp_ref, got_ref, *sums
):
    blocks = 16
    per = 8
    groups = staged.shape[0] // (8 * per)
    for ref in sums:
        ref[...] = jnp.zeros_like(ref)
    lane = lax.broadcasted_iota(jnp.int32, (8, TILE), 1)
    sub = lax.broadcasted_iota(jnp.int32, (8, TILE), 0)

    offset = (
        lax.broadcasted_iota(jnp.int32, (3 * TILE, TILE), 1)
        + TILE
        - lax.broadcasted_iota(jnp.int32, (3 * TILE, TILE), 0)
    )
    nonzero = jnp.where(offset == 0, 1, offset).astype(F32)
    ramp = jnp.where((offset & 1) == 1, -1.0 / (math.pi * math.pi * nonzero * nonzero), 0.0)
    ramp = jnp.where(offset == 0, 0.25, ramp)
    ramp = jnp.where(jnp.abs(offset) < TILE, ramp, 0.0)
    ramp_ref[...] = ramp
    got_ref[...] = sent_ref[...].astype(F32)

    def add(g, carry):
        turned = []
        for i in range(2 * per):
            source = g * 2 * per + i
            rows = got_ref[pl.ds(pl.multiple_of(source * MESSAGE, MESSAGE), MESSAGE), :]
            for k in range(4):
                start = starts_ref[source * 4 + k]
                turned.append((start >> 7, start & (TILE - 1), rows, i % 2 * 4 + k, k))
        turned = [
            (block, shift, pltpu.roll(rows, shift, 1), slot) for block, shift, rows, slot, k in turned
        ]
        for block, shift, value, slot in turned:
            tail = jnp.where(lane >= shift, value, 0.0)
            sums[slot][block, 0] += tail
            sums[slot][block, 1] += value - tail
        return carry

    lax.fori_loop(0, groups, add, 0)
    wide[...] = jnp.zeros_like(wide)
    for b in range(blocks):
        total = jnp.zeros((8, TILE), F32)
        for slot in range(8):
            here = sums[slot][b, 0]
            if b:
                here = here + sums[slot][b - 1, 1]
            total = total + jnp.where(sub == slot % 4, here, 0.0)
        home = pl.multiple_of((b * 8 + own_ref[0]) * MESSAGE, MESSAGE)
        given = got_ref[pl.ds(home, MESSAGE), :]
        for h in range(2):
            row = total[h : h + 1, :] + total[2 + h : 3 + h, :]
            wide[h * blocks + b : h * blocks + b + 1, TILE : 2 * TILE] = given[6 + h : 7 + h, :] * (
                given[4 + h : 5 + h, :] - row
            )
    centre = wide[:, TILE : 2 * TILE]
    at = lax.broadcasted_iota(jnp.int32, (2 * blocks, TILE), 0) % blocks
    wide[:, :TILE] = jnp.where(at == 0, 0.0, pltpu.roll(centre, 1, 0))
    wide[:, 2 * TILE :] = jnp.where(at == blocks - 1, 0.0, pltpu.roll(centre, 2 * blocks - 1, 0))
    done = jnp.dot(wide[...], ramp_ref[...], precision=lax.Precision.HIGHEST, preferred_element_type=F32)
    wide[:, :TILE] = done.astype(BF16).astype(F32)
    filt[...] = jnp.zeros_like(filt)
    for h in range(2):
        for b in range(blocks):
            row = wide[h * blocks + b : h * blocks + b + 1, :TILE]
            filt[h, b] = jnp.broadcast_to(row, (8, TILE))

    def take(g, carry):
        mixed = []
        for i in range(per):
            for k in range(8):
                start = starts_ref[(g * per + i) * 8 + k]
                block, shift = start >> 7, start & (TILE - 1)
                value = jnp.where(lane >= shift, filt[k % 2, block], filt[k % 2, block + 1])
                mixed.append((value, (TILE - shift) & (TILE - 1)))
        turned = [pltpu.roll(value, shift, 1) for value, shift in mixed]
        for i in range(per):
            rows = turned[i * 8]
            for k in range(1, 8):
                rows = jnp.where(sub == k, turned[i * 8 + k], rows)
            staged[pl.ds(pl.multiple_of((g * per + i) * 8, 8), 8), :] = rows
        return carry

    lax.fori_loop(0, groups, take, 0)
    out_ref[...] = staged[...].astype(BF16)


def backward_kernel(
    table_ref, delta_ref, lanes_ref, got_ref, image_ref,
    final_ref, left_ref, right_ref, top_ref, bottom_ref,
    rel, bands, shadows, staged, mirror, update, image, sems,
):
    slices = ROWS // 2
    coming = pltpu.make_async_copy(image_ref, image, sems.at[0])
    coming.start()
    pixel = lax.broadcasted_iota(jnp.int32, (PIX, BAND), 0)
    rel[...] = (
        (pixel // SIDE).astype(F32) * lanes_ref[0:1, :]
        + (pixel % SIDE).astype(F32) * lanes_ref[1:2, :]
    )
    staged[...] = got_ref[...].astype(F32)
    mirror[...] = jnp.dot(got_ref[...], reversal(), preferred_element_type=F32)
    for a in range(ANGLES):
        parts = []
        for ref in (staged, mirror):
            for t in range(2):
                row = (a // 2) * 4 + t * 2 + a % 2
                parts.append(ref[pl.ds(row, slices, stride=ROWS), :])
        shadows[a] = jnp.concatenate(parts + parts, axis=0).T

    def build(patch, band):
        shift = delta_ref[pl.ds(patch, 1), :]
        for r in range(0, PIX, 16):
            away = jnp.abs(rel[r : r + 16, :] + shift)
            rounded = (1.0 - away).astype(BF16)
            band[r : r + 16, :] = jnp.maximum(rounded, jnp.zeros_like(rounded))

    def spread(patch, band, half, col, own):
        pieces = []
        for a in range(ANGLES):
            start = pl.multiple_of(table_ref[patch, a].astype(jnp.int32), 8)
            pieces.append(shadows[a, pl.ds(start, BINS), :])
        seen = jnp.concatenate(pieces, axis=0).astype(BF16)
        got = jnp.dot(band[...], seen, preferred_element_type=F32)
        for u in range(SIDE):
            spot = pl.ds(pl.multiple_of(col * SIDE, SIDE), SIDE)
            piece = got[u * SIDE : (u + 1) * SIDE, :]
            if own:
                update[half * SIDE + u, spot, TILE // 2 :] = piece[:, TILE // 2 :]
            else:
                update[half * SIDE + u, spot, :] = piece

    pipeline(build, spread, bands)

    coming.wait()

    def finish(i, carry):
        image[i] = image[i] + 0.25 * reflected(update, i)
        return carry

    lax.fori_loop(0, SIDE, finish, 0, unroll=2)
    going = [
        pltpu.make_async_copy(
            image.at[pl.ds(h * SIDE, SIDE)], final_ref.at[pl.ds(h * SIDE, SIDE)], sems.at[h]
        )
        for h in range(2)
    ]
    going[0].start()
    lax.fori_loop(SIDE, 2 * SIDE, finish, 0, unroll=2)
    going[1].start()
    lane = lax.broadcasted_iota(jnp.int32, (8, TILE), 1)
    sub = lax.broadcasted_iota(jnp.int32, (8, TILE), 0)
    second = lane & slices != 0

    def column(u, start, far):
        value = [image[h * SIDE + u, start : start + 8, :] for h in range(2)]
        value[far] = pltpu.roll(value[far], 4, 0)
        return jnp.where(sub < 4, value[0], value[1])

    for u in range(8):
        here, there = column(u, 0, 1), column(u + 8, 0, 1)
        left_ref[u] = jnp.where(second, pltpu.roll(there, slices, 1), here)
        here, there = column(u, TILE - 8, 0), column(u + 8, TILE - 8, 0)
        right_ref[u] = jnp.where(second, here, pltpu.roll(there, TILE - slices, 1))
    lanes = lax.broadcasted_iota(jnp.int32, (TILE, TILE), 1) // ROWS
    for ref, row, shift in ((top_ref, 0, 0), (bottom_ref, SIDE - TV_STEPS, TILE - ROWS)):
        packed = jnp.zeros((TILE, TILE), F32)
        for k in range(TV_STEPS):
            turned = pltpu.roll(image[row + k], (k * ROWS + shift) % TILE, 1)
            packed = jnp.where(lanes == k, turned, packed)
        ref[...] = packed.reshape(TILE // 8, 8, TILE)
    for copy in going:
        copy.wait()


def smooth_kernel(half, place_ref, before_ref, after_ref, *refs):
    if half == 0:
        above_ref, below_ref, x_ref, unused, out_ref = refs[:5]
    else:
        x_ref, out_ref = refs[:2]
    first, second, other, flow, out0, out1, sems = refs[-7:]
    slices = ROWS // 2
    own = pl.ds(16, TILE)
    wide = TILE + 16
    last_rows = SIDE - TV_STEPS
    coming = [
        pltpu.make_async_copy(
            x_ref.at[pl.ds(start, count)], ref.at[pl.ds(row, count), own, :], sems.at[i]
        )
        for i, (start, count, ref, row) in enumerate(
            (
                (half * SIDE, SIDE, first, TV_STEPS),
                ((1 - half) * SIDE, TV_STEPS, other, 0),
                ((1 - half) * SIDE + last_rows, TV_STEPS, other, TV_STEPS),
            )
        )
    ]
    for copy in coming:
        copy.start()
    lane = lax.broadcasted_iota(jnp.int32, (8, TILE), 1)
    later = lane & slices != 0
    has_above, has_below, has_before, has_after = (place_ref[i] for i in range(4))

    def roll(value, shift):
        return pltpu.roll(value, shift % TILE, 1)

    def sink(value):
        return pltpu.roll(value, 4, 0)

    if half == 0:
        for ref, row, shift, left, right in (
            (above_ref, 0, 0, -ROWS, -ROWS),
            (below_ref, SIDE + TV_STEPS, ROWS, slices, ROWS + slices),
        ):
            for k in range(TV_STEPS):
                back = shift - k * ROWS
                lead = jnp.where(
                    later,
                    roll(ref[TILE // 8 - 1], back + slices),
                    sink(roll(ref[TILE // 8 + k], left)),
                )
                trail = jnp.where(
                    later,
                    roll(ref[TILE // 8 + TV_STEPS + k], right),
                    roll(ref[0], back - slices),
                )
                first[row + k, 8:16, :] = lead
                for g in range(TILE // 8):
                    first[row + k, 16 + 8 * g : 24 + 8 * g, :] = roll(ref[g], back)
                first[row + k, 16 + TILE : 24 + TILE, :] = trail
    for copy in coming:
        copy.wait()
    sides = [(first, u + TV_STEPS, u, half) for u in range(SIDE)]
    sides += [(other, k, k, 1 - half) for k in range(TV_STEPS)]
    sides += [(other, TV_STEPS + k, last_rows + k, 1 - half) for k in range(TV_STEPS)]
    for ref, row, u, h in sides:
        before = before_ref[u % 8]
        after = after_ref[u % 8]
        if u < 8:
            before, after = roll(before, -slices), roll(after, slices)
        if h:
            after = sink(after)
        else:
            before = sink(before)
        lead = jnp.where(later, roll(ref[row, 8 + TILE : 16 + TILE, :], slices), before)
        trail = jnp.where(later, after, roll(ref[row, 16:24, :], -slices))
        ref[row, 8:16, :] = lead
        ref[row, 16 + TILE : 24 + TILE, :] = trail

    group = lax.broadcasted_iota(jnp.int32, (wide, TILE), 1) // ROWS
    span = pl.ds(8, wide)
    for k in range(TV_STEPS):
        for mine, others, target, low in (
            (SIDE + k, TV_STEPS + k, k, True),
            (TV_STEPS + k, k, SIDE + TV_STEPS + k, False),
        ):
            mine = first[mine, span, :]
            others = other[others, span, :]
            if half == 0:
                value = roll(jnp.where(group == (1 if low else 0), others, mine), 2 * ROWS)
                outer = group == (0 if low else 1)
                value = jnp.where(outer, first[target, span, :], value)
            else:
                value = roll(jnp.where(group == (2 if low else 3), others, mine), 2 * ROWS)
                step = roll(mine, ROWS if low else -ROWS)
                value = jnp.where(group == (3 if low else 2), step, value)
            first[target, span, :] = value

    keep_lead = later | (has_before == 1)
    keep_trail = jnp.logical_not(later) | (has_after == 1)

    def flows(source, r):
        here = source[r, span, :]
        down = source[r + 1, span, :] - here
        right = source[r, pl.ds(9, wide), :] - here
        inverse = lax.rsqrt(smoothing * smoothing + down * down + right * right)
        return here, down * inverse, right * inverse

    for k in range(TV_STEPS):
        source, target = (first, second) if k % 2 == 0 else (second, first)
        last = k == TV_STEPS - 1

        def row(r, came, slot, inside=None, source=source, target=target, last=last):
            here, down, right = flows(source, r)
            flow[slot, span, :] = right
            left = flow[slot, pl.ds(7, wide), :]
            fresh = here - descent_step * (came - down + left - right)
            if last:
                turned = fresh[8 : 8 + TILE, :].T
                for g, block in enumerate(blocks_at(half)):
                    spot = pl.ds(block * SIDE + r - TV_STEPS, slices, stride=TILE)
                    for t, ref in enumerate((out0, out1)):
                        start = g * ROWS + t * slices
                        ref[spot, :] = turned[start : start + slices, :]
                return down
            if inside is not None:
                fresh = jnp.where(inside, fresh, 0.0)
            target[r, 8:16, :] = jnp.where(keep_lead, fresh[:8, :], 0.0)
            target[r, own, :] = fresh[8 : 8 + TILE, :]
            target[r, 16 + TILE : 24 + TILE, :] = jnp.where(keep_trail, fresh[wide - 8 :, :], 0.0)
            return down

        unused, came, unused = flows(source, k)
        for r in range(k + 1, TV_STEPS):
            came = row(r, came, r % 2, None if half else (group != 0) | (has_above == 1))

        def some(i, came, row=row):
            for j in range(STRIDE):
                came = row(TV_STEPS + STRIDE * i + j, came, j % 2)
            return came

        if not last:
            came = lax.fori_loop(0, SIDE // STRIDE, some, came)
        for r in range(SIDE + TV_STEPS, SIDE + 2 * TV_STEPS - 1 - k):
            came = row(r, came, r % 2, None if half else (group != 1) | (has_below == 1))
    going = []
    for part in range(2):
        came = lax.fori_loop(
            part * SIDE // 2 // STRIDE, (part + 1) * SIDE // 2 // STRIDE, some, came
        )
        for block in blocks_at(half):
            spot = pl.ds(block * SIDE + part * 8, 8)
            for t, ref in enumerate((out0, out1)):
                going.append(
                    pltpu.make_async_copy(
                        ref.reshape(slices, TILE, TILE).at[:, spot, :],
                        out_ref.at[:, spot, pl.ds(t * TILE, TILE)],
                        sems.at[len(going)],
                    )
                )
                going[-1].start()
    for copy in going:
        copy.wait()


def call(
    kernel, scalars, arrays, left, outs, scratch, flops, aliases=None, tight=True
):
    vmem = pl.BlockSpec(memory_space=VMEM)
    smem = pl.BlockSpec(memory_space=pltpu.SMEM)
    operands = (*scalars, *arrays, *left)
    bytes_of = lambda x: math.prod(x.shape) * x.dtype.itemsize
    stays = lambda x: bytes_of(x) > 1 << 20
    held = sum(bytes_of(x) for x in arrays)
    held += sum(bytes_of(x) for x in jax.tree.leaves(outs) if not stays(x))
    held += sum(bytes_of(x) for x in scratch if getattr(x, "memory_space", None) == VMEM)
    return pl.pallas_call(
        kernel,
        out_shape=outs,
        in_specs=[smem] * len(scalars)
        + [vmem] * len(arrays)
        + [pl.BlockSpec(memory_space=pl.ANY)] * len(left),
        out_specs=jax.tree.map(
            lambda x: pl.BlockSpec(memory_space=pl.ANY) if stays(x) else vmem, outs
        ),
        scratch_shapes=scratch,
        input_output_aliases=aliases or {},
        compiler_params=pltpu.CompilerParams(vmem_limit_bytes=held + (6 << 20) if tight else None),
        cost_estimate=pl.CostEstimate(
            flops=flops, bytes_accessed=sum(map(bytes_of, operands)), transcendentals=0
        ),
    )(*operands)


def local(current_image, measured, ray_weight, angle_ids, shadow_start):
    row_index = lax.axis_index("row")
    col_index = lax.axis_index("col")
    rows = lax.axis_size("row")
    cols = lax.axis_size("col")
    slices = current_image.shape[0]
    both = ("row", "col")
    half = VMEM((slices * TILE, TILE), F32)

    turned = jax.ShapeDtypeStruct((2 * SIDE, TILE, TILE), F32)
    sent, image, table = call(
        forward_kernel,
        (col_index.reshape(1), angle_ids),
        (),
        (current_image, measured[:, 0], ray_weight[:, 0]),
        (jax.ShapeDtypeStruct((rows * cols * MESSAGE, TILE), BF16), turned, jax.ShapeDtypeStruct((TABLE, TILE), F32)),
        [
            pltpu.SMEM((TABLE, TILE), F32),
            VMEM((2 * SIDE * TILE, TILE), BF16),
            VMEM((BAND, PIX), F32),
            VMEM((4 * PHASE, BAND, PIX), BF16),
            VMEM((ANGLES * TILE, TILE), F32),
            VMEM((rows * cols * MESSAGE, TILE), F32),
            half,
            half,
            VMEM(turned.shape, F32),
            VMEM(measured[:, 0].shape, F32),
            VMEM(ray_weight[:, 0].shape, F32),
            pltpu.SemaphoreType.DMA((11,)),
        ]
        + [VMEM((TILE, TILE), F32)] * ANGLES,
        30_000_000_000,
        tight=False,
    )
    got = lax.all_to_all(
        sent.reshape(rows * cols, MESSAGE, TILE), both, split_axis=0, concat_axis=0, tiled=True
    )
    blocks = rows
    starts = shadow_start.reshape(-1, ANGLES)
    starts = lax.dynamic_slice_in_dim(starts, col_index * 2, 2, 1).reshape(-1)
    out = call(
        owner_kernel,
        (starts, col_index.reshape(1)),
        (got.reshape(-1, TILE),),
        (),
        jax.ShapeDtypeStruct((rows * cols * 4, TILE), BF16),
        [
            VMEM((2 * blocks, 3 * TILE), F32),
            VMEM((2, blocks + 1, 8, TILE), F32),
            VMEM((rows * cols * 4, TILE), F32),
            VMEM((3 * TILE, TILE), F32),
            VMEM((rows * cols * MESSAGE, TILE), F32),
        ]
        + [VMEM((blocks, 2, 8, TILE), F32)] * 8,
        10_000_000_000,
    )
    shadows = lax.all_to_all(
        out.reshape(rows * cols, 4, TILE), both, split_axis=0, concat_axis=0, tiled=True
    )
    table = table[: 2 * PAIRS + 2, :ANGLES]
    bins = jnp.arange(BINS, dtype=F32)
    delta_lanes = (table[PAIRS : 2 * PAIRS, :, None] - bins).reshape(-1, BAND)
    angle_lanes = jnp.repeat(table[2 * PAIRS :], BINS, axis=1)
    side = jax.ShapeDtypeStruct((8, 8, TILE), F32)
    edge = jax.ShapeDtypeStruct((TILE // 8, 8, TILE), F32)
    x, left, right, top, bottom = call(
        backward_kernel,
        (table[:PAIRS],),
        (delta_lanes, angle_lanes, shadows.reshape(-1, TILE)),
        (image,),
        (turned, side, side, edge, edge),
        [
            VMEM((PIX, BAND), F32),
            VMEM((4 * PHASE, PIX, BAND), BF16),
            VMEM((ANGLES, TILE, TILE), F32),
            VMEM((rows * cols * 4, TILE), F32),
            VMEM((rows * cols * 4, TILE), F32),
            VMEM(turned.shape, F32),
            VMEM(turned.shape, F32),
            pltpu.SemaphoreType.DMA((2,)),
        ],
        30_000_000_000,
    )
    before = lax.ppermute(right, "col", [(i, i + 1) for i in range(cols - 1)])
    after = lax.ppermute(left, "col", [(i + 1, i) for i in range(cols - 1)])
    upward = jnp.concatenate([top, before[:TV_STEPS], after[:TV_STEPS]], axis=0)
    downward = jnp.concatenate([bottom, before[TV_STEPS:], after[TV_STEPS:]], axis=0)
    above = lax.ppermute(downward, "row", [(i, i + 1) for i in range(rows - 1)])
    below = lax.ppermute(upward, "row", [(i + 1, i) for i in range(rows - 1)])
    place = jnp.stack(
        [row_index > 0, row_index < rows - 1, col_index > 0, col_index < cols - 1]
    ).astype(jnp.int32)
    wide = VMEM((SIDE + 2 * TV_STEPS, TILE + 32, TILE), F32)
    few = VMEM((2 * TV_STEPS, TILE + 32, TILE), F32)
    scratch = [wide, wide, few, VMEM((2, TILE + 32, TILE), F32), half, half]
    scratch.append(pltpu.SemaphoreType.DMA((16,)))
    final = jax.ShapeDtypeStruct(current_image.shape, F32)
    smooth = call(
        functools.partial(smooth_kernel, 1),
        (place,),
        (before, after),
        (x,),
        final,
        scratch,
        10_000_000_000,
    )
    return call(
        functools.partial(smooth_kernel, 0),
        (place,),
        (before, after, above, below),
        (x, smooth),
        final,
        scratch,
        10_000_000_000,
        {6: 0},
    )


def solution(mesh):
    return jax.shard_map(
        local,
        mesh=mesh,
        in_specs=(
            P(None, "row", "col"),
            P("col", "row", None, None),
            P("col", "row", None),
            P(),
            P(),
        ),
        out_specs=P(None, "row", "col"),
        check_vma=False,
    )
```

```python
import functools
import math

import jax
import jax.numpy as jnp
from jax import lax
from jax.experimental import pallas as pl
from jax.experimental.pallas import tpu as pltpu
from jax.sharding import PartitionSpec as P

TILE = 128
ANGLES = 16
ALL_ANGLES = 256
TV_STEPS = 4
SIDE = 16
PATCHES = TILE // SIDE
PIX = SIDE * SIDE
BINS = 24
ROWS = 32
BAND = ANGLES * BINS
PAIRS = PATCHES * PATCHES // 2
PHASE = 4
STRIDE = 8
TABLE = 2 * PAIRS + 8
MESSAGE = 8

inverse_root = 0.7071067811865476
smoothing = 0.25
descent_step = 0.05

VMEM = pltpu.VMEM
F32 = jnp.float32
BF16 = jnp.bfloat16


def geometry(angle_ids):
    radians = angle_ids.astype(F32) * (math.pi / ALL_ANGLES)
    cosine = jnp.cos(radians) * inverse_root
    sine = jnp.sin(radians) * inverse_root
    row = lax.broadcasted_iota(jnp.int32, (TABLE, TILE), 0)
    patch = row & (PAIRS - 1)
    down = (patch >> 3).astype(F32) * SIDE - (TILE - 1) / 2.0
    across = (patch & (PATCHES - 1)).astype(F32) * SIDE - (TILE - 1) / 2.0
    corner = TILE / 2.0 + down * cosine + across * sine
    low = corner + (SIDE - 1) * (jnp.minimum(cosine, 0.0) + jnp.minimum(sine, 0.0))
    base = jnp.clip(jnp.floor((jnp.floor(low - 1.5) + 1.0) / 8.0) * 8.0, 0.0, TILE - BINS)
    delta = corner - base - 0.5
    ends = jnp.where(row == 2 * PAIRS, cosine, sine)
    return jnp.where(row < PAIRS, base, jnp.where(row < 2 * PAIRS, delta, ends))


def reversal():
    there = lax.broadcasted_iota(jnp.int32, (TILE, TILE), 0)
    here = lax.broadcasted_iota(jnp.int32, (TILE, TILE), 1)
    return jnp.where(there + here == TILE - 1, 1.0, 0.0).astype(BF16)


def reverse_lanes(value):
    high = value.astype(BF16)
    low = (value - high.astype(F32)).astype(BF16)
    both = jnp.concatenate([high, low], axis=1)
    turn = reversal()
    return jnp.dot(both, jnp.concatenate([turn, turn], axis=0), preferred_element_type=F32)


def pipeline(build, use, bands):
    def phase(i, action, slot):
        for j in range(PHASE):
            at = i * PHASE + j
            half = at // PATCHES
            col = at % PATCHES
            for own in range(2):
                patch = (2 * half + own) * PATCHES + col
                band = bands.at[(slot * PHASE + j) * 2 + own]
                if action is build:
                    build(patch, band)
                else:
                    use(patch, band, half, col, own)

    phase(0, build, 0)
    phases = 2 * PATCHES // PHASE

    def step(i, carry):
        phase(2 * i + 1, build, 1)
        phase(2 * i, use, 0)
        phase(jnp.minimum(2 * i + 2, phases - 1), build, 0)
        phase(2 * i + 1, use, 1)
        return carry

    lax.fori_loop(0, phases // 2, step, 0)


def blocks_at(half):
    return 2 * half, PATCHES - 1 - 2 * half, 2 * half + 1, PATCHES - 2 - 2 * half


def reflected(ref, i):
    other = (i // SIDE) * SIDE + SIDE - 1 - i % SIDE
    back = 7 - lax.broadcasted_iota(jnp.int32, (8, TILE), 0)
    mirrored = lax.broadcasted_iota(jnp.int32, (8, TILE), 1) & ROWS != 0
    parts = []
    for g in range(TILE // 8):
        far = ref[other, TILE - 8 * (g + 1) : TILE - 8 * g, :]
        far = jnp.take_along_axis(far, back, axis=0)
        parts.append(jnp.where(mirrored, far, ref[i, 8 * g : 8 * (g + 1), :]))
    return jnp.concatenate(parts, axis=0)


def forward_kernel(
    own_ref, angles_ref, image_ref, given_ref, given_weight_ref,
    out_ref, turned_ref, geometry_ref, table_ref, xt, rel, bands, tails, message, image0_ref,
    image1_ref, flat,
    measured_ref, weight_ref, sems, *sums,
):
    slices = ROWS // 2
    coming = [[], []]
    for part, start in ((0, 0), (0, 6), (1, 2), (1, 4)):
        spot = pl.ds(start * SIDE, 2 * SIDE)
        for t, ref in enumerate((image0_ref, image1_ref)):
            coming[part].append(
                pltpu.make_async_copy(
                    image_ref.at[:, spot, pl.ds(t * TILE, TILE)],
                    ref.reshape(slices, TILE, TILE).at[:, spot, :],
                    sems.at[2 + start + t],
                )
            )
    small = [
        pltpu.make_async_copy(given_ref, measured_ref, sems.at[0]),
        pltpu.make_async_copy(given_weight_ref, weight_ref, sems.at[1]),
    ]
    for copy in (*coming[0], *coming[1], *small):
        copy.start()
    place = lax.broadcasted_iota(jnp.int32, (1, TILE), 1)
    angles = jnp.zeros((1, TILE), jnp.int32)
    for a in range(ANGLES):
        angles = jnp.where(place == a, angles_ref[a], angles)
    geometry_ref[...] = geometry(angles)
    table = pltpu.make_async_copy(geometry_ref, table_ref, sems.at[10])
    table.start()
    for ref in sums:
        ref[...] = jnp.zeros_like(ref)
    def rows_of(u):
        return [ref[pl.ds(u, slices, stride=TILE), :] for ref in (image0_ref, image1_ref)]

    def flip(i, carry):
        rows = []
        for block in blocks_at(i // SIDE):
            rows += rows_of(block * SIDE + i % SIDE)
        flat[i] = jnp.concatenate(rows, axis=0).T
        return carry

    for part in range(2):
        for copy in coming[part]:
            copy.wait()
        lax.fori_loop(part * SIDE, (part + 1) * SIDE, flip, 0, unroll=16)
    for copy in small:
        copy.wait()
    going = pltpu.make_async_copy(flat, turned_ref, sems.at[0])
    going.start()

    def reflect(i, carry):
        value = reflected(flat, i)
        xt[pl.ds(pl.multiple_of(i * TILE, TILE), TILE), :] = value.astype(BF16)
        return carry

    lax.fori_loop(0, 2 * SIDE, reflect, 0, unroll=2)

    table.wait()
    lane = lax.broadcasted_iota(jnp.int32, (BINS, PIX), 1)
    bin_at = lax.broadcasted_iota(jnp.int32, (BINS, PIX), 0).astype(F32)
    down = (lane // SIDE).astype(F32)
    across = (lane % SIDE).astype(F32)
    for a in range(ANGLES):
        rel[a * BINS : (a + 1) * BINS, :] = (
            down * table_ref[2 * PAIRS, a] + across * table_ref[2 * PAIRS + 1, a] - bin_at
        )

    def build(patch, band):
        for a in range(0, ANGLES, 2):
            pair = []
            for b in (a, a + 1):
                away = jnp.abs(rel[b * BINS : (b + 1) * BINS, :] + table_ref[PAIRS + patch, b])
                pair.append(1.0 - away)
            rounded = jnp.concatenate(pair, axis=0).astype(BF16)
            band[a * BINS : (a + 2) * BINS, :] = jnp.maximum(rounded, jnp.zeros_like(rounded))

    first_half = lax.broadcasted_iota(jnp.int32, (PIX, TILE), 1) < TILE // 2

    def project(patch, band, half, col, own):
        pieces = []
        for u in range(SIDE):
            start = pl.multiple_of((half * SIDE + u) * TILE + col * SIDE, SIDE)
            pieces.append(xt[pl.ds(start, SIDE), :])
        pixels = jnp.concatenate(pieces, axis=0)
        nothing = jnp.zeros_like(pixels)
        pixels = jnp.where(first_half, *((nothing, pixels) if own else (pixels, nothing)))
        got = jnp.dot(band[...], pixels, preferred_element_type=F32)
        for a in range(ANGLES):
            start = pl.multiple_of(table_ref[patch, a].astype(jnp.int32), 8)
            sums[a][pl.ds(start, BINS), :] += got[a * BINS : (a + 1) * BINS, :]

    pipeline(build, project, bands)
    stride = MESSAGE * ANGLES // 2
    for a in range(ANGLES):
        tails[a * TILE : (a + 1) * TILE, :] = sums[a][...].T * 0.03125
    mirrored = [
        tails[a * TILE + ROWS : a * TILE + 2 * ROWS, :]
        + tails[a * TILE + 3 * ROWS : (a + 1) * TILE, :]
        for a in range(ANGLES)
    ]
    mirrored = reverse_lanes(jnp.concatenate(mirrored, axis=0))
    for a in range(ANGLES):
        total = tails[a * TILE : a * TILE + ROWS, :] + tails[a * TILE + 2 * ROWS : a * TILE + 3 * ROWS, :]
        total = total + mirrored[a * ROWS : (a + 1) * ROWS, :]
        for t in range(2):
            row = (a // 2) * MESSAGE + t * 2 + a % 2
            message[pl.ds(row, slices, stride=stride), :] = total[t * slices : (t + 1) * slices, :]
    row = own_ref[0] * MESSAGE + 4
    for h in range(2):
        message[pl.ds(row + h, slices, stride=stride), :] = measured_ref[h]
        weight = jnp.broadcast_to(weight_ref[h : h + 1, :], (slices, TILE))
        message[pl.ds(row + 2 + h, slices, stride=stride), :] = weight
    out_ref[...] = message[...].astype(BF16)
    going.wait()


def owner_kernel(
    starts_ref, own_ref, sent_ref, out_ref, wide, filt, staged, ramp_ref, got_ref, *sums
):
    blocks = 16
    per = 8
    groups = staged.shape[0] // (8 * per)
    for ref in sums:
        ref[...] = jnp.zeros_like(ref)
    lane = lax.broadcasted_iota(jnp.int32, (8, TILE), 1)
    sub = lax.broadcasted_iota(jnp.int32, (8, TILE), 0)

    offset = (
        lax.broadcasted_iota(jnp.int32, (3 * TILE, TILE), 1)
        + TILE
        - lax.broadcasted_iota(jnp.int32, (3 * TILE, TILE), 0)
    )
    nonzero = jnp.where(offset == 0, 1, offset).astype(F32)
    ramp = jnp.where((offset & 1) == 1, -1.0 / (math.pi * math.pi * nonzero * nonzero), 0.0)
    ramp = jnp.where(offset == 0, 0.25, ramp)
    ramp = jnp.where(jnp.abs(offset) < TILE, ramp, 0.0)
    ramp_ref[...] = ramp
    got_ref[...] = sent_ref[...].astype(F32)

    def add(g, carry):
        turned = []
        for i in range(2 * per):
            source = g * 2 * per + i
            rows = got_ref[pl.ds(pl.multiple_of(source * MESSAGE, MESSAGE), MESSAGE), :]
            for k in range(4):
                start = starts_ref[source * 4 + k]
                turned.append((start >> 7, start & (TILE - 1), rows, i % 2 * 4 + k, k))
        turned = [
            (block, shift, pltpu.roll(rows, shift, 1), slot) for block, shift, rows, slot, k in turned
        ]
        for block, shift, value, slot in turned:
            tail = jnp.where(lane >= shift, value, 0.0)
            sums[slot][block, 0] += tail
            sums[slot][block, 1] += value - tail
        return carry

    lax.fori_loop(0, groups, add, 0)
    wide[...] = jnp.zeros_like(wide)
    for b in range(blocks):
        total = jnp.zeros((8, TILE), F32)
        for slot in range(8):
            here = sums[slot][b, 0]
            if b:
                here = here + sums[slot][b - 1, 1]
            total = total + jnp.where(sub == slot % 4, here, 0.0)
        home = pl.multiple_of((b * 8 + own_ref[0]) * MESSAGE, MESSAGE)
        given = got_ref[pl.ds(home, MESSAGE), :]
        for h in range(2):
            row = total[h : h + 1, :] + total[2 + h : 3 + h, :]
            wide[h * blocks + b : h * blocks + b + 1, TILE : 2 * TILE] = given[6 + h : 7 + h, :] * (
                given[4 + h : 5 + h, :] - row
            )
    centre = wide[:, TILE : 2 * TILE]
    at = lax.broadcasted_iota(jnp.int32, (2 * blocks, TILE), 0) % blocks
    wide[:, :TILE] = jnp.where(at == 0, 0.0, pltpu.roll(centre, 1, 0))
    wide[:, 2 * TILE :] = jnp.where(at == blocks - 1, 0.0, pltpu.roll(centre, 2 * blocks - 1, 0))
    done = jnp.dot(wide[...], ramp_ref[...], precision=lax.Precision.HIGHEST, preferred_element_type=F32)
    wide[:, :TILE] = done.astype(BF16).astype(F32)
    filt[...] = jnp.zeros_like(filt)
    for h in range(2):
        for b in range(blocks):
            row = wide[h * blocks + b : h * blocks + b + 1, :TILE]
            filt[h, b] = jnp.broadcast_to(row, (8, TILE))

    def take(g, carry):
        mixed = []
        for i in range(per):
            for k in range(8):
                start = starts_ref[(g * per + i) * 8 + k]
                block, shift = start >> 7, start & (TILE - 1)
                value = jnp.where(lane >= shift, filt[k % 2, block], filt[k % 2, block + 1])
                mixed.append((value, (TILE - shift) & (TILE - 1)))
        turned = [pltpu.roll(value, shift, 1) for value, shift in mixed]
        for i in range(per):
            rows = turned[i * 8]
            for k in range(1, 8):
                rows = jnp.where(sub == k, turned[i * 8 + k], rows)
            staged[pl.ds(pl.multiple_of((g * per + i) * 8, 8), 8), :] = rows
        return carry

    lax.fori_loop(0, groups, take, 0)
    out_ref[...] = staged[...].astype(BF16)


def backward_kernel(
    table_ref, delta_ref, lanes_ref, got_ref, image_ref,
    final_ref, left_ref, right_ref, top_ref, bottom_ref,
    rel, bands, shadows, staged, mirror, update, image, sems,
):
    slices = ROWS // 2
    coming = pltpu.make_async_copy(image_ref, image, sems.at[0])
    coming.start()
    pixel = lax.broadcasted_iota(jnp.int32, (PIX, BAND), 0)
    rel[...] = (
        (pixel // SIDE).astype(F32) * lanes_ref[0:1, :]
        + (pixel % SIDE).astype(F32) * lanes_ref[1:2, :]
    )
    staged[...] = got_ref[...].astype(F32)
    mirror[...] = jnp.dot(got_ref[...], reversal(), preferred_element_type=F32)
    for a in range(ANGLES):
        parts = []
        for ref in (staged, mirror):
            for t in range(2):
                row = (a // 2) * 4 + t * 2 + a % 2
                parts.append(ref[pl.ds(row, slices, stride=ROWS), :])
        shadows[a] = jnp.concatenate(parts + parts, axis=0).T

    def build(patch, band):
        shift = delta_ref[pl.ds(patch, 1), :]
        for r in range(0, PIX, 16):
            away = jnp.abs(rel[r : r + 16, :] + shift)
            rounded = (1.0 - away).astype(BF16)
            band[r : r + 16, :] = jnp.maximum(rounded, jnp.zeros_like(rounded))

    def spread(patch, band, half, col, own):
        pieces = []
        for a in range(ANGLES):
            start = pl.multiple_of(table_ref[patch, a].astype(jnp.int32), 8)
            pieces.append(shadows[a, pl.ds(start, BINS), :])
        seen = jnp.concatenate(pieces, axis=0).astype(BF16)
        got = jnp.dot(band[...], seen, preferred_element_type=F32)
        for u in range(SIDE):
            spot = pl.ds(pl.multiple_of(col * SIDE, SIDE), SIDE)
            piece = got[u * SIDE : (u + 1) * SIDE, :]
            if own:
                update[half * SIDE + u, spot, TILE // 2 :] = piece[:, TILE // 2 :]
            else:
                update[half * SIDE + u, spot, :] = piece

    pipeline(build, spread, bands)

    coming.wait()

    def finish(i, carry):
        image[i] = image[i] + 0.25 * reflected(update, i)
        return carry

    lax.fori_loop(0, SIDE, finish, 0, unroll=2)
    going = [
        pltpu.make_async_copy(
            image.at[pl.ds(h * SIDE, SIDE)], final_ref.at[pl.ds(h * SIDE, SIDE)], sems.at[h]
        )
        for h in range(2)
    ]
    going[0].start()
    lax.fori_loop(SIDE, 2 * SIDE, finish, 0, unroll=2)
    going[1].start()
    lane = lax.broadcasted_iota(jnp.int32, (8, TILE), 1)
    sub = lax.broadcasted_iota(jnp.int32, (8, TILE), 0)
    second = lane & slices != 0

    def column(u, start, far):
        value = [image[h * SIDE + u, start : start + 8, :] for h in range(2)]
        value[far] = pltpu.roll(value[far], 4, 0)
        return jnp.where(sub < 4, value[0], value[1])

    for u in range(8):
        here, there = column(u, 0, 1), column(u + 8, 0, 1)
        left_ref[u] = jnp.where(second, pltpu.roll(there, slices, 1), here)
        here, there = column(u, TILE - 8, 0), column(u + 8, TILE - 8, 0)
        right_ref[u] = jnp.where(second, here, pltpu.roll(there, TILE - slices, 1))
    lanes = lax.broadcasted_iota(jnp.int32, (TILE, TILE), 1) // ROWS
    for ref, row, shift in ((top_ref, 0, 0), (bottom_ref, SIDE - TV_STEPS, TILE - ROWS)):
        packed = jnp.zeros((TILE, TILE), F32)
        for k in range(TV_STEPS):
            turned = pltpu.roll(image[row + k], (k * ROWS + shift) % TILE, 1)
            packed = jnp.where(lanes == k, turned, packed)
        ref[...] = packed.reshape(TILE // 8, 8, TILE)
    for copy in going:
        copy.wait()


def smooth_kernel(half, place_ref, before_ref, after_ref, *refs):
    if half == 0:
        above_ref, below_ref, x_ref, unused, out_ref = refs[:5]
    else:
        x_ref, out_ref = refs[:2]
    first, second, other, flow, out0, out1, sems = refs[-7:]
    slices = ROWS // 2
    own = pl.ds(16, TILE)
    wide = TILE + 16
    last_rows = SIDE - TV_STEPS
    coming = [
        pltpu.make_async_copy(
            x_ref.at[pl.ds(start, count)], ref.at[pl.ds(row, count), own, :], sems.at[i]
        )
        for i, (start, count, ref, row) in enumerate(
            (
                (half * SIDE, SIDE, first, TV_STEPS),
                ((1 - half) * SIDE, TV_STEPS, other, 0),
                ((1 - half) * SIDE + last_rows, TV_STEPS, other, TV_STEPS),
            )
        )
    ]
    for copy in coming:
        copy.start()
    lane = lax.broadcasted_iota(jnp.int32, (8, TILE), 1)
    later = lane & slices != 0
    has_above, has_below, has_before, has_after = (place_ref[i] for i in range(4))

    def roll(value, shift):
        return pltpu.roll(value, shift % TILE, 1)

    def sink(value):
        return pltpu.roll(value, 4, 0)

    if half == 0:
        for ref, row, shift, left, right in (
            (above_ref, 0, 0, -ROWS, -ROWS),
            (below_ref, SIDE + TV_STEPS, ROWS, slices, ROWS + slices),
        ):
            for k in range(TV_STEPS):
                back = shift - k * ROWS
                lead = jnp.where(
                    later,
                    roll(ref[TILE // 8 - 1], back + slices),
                    sink(roll(ref[TILE // 8 + k], left)),
                )
                trail = jnp.where(
                    later,
                    roll(ref[TILE // 8 + TV_STEPS + k], right),
                    roll(ref[0], back - slices),
                )
                first[row + k, 8:16, :] = lead
                for g in range(TILE // 8):
                    first[row + k, 16 + 8 * g : 24 + 8 * g, :] = roll(ref[g], back)
                first[row + k, 16 + TILE : 24 + TILE, :] = trail
    for copy in coming:
        copy.wait()
    sides = [(first, u + TV_STEPS, u, half) for u in range(SIDE)]
    sides += [(other, k, k, 1 - half) for k in range(TV_STEPS)]
    sides += [(other, TV_STEPS + k, last_rows + k, 1 - half) for k in range(TV_STEPS)]
    for ref, row, u, h in sides:
        before = before_ref[u % 8]
        after = after_ref[u % 8]
        if u < 8:
            before, after = roll(before, -slices), roll(after, slices)
        if h:
            after = sink(after)
        else:
            before = sink(before)
        lead = jnp.where(later, roll(ref[row, 8 + TILE : 16 + TILE, :], slices), before)
        trail = jnp.where(later, after, roll(ref[row, 16:24, :], -slices))
        ref[row, 8:16, :] = lead
        ref[row, 16 + TILE : 24 + TILE, :] = trail

    group = lax.broadcasted_iota(jnp.int32, (wide, TILE), 1) // ROWS
    span = pl.ds(8, wide)
    for k in range(TV_STEPS):
        for mine, others, target, low in (
            (SIDE + k, TV_STEPS + k, k, True),
            (TV_STEPS + k, k, SIDE + TV_STEPS + k, False),
        ):
            mine = first[mine, span, :]
            others = other[others, span, :]
            if half == 0:
                value = roll(jnp.where(group == (1 if low else 0), others, mine), 2 * ROWS)
                outer = group == (0 if low else 1)
                value = jnp.where(outer, first[target, span, :], value)
            else:
                value = roll(jnp.where(group == (2 if low else 3), others, mine), 2 * ROWS)
                step = roll(mine, ROWS if low else -ROWS)
                value = jnp.where(group == (3 if low else 2), step, value)
            first[target, span, :] = value

    keep_lead = later | (has_before == 1)
    keep_trail = jnp.logical_not(later) | (has_after == 1)

    def flows(source, r):
        here = source[r, span, :]
        down = source[r + 1, span, :] - here
        right = source[r, pl.ds(9, wide), :] - here
        inverse = lax.rsqrt(smoothing * smoothing + down * down + right * right)
        return here, down * inverse, right * inverse

    for k in range(TV_STEPS):
        source, target = (first, second) if k % 2 == 0 else (second, first)
        last = k == TV_STEPS - 1

        def row(r, came, slot, inside=None, source=source, target=target, last=last):
            here, down, right = flows(source, r)
            flow[slot, span, :] = right
            left = flow[slot, pl.ds(7, wide), :]
            fresh = here - descent_step * (came - down + left - right)
            if last:
                turned = fresh[8 : 8 + TILE, :].T
                for g, block in enumerate(blocks_at(half)):
                    spot = pl.ds(block * SIDE + r - TV_STEPS, slices, stride=TILE)
                    for t, ref in enumerate((out0, out1)):
                        start = g * ROWS + t * slices
                        ref[spot, :] = turned[start : start + slices, :]
                return down
            if inside is not None:
                fresh = jnp.where(inside, fresh, 0.0)
            target[r, 8:16, :] = jnp.where(keep_lead, fresh[:8, :], 0.0)
            target[r, own, :] = fresh[8 : 8 + TILE, :]
            target[r, 16 + TILE : 24 + TILE, :] = jnp.where(keep_trail, fresh[wide - 8 :, :], 0.0)
            return down

        unused, came, unused = flows(source, k)
        for r in range(k + 1, TV_STEPS):
            came = row(r, came, r % 2, None if half else (group != 0) | (has_above == 1))

        def some(i, came, row=row):
            for j in range(STRIDE):
                came = row(TV_STEPS + STRIDE * i + j, came, j % 2)
            return came

        if not last:
            came = lax.fori_loop(0, SIDE // STRIDE, some, came)
        for r in range(SIDE + TV_STEPS, SIDE + 2 * TV_STEPS - 1 - k):
            came = row(r, came, r % 2, None if half else (group != 1) | (has_below == 1))
    going = []
    for part in range(2):
        came = lax.fori_loop(
            part * SIDE // 2 // STRIDE, (part + 1) * SIDE // 2 // STRIDE, some, came
        )
        for block in blocks_at(half):
            spot = pl.ds(block * SIDE + part * 8, 8)
            for t, ref in enumerate((out0, out1)):
                going.append(
                    pltpu.make_async_copy(
                        ref.reshape(slices, TILE, TILE).at[:, spot, :],
                        out_ref.at[:, spot, pl.ds(t * TILE, TILE)],
                        sems.at[len(going)],
                    )
                )
                going[-1].start()
    for copy in going:
        copy.wait()


def call(
    kernel, scalars, arrays, left, outs, scratch, flops, aliases=None, tight=True
):
    vmem = pl.BlockSpec(memory_space=VMEM)
    smem = pl.BlockSpec(memory_space=pltpu.SMEM)
    operands = (*scalars, *arrays, *left)
    bytes_of = lambda x: math.prod(x.shape) * x.dtype.itemsize
    stays = lambda x: bytes_of(x) > 1 << 20
    held = sum(bytes_of(x) for x in arrays)
    held += sum(bytes_of(x) for x in jax.tree.leaves(outs) if not stays(x))
    held += sum(bytes_of(x) for x in scratch if getattr(x, "memory_space", None) == VMEM)
    return pl.pallas_call(
        kernel,
        out_shape=outs,
        in_specs=[smem] * len(scalars)
        + [vmem] * len(arrays)
        + [pl.BlockSpec(memory_space=pl.ANY)] * len(left),
        out_specs=jax.tree.map(
            lambda x: pl.BlockSpec(memory_space=pl.ANY) if stays(x) else vmem, outs
        ),
        scratch_shapes=scratch,
        input_output_aliases=aliases or {},
        compiler_params=pltpu.CompilerParams(vmem_limit_bytes=held + (6 << 20) if tight else None),
        cost_estimate=pl.CostEstimate(
            flops=flops, bytes_accessed=sum(map(bytes_of, operands)), transcendentals=0
        ),
    )(*operands)


def local(current_image, measured, ray_weight, angle_ids, shadow_start):
    row_index = lax.axis_index("row")
    col_index = lax.axis_index("col")
    rows = lax.axis_size("row")
    cols = lax.axis_size("col")
    slices = current_image.shape[0]
    both = ("row", "col")
    half = VMEM((slices * TILE, TILE), F32)

    turned = jax.ShapeDtypeStruct((2 * SIDE, TILE, TILE), F32)
    sent, image, table = call(
        forward_kernel,
        (col_index.reshape(1), angle_ids),
        (),
        (current_image, measured[:, 0], ray_weight[:, 0]),
        (jax.ShapeDtypeStruct((rows * cols * MESSAGE, TILE), BF16), turned, jax.ShapeDtypeStruct((TABLE, TILE), F32)),
        [
            pltpu.SMEM((TABLE, TILE), F32),
            VMEM((2 * SIDE * TILE, TILE), BF16),
            VMEM((BAND, PIX), F32),
            VMEM((4 * PHASE, BAND, PIX), BF16),
            VMEM((ANGLES * TILE, TILE), F32),
            VMEM((rows * cols * MESSAGE, TILE), F32),
            half,
            half,
            VMEM(turned.shape, F32),
            VMEM(measured[:, 0].shape, F32),
            VMEM(ray_weight[:, 0].shape, F32),
            pltpu.SemaphoreType.DMA((11,)),
        ]
        + [VMEM((TILE, TILE), F32)] * ANGLES,
        30_000_000_000,
        tight=False,
    )
    got = lax.all_to_all(
        sent.reshape(rows * cols, MESSAGE, TILE), both, split_axis=0, concat_axis=0, tiled=True
    )
    blocks = rows
    starts = shadow_start.reshape(-1, ANGLES)
    starts = lax.dynamic_slice_in_dim(starts, col_index * 2, 2, 1).reshape(-1)
    out = call(
        owner_kernel,
        (starts, col_index.reshape(1)),
        (got.reshape(-1, TILE),),
        (),
        jax.ShapeDtypeStruct((rows * cols * 4, TILE), BF16),
        [
            VMEM((2 * blocks, 3 * TILE), F32),
            VMEM((2, blocks + 1, 8, TILE), F32),
            VMEM((rows * cols * 4, TILE), F32),
            VMEM((3 * TILE, TILE), F32),
            VMEM((rows * cols * MESSAGE, TILE), F32),
        ]
        + [VMEM((blocks, 2, 8, TILE), F32)] * 8,
        10_000_000_000,
    )
    shadows = lax.all_to_all(
        out.reshape(rows * cols, 4, TILE), both, split_axis=0, concat_axis=0, tiled=True
    )
    table = table[: 2 * PAIRS + 2, :ANGLES]
    bins = jnp.arange(BINS, dtype=F32)
    delta_lanes = (table[PAIRS : 2 * PAIRS, :, None] - bins).reshape(-1, BAND)
    angle_lanes = jnp.repeat(table[2 * PAIRS :], BINS, axis=1)
    side = jax.ShapeDtypeStruct((8, 8, TILE), F32)
    edge = jax.ShapeDtypeStruct((TILE // 8, 8, TILE), F32)
    x, left, right, top, bottom = call(
        backward_kernel,
        (table[:PAIRS],),
        (delta_lanes, angle_lanes, shadows.reshape(-1, TILE)),
        (image,),
        (turned, side, side, edge, edge),
        [
            VMEM((PIX, BAND), F32),
            VMEM((4 * PHASE, PIX, BAND), BF16),
            VMEM((ANGLES, TILE, TILE), F32),
            VMEM((rows * cols * 4, TILE), F32),
            VMEM((rows * cols * 4, TILE), F32),
            VMEM(turned.shape, F32),
            VMEM(turned.shape, F32),
            pltpu.SemaphoreType.DMA((2,)),
        ],
        30_000_000_000,
    )
    before = lax.ppermute(right, "col", [(i, i + 1) for i in range(cols - 1)])
    after = lax.ppermute(left, "col", [(i + 1, i) for i in range(cols - 1)])
    upward = jnp.concatenate([top, before[:TV_STEPS], after[:TV_STEPS]], axis=0)
    downward = jnp.concatenate([bottom, before[TV_STEPS:], after[TV_STEPS:]], axis=0)
    above = lax.ppermute(downward, "row", [(i, i + 1) for i in range(rows - 1)])
    below = lax.ppermute(upward, "row", [(i + 1, i) for i in range(rows - 1)])
    place = jnp.stack(
        [row_index > 0, row_index < rows - 1, col_index > 0, col_index < cols - 1]
    ).astype(jnp.int32)
    wide = VMEM((SIDE + 2 * TV_STEPS, TILE + 32, TILE), F32)
    few = VMEM((2 * TV_STEPS, TILE + 32, TILE), F32)
    scratch = [wide, wide, few, VMEM((2, TILE + 32, TILE), F32), half, half]
    scratch.append(pltpu.SemaphoreType.DMA((16,)))
    final = jax.ShapeDtypeStruct(current_image.shape, F32)
    smooth = call(
        functools.partial(smooth_kernel, 1),
        (place,),
        (before, after),
        (x,),
        final,
        scratch,
        10_000_000_000,
    )
    return call(
        functools.partial(smooth_kernel, 0),
        (place,),
        (before, after, above, below),
        (x, smooth),
        final,
        scratch,
        10_000_000_000,
        {6: 0},
    )


def solution(mesh):
    return jax.shard_map(
        local,
        mesh=mesh,
        in_specs=(
            P(None, "row", "col"),
            P("col", "row", None, None),
            P("col", "row", None),
            P(),
            P(),
        ),
        out_specs=P(None, "row", "col"),
        check_vma=False,
    )
```
